32 devices in a mesh: ctx: 8 (over z, core), fsdp: 4 (over y, x).
Axes of the slice: x: 2, y: 2, z: 4, core: 2. Of those that a mesh axis runs over, the one named last changes fastest.
Arguments:
- inputs: bfloat16 [4, 2048, 1024], P('fsdp', 'ctx'), may hold values from -6 to 6
- encoder: bfloat16 [4, 512, 1024], P('fsdp', 'ctx'), may hold values from -6 to 6
- teacher: bfloat16 [4, 2048, 1024], P('fsdp', 'ctx'), may hold values from -6 to 6
- valid_mask: int32 [4, 2048], P('fsdp', 'ctx'), may hold values from 0 to 1, as said below
- doc_ids: int32 [4, 2048], P('fsdp'), may hold values from 0 to 2, never falling along the last dimension, each value on 1 to 1024 neighbouring positions
- block_order: int32 [16], replicated, may hold values from 0 to 15, as said below
- buckets: int32 [4096], replicated, may hold values from 0 to 31, as said below
- gain_self: bfloat16 [1024], P('fsdp'), may hold values from 0.5 to 1.5
- w_query: bfloat16 [1024, 1024], P('fsdp'), may hold values from -0.078125 to 0.078125
- w_key: bfloat16 [1024, 512], P('fsdp'), may hold values from -0.078125 to 0.078125
- w_value: bfloat16 [1024, 512], P('fsdp'), may hold values from -0.1875 to 0.1875
- w_out: bfloat16 [1024, 1024], P('fsdp'), may hold values from -1.5 to 1.5
- gain_cross: bfloat16 [1024], P('fsdp'), may hold values from 0.5 to 1.5
- c_query: bfloat16 [1024, 1024], P('fsdp'), may hold values from -0.078125 to 0.078125
- c_key: bfloat16 [1024, 512], P('fsdp'), may hold values from -0.078125 to 0.078125
- c_value: bfloat16 [1024, 512], P('fsdp'), may hold values from -0.1875 to 0.1875
- c_out: bfloat16 [1024, 1024], P('fsdp'), may hold values from -0.75 to 0.75
- gain_ffn: bfloat16 [1024], P('fsdp'), may hold values from 0.5 to 1.5
- w_gate: bfloat16 [1024, 2816], P('fsdp'), may hold values from -0.1875 to 0.1875
- w_up: bfloat16 [1024, 2816], P('fsdp'), may hold values from -0.1875 to 0.1875
- w_down: bfloat16 [2816, 1024], P('fsdp'), may hold values from -0.109375 to 0.109375
- bias_table: bfloat16 [32, 16], P('fsdp'), may hold values from -4 to 4
Outputs:
- layer_out: bfloat16 [4, 2048, 1024], P('fsdp', 'ctx')
- loss: float32 [], replicated
- grad_inputs: float32 [4, 2048, 1024], P('fsdp', 'ctx')
- grad_encoder: float32 [4, 512, 1024], P('fsdp', 'ctx')
- grad_gain_self: float32 [1024], P('fsdp')
- grad_w_query: float32 [1024, 1024], P('fsdp')
- grad_w_key: float32 [1024, 512], P('fsdp')
- grad_w_value: float32 [1024, 512], P('fsdp')
- grad_w_out: float32 [1024, 1024], P('fsdp')
- grad_gain_cross: float32 [1024], P('fsdp')
- grad_c_query: float32 [1024, 1024], P('fsdp')
- grad_c_key: float32 [1024, 512], P('fsdp')
- grad_c_value: float32 [1024, 512], P('fsdp')
- grad_c_out: float32 [1024, 1024], P('fsdp')
- grad_gain_ffn: float32 [1024], P('fsdp')
- grad_w_gate: float32 [1024, 2816], P('fsdp')
- grad_w_up: float32 [1024, 2816], P('fsdp')
- grad_w_down: float32 [2816, 1024], P('fsdp')
- grad_bias_table: float32 [32, 16], P('fsdp')
The draws below stay inside these ranges and needn't reach their ends.
Inputs may be any that keep to these rules, and one draw needn't show every extreme that they name: `valid_mask`: 1 marks a token whose teacher state counts. `block_order`: a permutation in which stored blocks 2 c and 2 c + 1, those of index c of ctx, hold natural blocks b and 15 - b for some b. `buckets`: entry 2048 + d is the bucket of the offset d from a query's position to a key's, for all offsets of one sequence; all offsets of one sign with |d| of 128 or more share one bucket; entry 0 is unused.
All inputs are finite; a program needn't handle non-finite values.
Results may differ from the reference program's by a relative error of at most 0.028.
Values may be sent and summed in bfloat16 or wider, within the bound.
No kernel may reach another device: no remote copies, remote signals or barrier semaphores. Data moves between devices by JAX's collectives and lax.ppermute only.
A program may use at most 256 MiB of HBM per device.

```python
import math
import jax
import jax.numpy as jnp
import numpy as np
from jax import lax

D = 1024
FF = 2816
HEADS = 16
KV_HEADS = 8
HEAD = 64
BUCKETS = 32
BLOCK = 128
ENC = 512
NBLK = 16
LEN = 2048
NSEQ = 4
TOKENS = 8192


def draw_block_order(key, part):
    pairs = NBLK // 2
    chosen = jax.random.permutation(jax.random.fold_in(key, 11), pairs).astype(jnp.int32)
    flips = jax.random.randint(jax.random.fold_in(key, 12), (pairs,), 0, 2, dtype=jnp.int32)
    first = jnp.where(flips == 1, NBLK - 1 - chosen, chosen)
    second = NBLK - 1 - first
    return jnp.stack([first, second], axis=1).reshape(NBLK).astype(jnp.int32)


def draw_buckets(key, part):
    bases = jnp.asarray(np.array([11, 16, 22, 32, 45, 64, 90], dtype=np.int32))
    extra = jax.random.randint(jax.random.fold_in(key, 21), (7,), 0, 1000, dtype=jnp.int32)
    limits = bases + extra * (bases // 4 + 1) // 1000
    offset = jnp.arange(2 * LEN, dtype=jnp.int32) - LEN
    distance = jnp.abs(offset)
    above = jnp.sum((distance[:, None] >= limits[None, :]).astype(jnp.int32), axis=1)
    half = BUCKETS // 2
    inner = jnp.where(distance < half // 2, distance, half // 2 + above)
    return (inner + jnp.where(offset > 0, half, 0)).astype(jnp.int32)


def draw_valid_mask(key, part):
    sequence = jnp.arange(NSEQ, dtype=jnp.int32)[:, None]
    place = jnp.arange(LEN, dtype=jnp.int32)[None, :]
    level = 250 + 600 * place // LEN + 100 * sequence // NSEQ
    drawn = jax.random.randint(jax.random.fold_in(key, 31), (NSEQ, LEN), 0, 1000, dtype=jnp.int32)
    return (drawn < level).astype(jnp.int32)


def levels(stream_key, extent, cuts, least, top_value):
    loudness, own = 1.0, jax.random.fold_in(stream_key, 6)
    for axis_at, parts in cuts:
        heights = jnp.exp(jax.random.uniform(jax.random.fold_in(own, axis_at), (parts,), jnp.float32, least / len(cuts), top_value / len(cuts)))
        loudness = loudness * jnp.repeat(heights, extent[axis_at] // parts).reshape([-1 if axis == axis_at else 1 for axis in range(len(extent))])
    return loudness


def profile(number_of, total, limit, slope):
    loads = [(1 << 20) // math.isqrt(standing ** slope) + 1 for standing in range(2, number_of + 1)]
    rest, holding = total - limit - (number_of - 1), [1] * (number_of - 1)
    while rest > 0:
        movable = [i for i in range(number_of - 1) if holding[i] < limit]
        whole, budget = sum([loads[i] for i in movable]), rest
        for i in movable:
            more = min(limit - holding[i], max(1, budget * loads[i] // whole), rest)
            holding[i] = holding[i] + more
            rest = rest - more
    return np.array([limit] + holding)


def uneven_parts(key, number_of, total, limit, skew):
    if number_of == 2:
        one = jax.random.randint(key, (), max(1, total - limit), min(limit, total - 1) + 1)
        return jnp.stack([one, total - one])
    tallies = jnp.asarray(profile(number_of, total, limit, skew), jnp.int32)
    twos = (number_of - 1) // 2
    source_of, sink = tallies[1:1 + 2 * twos:2], tallies[2:2 + 2 * twos:2]
    margin = jnp.minimum(source_of - 1, limit - sink)
    shifted = jax.random.randint(jax.random.fold_in(key, 1), (twos,), 0, 1 << 20) % (margin + 1)
    tallies = tallies.at[1:1 + 2 * twos:2].set(source_of - shifted).at[2:2 + 2 * twos:2].set(sink + shifted)
    return tallies[jax.random.permutation(jax.random.fold_in(key, 2), number_of)]


def gaussian(own_key, dims, width, bound, cuts=(), kind=jnp.bfloat16):
    factor_of = levels(own_key, dims, cuts, -0.22, 0.18) if cuts else 1.0
    values = jax.random.normal(own_key, dims, jnp.float32) * width * factor_of
    return jnp.minimum(jnp.maximum(values, -bound), bound).astype(kind)


def setup_inputs(seed: int = 0) -> dict:
    streams_of = jax.random.split(jax.random.key(seed), 23)
    inputs = gaussian(streams_of[0], (NSEQ, LEN, D), 1.0, 6.0, ((0, 4), (1, 8)))
    encoder = gaussian(streams_of[1], (NSEQ, ENC, D), 1.0, 6.0, ((0, 4), (1, 8)))
    teacher = gaussian(streams_of[2], (NSEQ, LEN, D), 1.0, 6.0, ((0, 4), (1, 8)))
    valid_mask = draw_valid_mask(jax.random.fold_in(streams_of[22], 71), 0)
    doc_ids = jax.vmap(lambda own: jnp.searchsorted(jnp.cumsum(uneven_parts(own, 3, LEN, LEN // 2, 0)), jnp.arange(LEN), side="right"))(jax.random.split(streams_of[4], NSEQ)).reshape((NSEQ, LEN)).astype(jnp.int32)
    block_order = draw_block_order(jax.random.fold_in(streams_of[22], 71), 0)
    buckets = draw_buckets(jax.random.fold_in(streams_of[22], 71), 0)
    gain_self = jnp.clip(1.0 + 0.1 * jax.random.normal(streams_of[7], (D,), jnp.float32), 0.5, 1.5).astype(jnp.bfloat16)
    w_query = gaussian(streams_of[8], (D, HEADS * HEAD), (5 * D) ** -0.5, 0.078125, ((0, 4),))
    w_key = gaussian(streams_of[9], (D, KV_HEADS * HEAD), (5 * D) ** -0.5, 0.078125, ((0, 4),))
    w_value = gaussian(streams_of[10], (D, KV_HEADS * HEAD), D ** -0.5, 0.1875, ((0, 4),))
    w_out = gaussian(streams_of[11], (HEADS * HEAD, D), (HEADS * HEAD // 64) ** -0.5, 1.5, ((0, 4),))
    gain_cross = jnp.clip(1.0 + 0.1 * jax.random.normal(streams_of[12], (D,), jnp.float32), 0.5, 1.5).astype(jnp.bfloat16)
    c_query = gaussian(streams_of[13], (D, HEADS * HEAD), (5 * D) ** -0.5, 0.078125, ((0, 4),))
    c_key = gaussian(streams_of[14], (D, KV_HEADS * HEAD), (5 * D) ** -0.5, 0.078125, ((0, 4),))
    c_value = gaussian(streams_of[15], (D, KV_HEADS * HEAD), D ** -0.5, 0.1875, ((0, 4),))
    c_out = gaussian(streams_of[16], (HEADS * HEAD, D), (HEADS * HEAD // 16) ** -0.5, 0.75, ((0, 4),))
    gain_ffn = jnp.clip(1.0 + 0.1 * jax.random.normal(streams_of[17], (D,), jnp.float32), 0.5, 1.5).astype(jnp.bfloat16)
    w_gate = gaussian(streams_of[18], (D, FF), D ** -0.5, 0.1875, ((0, 4),))
    w_up = gaussian(streams_of[19], (D, FF), D ** -0.5, 0.1875, ((0, 4),))
    w_down = gaussian(streams_of[20], (FF, D), FF ** -0.5, 0.109375, ((0, 4),))
    bias_table = gaussian(streams_of[21], (BUCKETS, HEADS), 1.0, 4.0, ((0, 4),))
    return {"inputs": inputs, "encoder": encoder, "teacher": teacher, "valid_mask": valid_mask, "doc_ids": doc_ids, "block_order": block_order, "buckets": buckets, "gain_self": gain_self, "w_query": w_query, "w_key": w_key, "w_value": w_value, "w_out": w_out, "gain_cross": gain_cross, "c_query": c_query, "c_key": c_key, "c_value": c_value, "c_out": c_out, "gain_ffn": gain_ffn, "w_gate": w_gate, "w_up": w_up, "w_down": w_down, "bias_table": bias_table}


EPS = 1e-06
NEGATIVE = -1e+30
HIGHEST = lax.Precision.HIGHEST

@jax.custom_vjp
def low(v):
    return lax.optimization_barrier(v.astype(jnp.bfloat16)).astype(jnp.float32)

@jax.custom_vjp
def low_back(v):
    return v

def low_keep(v):
    return (low(v), None)

def low_pass(kept, grad):
    return (grad,)

def back_keep(v):
    return (v, None)

def back_low(kept, grad):
    return (low(grad),)
low.defvjp(low_keep, low_pass)
low_back.defvjp(back_keep, back_low)

def both(value):
    return low_back(low(value))

def matmul(left, right):
    return jnp.dot(left, right, precision=HIGHEST, preferred_element_type=jnp.float32)

def norm_gain(values, gain):
    return values * lax.rsqrt(lax.optimization_barrier(jnp.mean(values * values, axis=-1, keepdims=True)) + EPS) * gain

def self_attention(query, keys, values, table, buckets, docs):
    length = query.shape[0]
    tile = 2 * BLOCK
    positions = jnp.arange(length, dtype=jnp.int32)

    def one_tile(start):
        rows = lax.dynamic_slice_in_dim(query, start, tile, axis=0)
        places = start + jnp.arange(tile, dtype=jnp.int32)
        raw = jnp.einsum('qgrd,kgd->grqk', rows, keys, precision=HIGHEST)
        index = (positions[None, :] - places[:, None] + length).astype(jnp.int32)
        bias = jnp.take(table, jnp.take(buckets, index), axis=0)
        bias = bias.transpose(2, 0, 1).reshape(raw.shape)
        scores = low_back(raw + bias)
        tile_docs = lax.dynamic_slice_in_dim(docs, start, tile)
        allowed = (positions[None, :] // BLOCK <= places[:, None] // BLOCK) & (docs[None, :] == tile_docs[:, None])
        prob = jax.nn.softmax(jnp.where(allowed, scores, NEGATIVE), axis=-1)
        return jnp.einsum('grqk,kgd->qgrd', low(prob), values, precision=HIGHEST)
    starts = jnp.arange(length // tile, dtype=jnp.int32) * tile
    tiles = lax.map(jax.checkpoint(one_tile), starts)
    return tiles.reshape(length, -1)

def cross_attention(query, keys, values):
    raw = jnp.einsum('qgrd,kgd->grqk', query, keys, precision=HIGHEST)
    prob = jax.nn.softmax(low_back(raw), axis=-1)
    return jnp.einsum('grqk,kgd->qgrd', low(prob), values, precision=HIGHEST).reshape(query.shape[0], -1)

def one_sequence(params, table, rows_in, encoder_rows, docs, buckets):
    length = rows_in.shape[0]
    groups = HEADS // KV_HEADS
    hidden_one = low(norm_gain(rows_in, params[0]))
    query = both(matmul(hidden_one, params[1])).reshape(length, KV_HEADS, groups, HEAD)
    keys = both(matmul(hidden_one, params[2])).reshape(length, KV_HEADS, HEAD)
    values = both(matmul(hidden_one, params[3])).reshape(length, KV_HEADS, HEAD)
    attention = both(self_attention(query, keys, values, table, buckets, docs))
    mid_one = rows_in + low_back(matmul(attention, params[4]))
    hidden_two = low(norm_gain(mid_one, params[5]))
    cross_query = both(matmul(hidden_two, params[6])).reshape(length, KV_HEADS, groups, HEAD)
    encoder_keys = both(matmul(encoder_rows, params[7])).reshape(-1, KV_HEADS, HEAD)
    encoder_values = both(matmul(encoder_rows, params[8])).reshape(-1, KV_HEADS, HEAD)
    cross = both(cross_attention(cross_query, encoder_keys, encoder_values))
    mid_two = mid_one + low_back(matmul(cross, params[9]))
    hidden_three = low(norm_gain(mid_two, params[10]))
    gate = low_back(matmul(hidden_three, params[11]))
    up = low_back(matmul(hidden_three, params[12]))
    mixed = low(jax.nn.gelu(gate, approximate=True) * up)
    return mid_two + low_back(matmul(mixed, params[13]))

def reference(inputs, encoder, teacher, valid_mask, doc_ids, block_order, buckets, gain_self, w_query, w_key, w_value, w_out, gain_cross, c_query, c_key, c_value, c_out, gain_ffn, w_gate, w_up, w_down, bias_table):
    weights = tuple((item.astype(jnp.float32) for item in (gain_self, w_query, w_key, w_value, w_out, gain_cross, c_query, c_key, c_value, c_out, gain_ffn, w_gate, w_up, w_down, bias_table)))
    order = jnp.zeros((NBLK,), jnp.int32).at[block_order].set(jnp.arange(NBLK, dtype=jnp.int32))

    def reorder(array, table):
        blocks = array.reshape((NSEQ, NBLK, BLOCK) + array.shape[2:])
        return jnp.take(blocks, table, axis=1).reshape(array.shape)
    target = reorder(teacher.astype(jnp.float32), order)
    mask = reorder(valid_mask, order).astype(jnp.float32)
    count = jnp.maximum(jnp.sum(mask), 1.0)

    def objective(params, rows_in, encoder_rows):
        natural = reorder(rows_in, order)
        table = low(params[14])

        def per_sequence(item):
            sequence_rows, sequence_encoder, sequence_docs = item
            return one_sequence(params, table, sequence_rows, sequence_encoder, sequence_docs, buckets)
        result = lax.map(jax.checkpoint(per_sequence), (natural, encoder_rows, doc_ids))
        diff = result - target
        value = jnp.sum(mask[..., None] * diff * diff) / (D * count)
        return (value, result)
    loss, pullback, result = jax.vjp(objective, weights, inputs.astype(jnp.float32), encoder.astype(jnp.float32), has_aux=True)
    grad_weights, grad_inputs, grad_encoder = pullback(jnp.asarray(TOKENS * D / 2, dtype=jnp.float32))
    layer_out = reorder(result, block_order).astype(jnp.bfloat16)
    return (layer_out, loss, grad_inputs, grad_encoder, grad_weights[0], grad_weights[1], grad_weights[2], grad_weights[3], grad_weights[4], grad_weights[5], grad_weights[6], grad_weights[7], grad_weights[8], grad_weights[9], grad_weights[10], grad_weights[11], grad_weights[12], grad_weights[13], grad_weights[14])
```

```python
import functools
import jax
import jax.numpy as jnp
from jax import lax
from jax.experimental import pallas as pl
from jax.experimental.pallas import tpu as pltpu
from jax.sharding import Mesh
from jax.sharding import PartitionSpec as P

HEAD = 64
BLOCK = 128
NEGATIVE = -1e30
SPAN = 512
F32 = jnp.float32
BF16 = jnp.bfloat16


def nt(left, right):
    return lax.dot_general(left, right, (((1,), (1,)), ((), ())), preferred_element_type=F32)


def nn(left, right):
    return jnp.dot(left, right, preferred_element_type=F32)


def pad_heads(block):
    wide = block.astype(F32)
    lane = lax.broadcasted_iota(jnp.int32, (BLOCK, BLOCK), 1)
    parts = []
    for group in range(2):
        slab = wide[:, group * BLOCK : (group + 1) * BLOCK]
        turned = pltpu.roll(slab, HEAD, 1)
        keep = (lane < HEAD) if group == 0 else (lane >= HEAD)
        for part in range(2):
            source = slab if part == group else turned
            parts.append(jnp.where(keep, source, 0.0))
    return jnp.concatenate(parts, axis=0).astype(BF16)


def unpad_heads(turned):
    parts = [turned[:, index * BLOCK : (index + 1) * BLOCK].T for index in range(4)]
    return jnp.concatenate(parts, axis=1)


def fill_bias(vectors_ref, bias_ref):
    for head in range(4):
        row = jnp.broadcast_to(vectors_ref[0, head : head + 1, :], (BLOCK, SPAN))
        turned = pltpu.roll(row, 0, 1, stride=1, stride_axis=0)
        lanes = slice(head * BLOCK, (head + 1) * BLOCK)
        bias_ref[0, :, lanes] = turned[:, :BLOCK]
        bias_ref[1, :, lanes] = turned[:, BLOCK : 2 * BLOCK]
        bias_ref[2, :, lanes] = jnp.broadcast_to(row[:, BLOCK : BLOCK + 1], (BLOCK, BLOCK))


def four(tile):
    return jnp.concatenate([tile] * 4, axis=1)


def forward_kernel(masked, table, *refs):
    if masked:
        q_ref, k_ref, v_ref, vec_ref, low_ref, high_ref, a_ref, o_ref, l_ref, bias_ref, acc_ref = refs
        fill_bias(vec_ref, bias_ref)
    else:
        q_ref, k_ref, v_ref, a_ref, o_ref, l_ref, acc_ref = refs
    pairs = q_ref.shape[0] // BLOCK
    steps = k_ref.shape[0] // BLOCK
    row = lax.broadcasted_iota(jnp.int32, (BLOCK, BLOCK), 0)
    for index in range(pairs):
        rows = slice(index * BLOCK, (index + 1) * BLOCK)
        query = pad_heads(q_ref[rows, :])
        if masked:
            mine = table[index]
            first = table[pairs + index]
            low = low_ref[index : index + 1, :]
            high = high_ref[index : index + 1, :]

        def scores(step, near):
            if not masked:
                place = pl.multiple_of(step * BLOCK, BLOCK)
                return place, nt(k_ref[pl.ds(place, BLOCK), :], query)
            block = mine - step
            place = pl.multiple_of(table[2 * pairs + block] * BLOCK, BLOCK)
            raw = nt(k_ref[pl.ds(place, BLOCK), :], query)
            position = row + block * BLOCK
            allowed = position >= low
            if near:
                allowed = allowed & (position <= high)
                raw = raw + bias_ref[0]
            else:
                raw = raw + bias_ref[jnp.minimum(step, 2)]
            return place, jnp.where(four(allowed), raw, NEGATIVE)

        def gather(place, weight):
            turned = v_ref[pl.ds(place, BLOCK), :].astype(F32).T.astype(BF16)
            low_half = nn(turned[:HEAD], weight[:, : 2 * BLOCK])
            high_half = nn(turned[HEAD:], weight[:, 2 * BLOCK :])
            return jnp.concatenate([low_half, high_half], axis=1)

        place, raw = scores(0, True)
        top = jnp.max(raw, axis=0, keepdims=True)
        weight = jnp.exp(raw - top)
        total = jnp.sum(weight, axis=0, keepdims=True)
        acc_ref[...] = gather(place, weight.astype(BF16))

        def advance(step, carry):
            top, total = carry
            place, raw = scores(step, False)
            new_top = jnp.maximum(top, jnp.max(raw, axis=0, keepdims=True))
            factor = jnp.exp(top - new_top)
            weight = jnp.exp(raw - new_top)
            total = total * factor + jnp.sum(weight, axis=0, keepdims=True)
            acc_ref[...] = acc_ref[...] * factor + gather(place, weight.astype(BF16))
            return new_top, total

        count = mine - first + 1 if masked else steps
        top, total = lax.fori_loop(1, count, advance, (top, total))
        out = acc_ref[...] / total
        o_ref[0, index] = out
        l_ref[0, index] = jnp.broadcast_to(top + jnp.log(total), (8, 4 * BLOCK))
        a_ref[rows, :] = unpad_heads(out).astype(BF16)


def backward_kernel(masked, table, *refs):
    if masked:
        (q_ref, k_ref, v_ref, g_ref, o_ref, l_ref, vec_ref, low_ref, high_ref,
         dq_ref, dkv_ref, dvec_ref, bias_ref, dk_acc, dv_acc, dq_acc, near_ref, far_ref) = refs
        fill_bias(vec_ref, bias_ref)
        near_ref[...] = jnp.zeros_like(near_ref)
        far_ref[...] = jnp.zeros_like(far_ref)
    else:
        (q_ref, k_ref, v_ref, g_ref, o_ref, l_ref, dq_ref, dkv_ref, dk_acc, dv_acc, dq_acc) = refs
    pairs = q_ref.shape[0] // BLOCK
    steps = k_ref.shape[0] // BLOCK
    dk_acc[...] = jnp.zeros_like(dk_acc)
    dv_acc[...] = jnp.zeros_like(dv_acc)
    row = lax.broadcasted_iota(jnp.int32, (BLOCK, BLOCK), 0)
    for index in range(pairs):
        rows = slice(index * BLOCK, (index + 1) * BLOCK)
        query = pad_heads(q_ref[rows, :])
        grad = pad_heads(g_ref[rows, :])
        log_total = l_ref[0, index, :1, :]
        raw_grad = g_ref[rows, :].astype(F32)
        turned_grad = jnp.concatenate(
            [raw_grad[:, head * HEAD : (head + 1) * HEAD].T for head in range(4)], axis=1
        )
        delta = jnp.sum(turned_grad * o_ref[0, index], axis=0, keepdims=True)
        if masked:
            mine = table[index]
            first = table[pairs + index]
            low = low_ref[index : index + 1, :]
            high = high_ref[index : index + 1, :]

        def tile(step, near, start):
            if masked:
                block = mine - step
                place = pl.multiple_of(table[2 * pairs + block] * BLOCK, BLOCK)
            else:
                place = pl.multiple_of(step * BLOCK, BLOCK)
            keys = k_ref[pl.ds(place, BLOCK), :]
            raw = nt(keys, query)
            if masked:
                position = row + block * BLOCK
                allowed = position >= low
                if near:
                    allowed = allowed & (position <= high)
                    raw = raw + bias_ref[0]
                else:
                    raw = raw + bias_ref[jnp.minimum(step, 2)]
                raw = jnp.where(four(allowed), raw, NEGATIVE)
            prob = jnp.exp(raw - log_total)
            grad_prob = nt(v_ref[pl.ds(place, BLOCK), :], grad)
            grad_score = (prob * (grad_prob - delta)).astype(BF16)
            dv_acc[pl.ds(place, BLOCK), :] += nn(prob.astype(BF16), grad)
            dk_acc[pl.ds(place, BLOCK), :] += nn(grad_score, query)
            turned = keys.astype(F32).T.astype(BF16)
            part = jnp.concatenate(
                [nn(turned[:HEAD], grad_score[:, : 2 * BLOCK]), nn(turned[HEAD:], grad_score[:, 2 * BLOCK :])],
                axis=1,
            )
            if start:
                dq_acc[...] = part
            else:
                dq_acc[...] += part
            return grad_score

        grad_score = tile(0, True, True)
        if masked:
            near_ref[0] += grad_score.astype(F32)
            last = mine - first

            @pl.when(last >= 1)
            def _():
                near_ref[1] += tile(1, False, False).astype(F32)

            def advance(step, carry):
                wide = tile(step, False, False).astype(F32)
                far_ref[...] += jnp.sum(wide.reshape(BLOCK // 8, 8, 4 * BLOCK), axis=0)
                return carry

            lax.fori_loop(2, last + 1, advance, 0)
        else:

            def advance(step, carry):
                tile(step, False, False)
                return carry

            lax.fori_loop(1, steps, advance, 0)
        dq_ref[rows, :] = unpad_heads(dq_acc[...]).astype(BF16)
    dkv_ref[0] = dk_acc[...].astype(BF16)
    dkv_ref[1] = dv_acc[...].astype(BF16)
    if masked:
        rowid = lax.broadcasted_iota(jnp.int32, (BLOCK, SPAN), 0)
        lane = lax.broadcasted_iota(jnp.int32, (1, SPAN), 1)
        for head in range(4):
            lanes = slice(head * BLOCK, (head + 1) * BLOCK)
            wide = jnp.concatenate(
                [near_ref[0, :, lanes], near_ref[1, :, lanes], jnp.zeros((BLOCK, 2 * BLOCK), F32)], axis=1
            )
            bit = 1
            while bit < BLOCK:
                wide = jnp.where((rowid & bit) != 0, pltpu.roll(wide, SPAN - bit, 1), wide)
                bit = bit * 2
            sums = jnp.sum(wide, axis=0, keepdims=True)
            far = jnp.sum(far_ref[:, lanes])
            dvec_ref[0, head : head + 1, :] = sums + jnp.where(lane == BLOCK, far, 0.0)


def specs_of(rows, length, pairs, groups):
    cols = pl.BlockSpec((rows, 2 * BLOCK), lambda g, *_: (0, g))
    keys = pl.BlockSpec((length, BLOCK), lambda g, *_: (0, g))
    values = pl.BlockSpec((length, BLOCK), lambda g, *_: (0, groups + g))
    outs = pl.BlockSpec((1, pairs, HEAD, 4 * BLOCK), lambda g, *_: (g, 0, 0, 0))
    logs = pl.BlockSpec((1, pairs, 8, 4 * BLOCK), lambda g, *_: (g, 0, 0, 0))
    vecs = pl.BlockSpec((1, 4, SPAN), lambda g, *_: (g, 0, 0))
    lims = pl.BlockSpec((pairs, BLOCK), lambda g, *_: (0, 0))
    return cols, keys, values, outs, logs, vecs, lims


def attend(query, keys_values, table, extra, masked):
    rows, width = query.shape
    length = keys_values.shape[0]
    groups = width // (4 * HEAD)
    pairs = rows // BLOCK
    cols, kspec, vspec, outs, logs, vecs, lims = specs_of(rows, length, pairs, groups)
    scratch = [pltpu.VMEM((HEAD, 4 * BLOCK), F32)]
    if masked:
        scratch = [pltpu.VMEM((3, BLOCK, 4 * BLOCK), F32)] + scratch
    return pl.pallas_call(
        functools.partial(forward_kernel, masked),
        grid_spec=pltpu.PrefetchScalarGridSpec(
            num_scalar_prefetch=1,
            grid=(groups,),
            in_specs=[cols, kspec, vspec] + ([vecs, lims, lims] if masked else []),
            out_specs=[cols, outs, logs],
            scratch_shapes=scratch,
        ),
        out_shape=[
            jax.ShapeDtypeStruct((rows, width), BF16),
            jax.ShapeDtypeStruct((groups, pairs, HEAD, 4 * BLOCK), F32),
            jax.ShapeDtypeStruct((groups, pairs, 8, 4 * BLOCK), F32),
        ],
        cost_estimate=pl.CostEstimate(
            flops=4 * rows * length * width, bytes_accessed=4 * length * width, transcendentals=rows * length * 16
        ),
        name="attend_self" if masked else "attend_cross",
    )(table, query, keys_values, keys_values, *extra)


def attend_back(query, keys_values, grad, outs_in, logs_in, table, extra, masked):
    rows, width = query.shape
    length = keys_values.shape[0]
    groups = width // (4 * HEAD)
    pairs = rows // BLOCK
    cols, kspec, vspec, outs, logs, vecs, lims = specs_of(rows, length, pairs, groups)
    scratch = [pltpu.VMEM((length, BLOCK), F32), pltpu.VMEM((length, BLOCK), F32), pltpu.VMEM((HEAD, 4 * BLOCK), F32)]
    out_specs = [cols, pl.BlockSpec((2, length, BLOCK), lambda g, *_: (0, 0, g))]
    out_shape = [
        jax.ShapeDtypeStruct((rows, width), BF16),
        jax.ShapeDtypeStruct((2, length, width // 2), BF16),
    ]
    if masked:
        scratch = [pltpu.VMEM((3, BLOCK, 4 * BLOCK), F32)] + scratch
        scratch += [pltpu.VMEM((2, BLOCK, 4 * BLOCK), F32), pltpu.VMEM((8, 4 * BLOCK), F32)]
        out_specs = out_specs + [vecs]
        out_shape = out_shape + [jax.ShapeDtypeStruct((groups, 4, SPAN), F32)]
    return pl.pallas_call(
        functools.partial(backward_kernel, masked),
        grid_spec=pltpu.PrefetchScalarGridSpec(
            num_scalar_prefetch=1,
            grid=(groups,),
            in_specs=[cols, kspec, vspec, cols, outs, logs] + ([vecs, lims, lims] if masked else []),
            out_specs=out_specs,
            scratch_shapes=scratch,
        ),
        out_shape=out_shape,
        cost_estimate=pl.CostEstimate(
            flops=10 * rows * length * width, bytes_accessed=8 * length * width, transcendentals=rows * length * 16
        ),
        name="attend_self_back" if masked else "attend_cross_back",
    )(table, query, keys_values, keys_values, grad, outs_in, logs_in, *extra)


def offset_index(half):
    place = jnp.arange(SPAN, dtype=jnp.int32)
    behind = jnp.where(place >= 2 * BLOCK, place - SPAN, place)
    return behind, jnp.clip(half - behind, 0, 2 * half - 1)


D = 1024
HEADS = 16
KV_HEADS = 8
BUCKETS = 32
EPS = 1e-06
CTX = ("line", "core")


def tn(left, right):
    return lax.dot_general(left, right, (((0,), (0,)), ((), ())), preferred_element_type=F32)


def norm_rows(values, gain):
    scale = lax.rsqrt(jnp.mean(values * values, axis=-1, keepdims=True) + EPS)
    normed = values * scale
    return normed, scale, (normed * gain).astype(BF16)


def norm_back(grad_out, normed, scale, gain):
    grad_gain = jnp.sum(grad_out * normed, axis=0)
    inner = grad_out * gain
    grad_in = scale * (inner - normed * jnp.mean(inner * normed, axis=-1, keepdims=True))
    return grad_in, grad_gain


def gelu_tanh(value):
    return jax.nn.gelu(value, approximate=True)


def partners(size, bit):
    return [(index, index ^ bit) for index in range(size)]


def sum_everywhere(value):
    for axis in ("core", "line", "fsdp"):
        size = lax.axis_size(axis)
        bit = 1
        while bit < size:
            value = value + lax.ppermute(value, axis, partners(size, bit))
            bit = bit * 2
    return value


def half_rows(part):
    half = part.shape[0] // 2
    return lax.dynamic_slice_in_dim(part, lax.axis_index("core") * half, half, axis=0)


def fetch(*parts):
    joined = parts[0] if len(parts) == 1 else jnp.concatenate(parts, axis=1)
    return lax.all_gather(half_rows(joined), ("fsdp", "core"), axis=0, tiled=True)


def swap(value):
    return lax.ppermute(value, "core", [(0, 1), (1, 0)])


def my_columns(value, other=False):
    half = value.shape[1] // 2
    core = lax.axis_index("core")
    core = 1 - core if other else core
    return lax.dynamic_slice_in_dim(value, core * half, half, axis=1)


def weight_grad(hidden, hidden_swapped, *grads):
    mine = jnp.concatenate([my_columns(item) for item in grads], axis=1)
    other = swap(jnp.concatenate([my_columns(item, True) for item in grads], axis=1))
    both_hidden = jnp.concatenate([hidden, hidden_swapped], axis=0)
    both_grad = jnp.concatenate([mine, other], axis=0)
    return tn(both_hidden, both_grad).astype(BF16)


def reduce_grad(partial, widths):
    shard = lax.psum_scatter(partial, "fsdp", scatter_dimension=0, tiled=True)
    piece = lax.psum_scatter(shard, "line", scatter_dimension=0, tiled=True)
    whole = lax.all_gather(piece, CTX, axis=0, tiled=False)
    lines = lax.axis_size("line")
    whole = whole.reshape(lines, 2, piece.shape[0], piece.shape[1])
    rows = lines * piece.shape[0]
    outs = []
    start = 0
    for width in widths:
        part = whole[..., start : start + width // 2]
        outs.append(part.transpose(0, 2, 1, 3).reshape(rows, width).astype(F32))
        start = start + width // 2
    return outs


def body(
    inputs, encoder, teacher, valid_mask, doc_ids, block_order, buckets,
    gain_self, w_query, w_key, w_value, w_out, gain_cross, c_query, c_key, c_value, c_out,
    gain_ffn, w_gate, w_up, w_down, bias_table,
):
    rows, width = inputs.shape[1:]
    lines = lax.axis_size("line")
    shards = lax.axis_size("fsdp")
    contexts = 2 * lines
    length = rows * contexts
    pair = rows // BLOCK
    token_total = length * shards
    key_width = KV_HEADS * HEAD
    context = lax.axis_index("line") * 2 + lax.axis_index("core")
    fsdp = lax.axis_index("fsdp")

    mask_rows = valid_mask.reshape(rows).astype(F32)
    count = sum_everywhere(jnp.broadcast_to(jnp.sum(mask_rows), (8, 128)))[0, 0]
    count = jnp.maximum(count, 1.0)

    small = jnp.concatenate([gain_self, gain_cross, gain_ffn, bias_table.reshape(-1)])
    share = gain_self.shape[0]
    small = lax.all_gather(small, "fsdp", axis=0, tiled=False)
    gains = [
        small[:, index * share : (index + 1) * share].reshape(D).astype(F32) for index in range(3)
    ]
    gain_one, gain_two, gain_three = gains
    table_whole = small[:, 3 * share :].reshape(BUCKETS, HEADS)

    wqkv = fetch(w_query, w_key, w_value)
    wo = fetch(w_out)
    wcq = fetch(c_query)
    wckv = fetch(c_key, c_value)
    wco = fetch(c_out)
    wgu = fetch(w_gate, w_up)
    wd = fetch(w_down)
    hidden_ff = w_gate.shape[1]

    query_blocks = lax.dynamic_slice_in_dim(block_order, context * pair, pair)
    slots = jnp.arange(contexts * pair, dtype=jnp.int32)
    inverse = jnp.sum(jnp.where(block_order[None, :] == slots[:, None], slots[None, :], 0), axis=1)
    docs = doc_ids.reshape(length)
    query_docs = jnp.stack(
        [lax.dynamic_slice_in_dim(docs, query_blocks[index] * BLOCK, BLOCK) for index in range(pair)]
    )
    low = jnp.sum((docs[None, None, :] < query_docs[:, :, None]).astype(jnp.int32), axis=-1)
    high = jnp.sum((docs[None, None, :] <= query_docs[:, :, None]).astype(jnp.int32), axis=-1) - 1
    place_table = jnp.concatenate([query_blocks, low[:, 0] // BLOCK, inverse]).astype(jnp.int32)
    behind, index_of = offset_index(length)
    bucket_match = (jnp.take(buckets, index_of)[None, :] == jnp.arange(BUCKETS, dtype=jnp.int32)[:, None])
    vectors = tn(table_whole, bucket_match.astype(BF16)).reshape(HEADS // 4, 4, SPAN)
    extra = (vectors, low, high)

    flat_in = inputs.reshape(rows, width).astype(F32)
    normed_one, scale_one, hidden_one = norm_rows(flat_in, gain_one)
    packed = nn(hidden_one, wqkv).astype(BF16)
    query = packed[:, :D]
    pairs_whole = lax.all_gather(packed[:, D:], CTX, axis=0, tiled=True)
    attention, outs_one, logs_one = attend(query, pairs_whole, place_table, extra, True)
    mid_one = flat_in + nn(attention, wo)

    encoder_rows = encoder.reshape(encoder.shape[1], width)
    encoder_pairs = nn(encoder_rows, wckv).astype(BF16)
    encoder_whole = lax.all_gather(encoder_pairs, CTX, axis=0, tiled=True)

    normed_two, scale_two, hidden_two = norm_rows(mid_one, gain_two)
    cross_q = nn(hidden_two, wcq).astype(BF16)
    cross, outs_two, logs_two = attend(cross_q, encoder_whole, place_table, (), False)
    mid_two = mid_one + nn(cross, wco)
    normed_three, scale_three, hidden_three = norm_rows(mid_two, gain_three)
    gate = nn(hidden_three, wgu[:, :hidden_ff])
    up = nn(hidden_three, wgu[:, hidden_ff:])
    active, gelu_pull = jax.vjp(gelu_tanh, gate)
    mixed = (active * up).astype(BF16)
    result = mid_two + nn(mixed, wd)
    layer_out = result.astype(BF16)
    diff = result - teacher.reshape(rows, width).astype(F32)
    squared_local = jnp.sum(mask_rows[:, None] * diff * diff)
    grad_result = token_total / count * mask_rows[:, None] * diff

    e_three = grad_result.astype(BF16)
    grad_mixed = nt(e_three, wd)
    (gelu_slope,) = gelu_pull(grad_mixed * up)
    grad_gate = gelu_slope.astype(BF16)
    grad_up = (grad_mixed * active).astype(BF16)
    (grad_down,) = reduce_grad(weight_grad(mixed, swap(mixed), e_three), (D,))
    grad_gate_weight, grad_up_weight = reduce_grad(
        weight_grad(hidden_three, swap(hidden_three), grad_gate, grad_up), (hidden_ff, hidden_ff)
    )
    grad_hidden_three = nt(grad_gate, wgu[:, :hidden_ff]) + nt(grad_up, wgu[:, hidden_ff:])
    grad_norm_three, grad_gain_three = norm_back(grad_hidden_three, normed_three, scale_three, gain_three)
    grad_mid_two = grad_result + grad_norm_three

    e_two = grad_mid_two.astype(BF16)
    (grad_cross_out,) = reduce_grad(weight_grad(cross, swap(cross), e_two), (D,))
    grad_cross = nt(e_two, wco).astype(BF16)
    grad_cross_q, encoder_grad = attend_back(
        cross_q, encoder_whole, grad_cross, outs_two, logs_two, place_table, (), False
    )
    encoder_mine = lax.psum_scatter(encoder_grad, CTX, scatter_dimension=1, tiled=True)
    encoder_mine = jnp.concatenate([encoder_mine[0], encoder_mine[1]], axis=1)
    grad_encoder = nt(encoder_mine, wckv)
    grad_cross_key, grad_cross_value = reduce_grad(
        weight_grad(
            encoder_rows, swap(encoder_rows), encoder_mine[:, :key_width], encoder_mine[:, key_width:]
        ),
        (key_width, key_width),
    )
    (grad_cross_query,) = reduce_grad(weight_grad(hidden_two, swap(hidden_two), grad_cross_q), (D,))
    grad_norm_two, grad_gain_two = norm_back(nt(grad_cross_q, wcq), normed_two, scale_two, gain_two)
    grad_mid_one = grad_mid_two + grad_norm_two

    e_one = grad_mid_one.astype(BF16)
    (grad_out_weight,) = reduce_grad(weight_grad(attention, swap(attention), e_one), (D,))
    grad_attention = nt(e_one, wo).astype(BF16)
    grad_query, grad_pairs, grad_vectors = attend_back(
        query, pairs_whole, grad_attention, outs_one, logs_one, place_table, extra, True
    )
    mine = lax.psum_scatter(grad_pairs, CTX, scatter_dimension=1, tiled=True)
    grad_packed = jnp.concatenate([grad_query, mine[0], mine[1]], axis=1)
    grad_query_weight, grad_key_weight, grad_value_weight = reduce_grad(
        weight_grad(hidden_one, swap(hidden_one), grad_query, mine[0], mine[1]), (D, key_width, key_width)
    )
    grad_norm_one, grad_gain_one = norm_back(nt(grad_packed, wqkv), normed_one, scale_one, gain_one)
    grad_inputs = grad_mid_one + grad_norm_one

    grad_table = lax.dot_general(
        bucket_match.astype(F32) * ((behind >= 1 - BLOCK) & (behind < 2 * BLOCK)).astype(F32)[None, :],
        grad_vectors.reshape(HEADS, SPAN),
        (((1,), (1,)), ((), ())),
        precision=lax.Precision.HIGHEST,
        preferred_element_type=F32,
    )
    sums = jnp.concatenate(
        [
            grad_gain_one,
            grad_gain_two,
            grad_gain_three,
            grad_table.reshape(-1),
            jnp.broadcast_to(squared_local, (512,)),
        ]
    )
    sums = sum_everywhere(sums.reshape(-1, 128)).reshape(-1)
    loss = sums[3 * D + 512] / (D * count)

    def shard_of(offset, amount):
        return lax.dynamic_slice_in_dim(sums, offset + fsdp * (amount // shards), amount // shards)

    return (
        layer_out.reshape(1, rows, width),
        loss,
        grad_inputs.reshape(1, rows, width),
        grad_encoder.reshape(1, encoder.shape[1], width),
        shard_of(0, D),
        grad_query_weight,
        grad_key_weight,
        grad_value_weight,
        grad_out_weight,
        shard_of(D, D),
        grad_cross_query,
        grad_cross_key,
        grad_cross_value,
        grad_cross_out,
        shard_of(2 * D, D),
        grad_gate_weight,
        grad_up_weight,
        grad_down,
        shard_of(3 * D, 512).reshape(BUCKETS // shards, HEADS),
    )


def solution(mesh):
    shape = mesh.devices.shape
    fine = Mesh(mesh.devices.reshape(shape[0] // 2, 2, shape[1]), ("line", "core", "fsdp"))
    tokens = P("fsdp", CTX, None)
    matrix = P("fsdp", None)
    vector = P("fsdp")
    weights = (vector, matrix, matrix, matrix, matrix, vector, matrix, matrix, matrix, matrix, vector)
    weights = weights + (matrix, matrix, matrix, matrix)
    in_specs = (tokens, tokens, tokens, P("fsdp", CTX), matrix, P(), P()) + weights
    out_specs = (tokens, P(), tokens, tokens) + weights
    return jax.shard_map(body, mesh=fine, in_specs=in_specs, out_specs=out_specs, check_vma=False)
```

```python
import functools
import jax
import jax.numpy as jnp
from jax import lax
from jax.experimental import pallas as pl
from jax.experimental.pallas import tpu as pltpu
from jax.sharding import Mesh
from jax.sharding import PartitionSpec as P

HEAD = 64
BLOCK = 128
NEGATIVE = -1e30
SPAN = 512
F32 = jnp.float32
BF16 = jnp.bfloat16


def nt(left, right):
    return lax.dot_general(left, right, (((1,), (1,)), ((), ())), preferred_element_type=F32)


def nn(left, right):
    return jnp.dot(left, right, preferred_element_type=F32)


def pad_heads(block):
    wide = block.astype(F32)
    lane = lax.broadcasted_iota(jnp.int32, (BLOCK, BLOCK), 1)
    parts = []
    for group in range(2):
        slab = wide[:, group * BLOCK : (group + 1) * BLOCK]
        turned = pltpu.roll(slab, HEAD, 1)
        keep = (lane < HEAD) if group == 0 else (lane >= HEAD)
        for part in range(2):
            source = slab if part == group else turned
            parts.append(jnp.where(keep, source, 0.0))
    return jnp.concatenate(parts, axis=0).astype(BF16)


def unpad_heads(turned):
    parts = [turned[:, index * BLOCK : (index + 1) * BLOCK].T for index in range(4)]
    return jnp.concatenate(parts, axis=1)


def fill_bias(vectors_ref, bias_ref):
    for head in range(4):
        row = jnp.broadcast_to(vectors_ref[0, head : head + 1, :], (BLOCK, SPAN))
        turned = pltpu.roll(row, 0, 1, stride=1, stride_axis=0)
        lanes = slice(head * BLOCK, (head + 1) * BLOCK)
        bias_ref[0, :, lanes] = turned[:, :BLOCK]
        bias_ref[1, :, lanes] = turned[:, BLOCK : 2 * BLOCK]
        bias_ref[2, :, lanes] = jnp.broadcast_to(row[:, BLOCK : BLOCK + 1], (BLOCK, BLOCK))


def four(tile):
    return jnp.concatenate([tile] * 4, axis=1)


def forward_kernel(masked, table, *refs):
    if masked:
        q_ref, k_ref, v_ref, vec_ref, low_ref, high_ref, a_ref, o_ref, l_ref, bias_ref, acc_ref = refs
        fill_bias(vec_ref, bias_ref)
    else:
        q_ref, k_ref, v_ref, a_ref, o_ref, l_ref, acc_ref = refs
    pairs = q_ref.shape[0] // BLOCK
    steps = k_ref.shape[0] // BLOCK
    row = lax.broadcasted_iota(jnp.int32, (BLOCK, BLOCK), 0)
    for index in range(pairs):
        rows = slice(index * BLOCK, (index + 1) * BLOCK)
        query = pad_heads(q_ref[rows, :])
        if masked:
            mine = table[index]
            first = table[pairs + index]
            low = low_ref[index : index + 1, :]
            high = high_ref[index : index + 1, :]

        def scores(step, near):
            if not masked:
                place = pl.multiple_of(step * BLOCK, BLOCK)
                return place, nt(k_ref[pl.ds(place, BLOCK), :], query)
            block = mine - step
            place = pl.multiple_of(table[2 * pairs + block] * BLOCK, BLOCK)
            raw = nt(k_ref[pl.ds(place, BLOCK), :], query)
            position = row + block * BLOCK
            allowed = position >= low
            if near:
                allowed = allowed & (position <= high)
                raw = raw + bias_ref[0]
            else:
                raw = raw + bias_ref[jnp.minimum(step, 2)]
            return place, jnp.where(four(allowed), raw, NEGATIVE)

        def gather(place, weight):
            turned = v_ref[pl.ds(place, BLOCK), :].astype(F32).T.astype(BF16)
            low_half = nn(turned[:HEAD], weight[:, : 2 * BLOCK])
            high_half = nn(turned[HEAD:], weight[:, 2 * BLOCK :])
            return jnp.concatenate([low_half, high_half], axis=1)

        place, raw = scores(0, True)
        top = jnp.max(raw, axis=0, keepdims=True)
        weight = jnp.exp(raw - top)
        total = jnp.sum(weight, axis=0, keepdims=True)
        acc_ref[...] = gather(place, weight.astype(BF16))

        def advance(step, carry):
            top, total = carry
            place, raw = scores(step, False)
            new_top = jnp.maximum(top, jnp.max(raw, axis=0, keepdims=True))
            factor = jnp.exp(top - new_top)
            weight = jnp.exp(raw - new_top)
            total = total * factor + jnp.sum(weight, axis=0, keepdims=True)
            acc_ref[...] = acc_ref[...] * factor + gather(place, weight.astype(BF16))
            return new_top, total

        count = mine - first + 1 if masked else steps
        top, total = lax.fori_loop(1, count, advance, (top, total))
        out = acc_ref[...] / total
        o_ref[0, index] = out
        l_ref[0, index] = jnp.broadcast_to(top + jnp.log(total), (8, 4 * BLOCK))
        a_ref[rows, :] = unpad_heads(out).astype(BF16)


def backward_kernel(masked, table, *refs):
    if masked:
        (q_ref, k_ref, v_ref, g_ref, o_ref, l_ref, vec_ref, low_ref, high_ref,
         dq_ref, dkv_ref, dvec_ref, bias_ref, dk_acc, dv_acc, dq_acc, near_ref, far_ref) = refs
        fill_bias(vec_ref, bias_ref)
        near_ref[...] = jnp.zeros_like(near_ref)
        far_ref[...] = jnp.zeros_like(far_ref)
    else:
        (q_ref, k_ref, v_ref, g_ref, o_ref, l_ref, dq_ref, dkv_ref, dk_acc, dv_acc, dq_acc) = refs
    pairs = q_ref.shape[0] // BLOCK
    steps = k_ref.shape[0] // BLOCK
    dk_acc[...] = jnp.zeros_like(dk_acc)
    dv_acc[...] = jnp.zeros_like(dv_acc)
    row = lax.broadcasted_iota(jnp.int32, (BLOCK, BLOCK), 0)
    for index in range(pairs):
        rows = slice(index * BLOCK, (index + 1) * BLOCK)
        query = pad_heads(q_ref[rows, :])
        grad = pad_heads(g_ref[rows, :])
        log_total = l_ref[0, index, :1, :]
        raw_grad = g_ref[rows, :].astype(F32)
        turned_grad = jnp.concatenate(
            [raw_grad[:, head * HEAD : (head + 1) * HEAD].T for head in range(4)], axis=1
        )
        delta = jnp.sum(turned_grad * o_ref[0, index], axis=0, keepdims=True)
        if masked:
            mine = table[index]
            first = table[pairs + index]
            low = low_ref[index : index + 1, :]
            high = high_ref[index : index + 1, :]

        def tile(step, near, start):
            if masked:
                block = mine - step
                place = pl.multiple_of(table[2 * pairs + block] * BLOCK, BLOCK)
            else:
                place = pl.multiple_of(step * BLOCK, BLOCK)
            keys = k_ref[pl.ds(place, BLOCK), :]
            raw = nt(keys, query)
            if masked:
                position = row + block * BLOCK
                allowed = position >= low
                if near:
                    allowed = allowed & (position <= high)
                    raw = raw + bias_ref[0]
                else:
                    raw = raw + bias_ref[jnp.minimum(step, 2)]
                raw = jnp.where(four(allowed), raw, NEGATIVE)
            prob = jnp.exp(raw - log_total)
            grad_prob = nt(v_ref[pl.ds(place, BLOCK), :], grad)
            grad_score = (prob * (grad_prob - delta)).astype(BF16)
            dv_acc[pl.ds(place, BLOCK), :] += nn(prob.astype(BF16), grad)
            dk_acc[pl.ds(place, BLOCK), :] += nn(grad_score, query)
            turned = keys.astype(F32).T.astype(BF16)
            part = jnp.concatenate(
                [nn(turned[:HEAD], grad_score[:, : 2 * BLOCK]), nn(turned[HEAD:], grad_score[:, 2 * BLOCK :])],
                axis=1,
            )
            if start:
                dq_acc[...] = part
            else:
                dq_acc[...] += part
            return grad_score

        grad_score = tile(0, True, True)
        if masked:
            near_ref[0] += grad_score.astype(F32)
            last = mine - first

            @pl.when(last >= 1)
            def _():
                near_ref[1] += tile(1, False, False).astype(F32)

            def advance(step, carry):
                wide = tile(step, False, False).astype(F32)
                far_ref[...] += jnp.sum(wide.reshape(BLOCK // 8, 8, 4 * BLOCK), axis=0)
                return carry

            lax.fori_loop(2, last + 1, advance, 0)
        else:

            def advance(step, carry):
                tile(step, False, False)
                return carry

            lax.fori_loop(1, steps, advance, 0)
        dq_ref[rows, :] = unpad_heads(dq_acc[...]).astype(BF16)
    dkv_ref[0] = dk_acc[...].astype(BF16)
    dkv_ref[1] = dv_acc[...].astype(BF16)
    if masked:
        rowid = lax.broadcasted_iota(jnp.int32, (BLOCK, SPAN), 0)
        lane = lax.broadcasted_iota(jnp.int32, (1, SPAN), 1)
        for head in range(4):
            lanes = slice(head * BLOCK, (head + 1) * BLOCK)
            wide = jnp.concatenate(
                [near_ref[0, :, lanes], near_ref[1, :, lanes], jnp.zeros((BLOCK, 2 * BLOCK), F32)], axis=1
            )
            bit = 1
            while bit < BLOCK:
                wide = jnp.where((rowid & bit) != 0, pltpu.roll(wide, SPAN - bit, 1), wide)
                bit = bit * 2
            sums = jnp.sum(wide, axis=0, keepdims=True)
            far = jnp.sum(far_ref[:, lanes])
            dvec_ref[0, head : head + 1, :] = sums + jnp.where(lane == BLOCK, far, 0.0)


def specs_of(rows, length, pairs, groups):
    cols = pl.BlockSpec((rows, 2 * BLOCK), lambda g, *_: (0, g))
    keys = pl.BlockSpec((length, BLOCK), lambda g, *_: (0, g))
    values = pl.BlockSpec((length, BLOCK), lambda g, *_: (0, groups + g))
    outs = pl.BlockSpec((1, pairs, HEAD, 4 * BLOCK), lambda g, *_: (g, 0, 0, 0))
    logs = pl.BlockSpec((1, pairs, 8, 4 * BLOCK), lambda g, *_: (g, 0, 0, 0))
    vecs = pl.BlockSpec((1, 4, SPAN), lambda g, *_: (g, 0, 0))
    lims = pl.BlockSpec((pairs, BLOCK), lambda g, *_: (0, 0))
    return cols, keys, values, outs, logs, vecs, lims


def attend(query, keys_values, table, extra, masked):
    rows, width = query.shape
    length = keys_values.shape[0]
    groups = width // (4 * HEAD)
    pairs = rows // BLOCK
    cols, kspec, vspec, outs, logs, vecs, lims = specs_of(rows, length, pairs, groups)
    scratch = [pltpu.VMEM((HEAD, 4 * BLOCK), F32)]
    if masked:
        scratch = [pltpu.VMEM((3, BLOCK, 4 * BLOCK), F32)] + scratch
    return pl.pallas_call(
        functools.partial(forward_kernel, masked),
        grid_spec=pltpu.PrefetchScalarGridSpec(
            num_scalar_prefetch=1,
            grid=(groups,),
            in_specs=[cols, kspec, vspec] + ([vecs, lims, lims] if masked else []),
            out_specs=[cols, outs, logs],
            scratch_shapes=scratch,
        ),
        out_shape=[
            jax.ShapeDtypeStruct((rows, width), BF16),
            jax.ShapeDtypeStruct((groups, pairs, HEAD, 4 * BLOCK), F32),
            jax.ShapeDtypeStruct((groups, pairs, 8, 4 * BLOCK), F32),
        ],
        cost_estimate=pl.CostEstimate(
            flops=4 * rows * length * width, bytes_accessed=4 * length * width, transcendentals=rows * length * 16
        ),
        name="attend_self" if masked else "attend_cross",
    )(table, query, keys_values, keys_values, *extra)


def attend_back(query, keys_values, grad, outs_in, logs_in, table, extra, masked):
    rows, width = query.shape
    length = keys_values.shape[0]
    groups = width // (4 * HEAD)
    pairs = rows // BLOCK
    cols, kspec, vspec, outs, logs, vecs, lims = specs_of(rows, length, pairs, groups)
    scratch = [pltpu.VMEM((length, BLOCK), F32), pltpu.VMEM((length, BLOCK), F32), pltpu.VMEM((HEAD, 4 * BLOCK), F32)]
    out_specs = [cols, pl.BlockSpec((2, length, BLOCK), lambda g, *_: (0, 0, g))]
    out_shape = [
        jax.ShapeDtypeStruct((rows, width), BF16),
        jax.ShapeDtypeStruct((2, length, width // 2), BF16),
    ]
    if masked:
        scratch = [pltpu.VMEM((3, BLOCK, 4 * BLOCK), F32)] + scratch
        scratch += [pltpu.VMEM((2, BLOCK, 4 * BLOCK), F32), pltpu.VMEM((8, 4 * BLOCK), F32)]
        out_specs = out_specs + [vecs]
        out_shape = out_shape + [jax.ShapeDtypeStruct((groups, 4, SPAN), F32)]
    return pl.pallas_call(
        functools.partial(backward_kernel, masked),
        grid_spec=pltpu.PrefetchScalarGridSpec(
            num_scalar_prefetch=1,
            grid=(groups,),
            in_specs=[cols, kspec, vspec, cols, outs, logs] + ([vecs, lims, lims] if masked else []),
            out_specs=out_specs,
            scratch_shapes=scratch,
        ),
        out_shape=out_shape,
        cost_estimate=pl.CostEstimate(
            flops=10 * rows * length * width, bytes_accessed=8 * length * width, transcendentals=rows * length * 16
        ),
        name="attend_self_back" if masked else "attend_cross_back",
    )(table, query, keys_values, keys_values, grad, outs_in, logs_in, *extra)


def offset_index(half):
    place = jnp.arange(SPAN, dtype=jnp.int32)
    behind = jnp.where(place >= 2 * BLOCK, place - SPAN, place)
    return behind, jnp.clip(half - behind, 0, 2 * half - 1)


D = 1024
HEADS = 16
KV_HEADS = 8
BUCKETS = 32
EPS = 1e-06
CTX = ("line", "core")


def tn(left, right):
    return lax.dot_general(left, right, (((0,), (0,)), ((), ())), preferred_element_type=F32)


def norm_rows(values, gain):
    scale = lax.rsqrt(jnp.mean(values * values, axis=-1, keepdims=True) + EPS)
    normed = values * scale
    return normed, scale, (normed * gain).astype(BF16)


def norm_back(grad_out, normed, scale, gain):
    grad_gain = jnp.sum(grad_out * normed, axis=0)
    inner = grad_out * gain
    grad_in = scale * (inner - normed * jnp.mean(inner * normed, axis=-1, keepdims=True))
    return grad_in, grad_gain


def gelu_tanh(value):
    return jax.nn.gelu(value, approximate=True)


def partners(size, bit):
    return [(index, index ^ bit) for index in range(size)]


def bits_of(size):
    return [1 << place for place in range(size.bit_length() - 1)]


def cross(value, axis, bit):
    return lax.ppermute(value, axis, partners(lax.axis_size(axis), bit))


def swap(value):
    return cross(value, "core", 1)


def after(value, *earlier):
    return lax.optimization_barrier((value,) + earlier)[0]


def sum_everywhere(value):
    for axis in ("core", "line", "fsdp"):
        for bit in bits_of(lax.axis_size(axis)):
            value = value + cross(value, axis, bit)
    return value


def add(left, right):
    return (left.astype(F32) + right.astype(F32)).astype(BF16)


def blank(shape):
    return pl.pallas_call(
        lambda out_ref: None,
        out_shape=jax.ShapeDtypeStruct(shape, BF16),
        out_specs=pl.BlockSpec(memory_space=pl.ANY),
        name="blank",
    )()


def spread(have, axis, bits):
    for bit in bits:
        have = have + [(mask ^ bit, cross(piece, axis, bit)) for mask, piece in have]
    return have


def gather_small(value):
    size = lax.axis_size("fsdp")
    me = lax.axis_index("fsdp")
    whole = jnp.zeros((size, value.shape[0]), value.dtype)
    for mask, piece in spread([(0, value)], "fsdp", bits_of(size)):
        whole = lax.dynamic_update_slice(whole, piece[None], (me ^ mask, 0))
    return whole


def columns_of(value, core):
    half = value.shape[1] // 2
    return lax.dynamic_slice_in_dim(value, core * half, half, axis=1)


def gather_weights(parts, earlier):
    size = lax.axis_size("fsdp")
    me = lax.axis_index("fsdp")
    core = lax.axis_index("core")
    mine = jnp.concatenate([columns_of(part, core) for part in parts], axis=1)
    mine = after(mine, *earlier)
    rows, width = mine.shape
    bits = bits_of(size)
    half = rows // 2
    whole = lax.dynamic_update_slice(blank((size * rows, width)), mine, (me * rows, 0))
    first = []
    for stream in range(2):
        order = bits if stream == 0 else bits[::-1]
        have = spread([(0, mine[stream * half : (stream + 1) * half])], "fsdp", order)
        first.append(have[1][1])
        for mask, piece in have[1:]:
            start = (me ^ mask) * rows + stream * half
            whole = lax.dynamic_update_slice(whole, piece, (start, 0))
    other = swap(whole)
    return whole, other, first


def by_core(mine, other):
    first = lax.axis_index("core") == 0
    return jnp.where(first, mine, other), jnp.where(first, other, mine)


def weight_grad(hidden, hidden_swapped, *grads):
    core = lax.axis_index("core")
    mine = jnp.concatenate([columns_of(item, core) for item in grads], axis=1)
    other = swap(jnp.concatenate([columns_of(item, 1 - core) for item in grads], axis=1))
    both_hidden = jnp.concatenate([hidden, hidden_swapped], axis=0)
    both_grad = jnp.concatenate([mine, other], axis=0)
    return tn(both_hidden, both_grad).astype(BF16)


def halve(value, axis, bit, place):
    mine = (lax.axis_index(axis) // bit) % 2
    keep = lax.dynamic_index_in_dim(value, mine, place, keepdims=False)
    send = lax.dynamic_index_in_dim(value, 1 - mine, place, keepdims=False)
    return add(keep, cross(send, axis, bit))


def reduce_grad(partial, widths):
    size = lax.axis_size("fsdp")
    lines = lax.axis_size("line")
    rows = partial.shape[0] // size
    width = partial.shape[1]
    bits = bits_of(size)
    folded = partial.reshape([2] * len(bits) + [2, rows // 2, width])
    sums = []
    for stream in range(2):
        order = bits if stream == 0 else bits[::-1]
        value = lax.index_in_dim(folded, stream, len(bits), keepdims=False)
        left = bits[::-1]
        for bit in order:
            place = left.index(bit)
            value = halve(value, "fsdp", bit, place)
            left = [item for item in left if item != bit]
        sums.append(value)
    shard = jnp.stack(sums)
    line_bits = bits_of(lines)
    value = shard.reshape([2] * len(line_bits) + [rows // lines, width])
    for bit in line_bits:
        value = halve(value, "line", bit, value.ndim - 3)
    have = spread([(0, value)], "line", line_bits[::-1])
    have = [piece for _, piece in sorted(have, key=lambda item: item[0])]
    mine = jnp.stack(have)
    other = swap(mine)
    me = lax.axis_index("line")
    outs = []
    start = 0
    for wide in widths:
        part = slice(start, start + wide // 2)
        both = jnp.concatenate(by_core(mine[..., part], other[..., part]), axis=2)
        ordered = [lax.dynamic_index_in_dim(both, me ^ index, 0, keepdims=False) for index in range(lines)]
        outs.append(jnp.concatenate(ordered, axis=0).astype(F32))
        start = start + wide // 2
    return outs


def gather_context(value):
    have = spread([(0, value)], "line", bits_of(lax.axis_size("line"))[::-1])
    have = [piece for _, piece in sorted(have, key=lambda item: item[0])]
    return jnp.concatenate(have + [swap(piece) for piece in have], axis=0)


def reduce_context(value):
    lines = lax.axis_size("line")
    two, total, width = value.shape
    value = value.reshape(two, 2, lines, total // (2 * lines), width)
    value = add(value[:, 0], swap(value[:, 1]))
    for bit in bits_of(lines):
        value = value.reshape(two, value.shape[1] // 2, 2, value.shape[2], width)
        value = add(value[:, :, 0], cross(value[:, :, 1], "line", bit))
    return value[:, 0]


def body(
    inputs, encoder, teacher, valid_mask, doc_ids, block_order, buckets,
    gain_self, w_query, w_key, w_value, w_out, gain_cross, c_query, c_key, c_value, c_out,
    gain_ffn, w_gate, w_up, w_down, bias_table,
):
    rows, width = inputs.shape[1:]
    lines = lax.axis_size("line")
    shards = lax.axis_size("fsdp")
    contexts = 2 * lines
    length = rows * contexts
    pair = rows // BLOCK
    token_total = length * shards
    key_width = KV_HEADS * HEAD
    context = lax.axis_index("line") * 2 + lax.axis_index("core")
    fsdp = lax.axis_index("fsdp")

    mask_rows = valid_mask.reshape(rows).astype(F32)
    count = sum_everywhere(jnp.broadcast_to(jnp.sum(mask_rows), (8, 128)))[0, 0]
    count = jnp.maximum(count, 1.0)

    small = jnp.concatenate([gain_self, gain_cross, gain_ffn, bias_table.reshape(-1)])
    share = gain_self.shape[0]
    small = gather_small(small)
    gain_one, gain_two, gain_three = [
        small[:, index * share : (index + 1) * share].reshape(D).astype(F32) for index in range(3)
    ]
    table_whole = small[:, 3 * share :].reshape(BUCKETS, HEADS)

    joint = jnp.concatenate
    qkv_mine, qkv_other, first = gather_weights((joint([w_query, w_key, w_value], axis=1),), ())
    mid_mine, mid_other, first = gather_weights((w_out, c_query, joint([c_key, c_value], axis=1), c_out), first)
    gu_mine, gu_other, first = gather_weights((joint([w_gate, w_up], axis=1),), first)
    wd_mine, wd_other, first = gather_weights((w_down,), first)
    halves = D // 2
    wo, wcq, wckv, wco = [
        (mid_mine[:, index * halves : (index + 1) * halves], mid_other[:, index * halves : (index + 1) * halves])
        for index in range(4)
    ]
    core = lax.axis_index("core")
    hidden_ff = w_gate.shape[1]

    def times(left, weight):
        return joint(by_core(nn(left, weight[0]), nn(left, weight[1])), axis=1)

    def times_back(grad, weight):
        return nt(columns_of(grad, core), weight[0]) + nt(columns_of(grad, 1 - core), weight[1])

    query_blocks = lax.dynamic_slice_in_dim(block_order, context * pair, pair)
    slots = jnp.arange(contexts * pair, dtype=jnp.int32)
    owner = slots // pair
    near = ((owner % 2) ^ core) * lines + ((owner // 2) ^ lax.axis_index("line"))
    slots_near = near * pair + slots % pair
    inverse = jnp.sum(jnp.where(block_order[None, :] == slots[:, None], slots_near[None, :], 0), axis=1)
    docs = doc_ids.reshape(length)
    query_docs = jnp.stack(
        [lax.dynamic_slice_in_dim(docs, query_blocks[index] * BLOCK, BLOCK) for index in range(pair)]
    )
    low = jnp.sum((docs[None, None, :] < query_docs[:, :, None]).astype(jnp.int32), axis=-1)
    high = jnp.sum((docs[None, None, :] <= query_docs[:, :, None]).astype(jnp.int32), axis=-1) - 1
    place_table = jnp.concatenate([query_blocks, low[:, 0] // BLOCK, inverse]).astype(jnp.int32)
    behind, index_of = offset_index(length)
    bucket_match = (jnp.take(buckets, index_of)[None, :] == jnp.arange(BUCKETS, dtype=jnp.int32)[:, None])
    vectors = tn(table_whole, bucket_match.astype(BF16)).reshape(HEADS // 4, 4, SPAN)
    extra = (vectors, low, high)

    flat_in = inputs.reshape(rows, width).astype(F32)
    normed_one, scale_one, hidden_one = norm_rows(flat_in, gain_one)
    query, pairs = by_core(nn(hidden_one, qkv_mine).astype(BF16), nn(hidden_one, qkv_other).astype(BF16))
    pairs_whole = gather_context(pairs)
    attention, outs_one, logs_one = attend(query, pairs_whole, place_table, extra, True)
    mid_one = flat_in + times(attention, wo)

    encoder_rows = encoder.reshape(encoder.shape[1], width)
    encoder_pairs = times(encoder_rows, wckv).astype(BF16)
    encoder_whole = gather_context(encoder_pairs)

    normed_two, scale_two, hidden_two = norm_rows(mid_one, gain_two)
    cross_q = times(hidden_two, wcq).astype(BF16)
    crossed, outs_two, logs_two = attend(cross_q, encoder_whole, place_table, (), False)
    mid_two = mid_one + times(crossed, wco)
    normed_three, scale_three, hidden_three = norm_rows(mid_two, gain_three)
    gate, up = by_core(nn(hidden_three, gu_mine), nn(hidden_three, gu_other))
    active, gelu_pull = jax.vjp(gelu_tanh, gate)
    mixed = (active * up).astype(BF16)
    result = mid_two + times(mixed, (wd_mine, wd_other))
    layer_out = result.astype(BF16)
    diff = result - teacher.reshape(rows, width).astype(F32)
    squared_local = jnp.sum(mask_rows[:, None] * diff * diff)
    grad_result = token_total / count * mask_rows[:, None] * diff

    e_three = grad_result.astype(BF16)
    grad_mixed = times_back(e_three, (wd_mine, wd_other))
    (gelu_slope,) = gelu_pull(grad_mixed * up)
    grad_gate = gelu_slope.astype(BF16)
    grad_up = (grad_mixed * active).astype(BF16)
    (grad_down,) = reduce_grad(weight_grad(mixed, swap(mixed), e_three), (D,))
    grad_gate_weight, grad_up_weight = reduce_grad(
        weight_grad(hidden_three, swap(hidden_three), grad_gate, grad_up), (hidden_ff, hidden_ff)
    )
    grad_hidden_three = times_back(joint([grad_gate, grad_up], axis=1), (gu_mine, gu_other))
    grad_norm_three, grad_gain_three = norm_back(grad_hidden_three, normed_three, scale_three, gain_three)
    grad_mid_two = grad_result + grad_norm_three

    e_two = grad_mid_two.astype(BF16)
    (grad_cross_out,) = reduce_grad(weight_grad(crossed, swap(crossed), e_two), (D,))
    grad_cross = times_back(e_two, wco).astype(BF16)
    grad_cross_q, encoder_grad = attend_back(
        cross_q, encoder_whole, grad_cross, outs_two, logs_two, place_table, (), False
    )
    encoder_mine = reduce_context(encoder_grad)
    encoder_mine = jnp.concatenate([encoder_mine[0], encoder_mine[1]], axis=1)
    grad_encoder = times_back(encoder_mine, wckv)
    grad_cross_key, grad_cross_value = reduce_grad(
        weight_grad(
            encoder_rows, swap(encoder_rows), encoder_mine[:, :key_width], encoder_mine[:, key_width:]
        ),
        (key_width, key_width),
    )
    (grad_cross_query,) = reduce_grad(weight_grad(hidden_two, swap(hidden_two), grad_cross_q), (D,))
    grad_norm_two, grad_gain_two = norm_back(times_back(grad_cross_q, wcq), normed_two, scale_two, gain_two)
    grad_mid_one = grad_mid_two + grad_norm_two

    e_one = grad_mid_one.astype(BF16)
    (grad_out_weight,) = reduce_grad(weight_grad(attention, swap(attention), e_one), (D,))
    grad_attention = times_back(e_one, wo).astype(BF16)
    grad_query, grad_pairs, grad_vectors = attend_back(
        query, pairs_whole, grad_attention, outs_one, logs_one, place_table, extra, True
    )
    mine = reduce_context(grad_pairs)
    grad_packed = jnp.concatenate([grad_query, mine[0], mine[1]], axis=1)
    grad_query_weight, grad_key_weight, grad_value_weight = reduce_grad(
        weight_grad(hidden_one, swap(hidden_one), grad_query, mine[0], mine[1]), (D, key_width, key_width)
    )
    grad_norm_one, grad_gain_one = norm_back(times_back(grad_packed, (qkv_mine, qkv_other)), normed_one, scale_one, gain_one)
    grad_inputs = grad_mid_one + grad_norm_one

    grad_table = lax.dot_general(
        bucket_match.astype(F32) * ((behind >= 1 - BLOCK) & (behind < 2 * BLOCK)).astype(F32)[None, :],
        grad_vectors.reshape(HEADS, SPAN),
        (((1,), (1,)), ((), ())),
        precision=lax.Precision.HIGHEST,
        preferred_element_type=F32,
    )
    sums = jnp.concatenate(
        [
            grad_gain_one,
            grad_gain_two,
            grad_gain_three,
            grad_table.reshape(-1),
            jnp.broadcast_to(squared_local, (512,)),
        ]
    )
    sums = sum_everywhere(sums.reshape(-1, 128)).reshape(-1)
    loss = sums[3 * D + 512] / (D * count)

    def shard_of(offset, amount):
        return lax.dynamic_slice_in_dim(sums, offset + fsdp * (amount // shards), amount // shards)

    return (
        layer_out.reshape(1, rows, width),
        loss,
        grad_inputs.reshape(1, rows, width),
        grad_encoder.reshape(1, encoder.shape[1], width),
        shard_of(0, D),
        grad_query_weight,
        grad_key_weight,
        grad_value_weight,
        grad_out_weight,
        shard_of(D, D),
        grad_cross_query,
        grad_cross_key,
        grad_cross_value,
        grad_cross_out,
        shard_of(2 * D, D),
        grad_gate_weight,
        grad_up_weight,
        grad_down,
        shard_of(3 * D, 512).reshape(BUCKETS // shards, HEADS),
    )


def solution(mesh):
    shape = mesh.devices.shape
    fine = Mesh(mesh.devices.reshape(shape[0] // 2, 2, shape[1]), ("line", "core", "fsdp"))
    tokens = P("fsdp", CTX, None)
    matrix = P("fsdp", None)
    vector = P("fsdp")
    weights = (vector, matrix, matrix, matrix, matrix, vector, matrix, matrix, matrix, matrix, vector)
    weights = weights + (matrix, matrix, matrix, matrix)
    in_specs = (tokens, tokens, tokens, P("fsdp", CTX), matrix, P(), P()) + weights
    out_specs = (tokens, P(), tokens, tokens) + weights
    return jax.shard_map(body, mesh=fine, in_specs=in_specs, out_specs=out_specs, check_vma=False)
```

```python
import functools
import jax
import jax.numpy as jnp
from jax import lax
from jax.experimental import pallas as pl
from jax.experimental.pallas import tpu as pltpu
from jax.sharding import Mesh
from jax.sharding import PartitionSpec as P

HEAD = 64
BLOCK = 128
NEGATIVE = -1e30
SPAN = 512
F32 = jnp.float32
BF16 = jnp.bfloat16


def nt(left, right):
    return lax.dot_general(left, right, (((1,), (1,)), ((), ())), preferred_element_type=F32)


def nn(left, right):
    return jnp.dot(left, right, preferred_element_type=F32)


def pad_heads(block):
    wide = block.astype(F32)
    lane = lax.broadcasted_iota(jnp.int32, (BLOCK, BLOCK), 1)
    parts = []
    for group in range(2):
        slab = wide[:, group * BLOCK : (group + 1) * BLOCK]
        turned = pltpu.roll(slab, HEAD, 1)
        keep = (lane < HEAD) if group == 0 else (lane >= HEAD)
        for part in range(2):
            source = slab if part == group else turned
            parts.append(jnp.where(keep, source, 0.0))
    return jnp.concatenate(parts, axis=0).astype(BF16)


def unpad_heads(turned):
    parts = [turned[:, index * BLOCK : (index + 1) * BLOCK].T for index in range(4)]
    return jnp.concatenate(parts, axis=1)


def fill_bias(vectors_ref, bias_ref):
    for head in range(4):
        row = jnp.broadcast_to(vectors_ref[0, head : head + 1, :], (BLOCK, SPAN))
        turned = pltpu.roll(row, 0, 1, stride=1, stride_axis=0)
        lanes = slice(head * BLOCK, (head + 1) * BLOCK)
        bias_ref[0, :, lanes] = turned[:, :BLOCK]
        bias_ref[1, :, lanes] = turned[:, BLOCK : 2 * BLOCK]
        bias_ref[2, :, lanes] = jnp.broadcast_to(row[:, BLOCK : BLOCK + 1], (BLOCK, BLOCK))


def four(tile):
    return jnp.concatenate([tile] * 4, axis=1)


def forward_kernel(masked, table, *refs):
    if masked:
        q_ref, k_ref, v_ref, vec_ref, low_ref, high_ref, a_ref, o_ref, l_ref, bias_ref, acc_ref = refs
        fill_bias(vec_ref, bias_ref)
    else:
        q_ref, k_ref, v_ref, a_ref, o_ref, l_ref, acc_ref = refs
    pairs = q_ref.shape[0] // BLOCK
    steps = k_ref.shape[0] // BLOCK
    row = lax.broadcasted_iota(jnp.int32, (BLOCK, BLOCK), 0)
    for index in range(pairs):
        rows = slice(index * BLOCK, (index + 1) * BLOCK)
        query = pad_heads(q_ref[rows, :])
        if masked:
            mine = table[index]
            first = table[pairs + index]
            low = low_ref[index : index + 1, :]
            high = high_ref[index : index + 1, :]

        def scores(step, near):
            if not masked:
                place = pl.multiple_of(step * BLOCK, BLOCK)
                return place, nt(k_ref[pl.ds(place, BLOCK), :], query)
            block = mine - step
            place = pl.multiple_of(table[2 * pairs + block] * BLOCK, BLOCK)
            raw = nt(k_ref[pl.ds(place, BLOCK), :], query)
            position = row + block * BLOCK
            allowed = position >= low
            if near:
                allowed = allowed & (position <= high)
                raw = raw + bias_ref[0]
            else:
                raw = raw + bias_ref[jnp.minimum(step, 2)]
            return place, jnp.where(four(allowed), raw, NEGATIVE)

        def gather(place, weight):
            turned = v_ref[pl.ds(place, BLOCK), :].astype(F32).T.astype(BF16)
            low_half = nn(turned[:HEAD], weight[:, : 2 * BLOCK])
            high_half = nn(turned[HEAD:], weight[:, 2 * BLOCK :])
            return jnp.concatenate([low_half, high_half], axis=1)

        place, raw = scores(0, True)
        top = jnp.max(raw, axis=0, keepdims=True)
        weight = jnp.exp(raw - top)
        total = jnp.sum(weight, axis=0, keepdims=True)
        acc_ref[...] = gather(place, weight.astype(BF16))

        def advance(step, carry):
            top, total = carry
            place, raw = scores(step, False)
            new_top = jnp.maximum(top, jnp.max(raw, axis=0, keepdims=True))
            factor = jnp.exp(top - new_top)
            weight = jnp.exp(raw - new_top)
            total = total * factor + jnp.sum(weight, axis=0, keepdims=True)
            acc_ref[...] = acc_ref[...] * factor + gather(place, weight.astype(BF16))
            return new_top, total

        count = mine - first + 1 if masked else steps
        top, total = lax.fori_loop(1, count, advance, (top, total))
        out = acc_ref[...] / total
        o_ref[0, index] = out
        l_ref[0, index] = jnp.broadcast_to(top + jnp.log(total), (8, 4 * BLOCK))
        a_ref[rows, :] = unpad_heads(out).astype(BF16)


def backward_kernel(masked, table, *refs):
    if masked:
        (q_ref, k_ref, v_ref, g_ref, o_ref, l_ref, vec_ref, low_ref, high_ref,
         dq_ref, dkv_ref, dvec_ref, bias_ref, dk_acc, dv_acc, dq_acc, near_ref, far_ref) = refs
        fill_bias(vec_ref, bias_ref)
        near_ref[...] = jnp.zeros_like(near_ref)
        far_ref[...] = jnp.zeros_like(far_ref)
    else:
        (q_ref, k_ref, v_ref, g_ref, o_ref, l_ref, dq_ref, dkv_ref, dk_acc, dv_acc, dq_acc) = refs
    pairs = q_ref.shape[0] // BLOCK
    steps = k_ref.shape[0] // BLOCK
    dk_acc[...] = jnp.zeros_like(dk_acc)
    dv_acc[...] = jnp.zeros_like(dv_acc)
    row = lax.broadcasted_iota(jnp.int32, (BLOCK, BLOCK), 0)
    for index in range(pairs):
        rows = slice(index * BLOCK, (index + 1) * BLOCK)
        query = pad_heads(q_ref[rows, :])
        grad = pad_heads(g_ref[rows, :])
        log_total = l_ref[0, index, :1, :]
        raw_grad = g_ref[rows, :].astype(F32)
        turned_grad = jnp.concatenate(
            [raw_grad[:, head * HEAD : (head + 1) * HEAD].T for head in range(4)], axis=1
        )
        delta = jnp.sum(turned_grad * o_ref[0, index], axis=0, keepdims=True)
        if masked:
            mine = table[index]
            first = table[pairs + index]
            low = low_ref[index : index + 1, :]
            high = high_ref[index : index + 1, :]

        def tile(step, near, start):
            if masked:
                block = mine - step
                place = pl.multiple_of(table[2 * pairs + block] * BLOCK, BLOCK)
            else:
                place = pl.multiple_of(step * BLOCK, BLOCK)
            keys = k_ref[pl.ds(place, BLOCK), :]
            raw = nt(keys, query)
            if masked:
                position = row + block * BLOCK
                allowed = position >= low
                if near:
                    allowed = allowed & (position <= high)
                    raw = raw + bias_ref[0]
                else:
                    raw = raw + bias_ref[jnp.minimum(step, 2)]
                raw = jnp.where(four(allowed), raw, NEGATIVE)
            prob = jnp.exp(raw - log_total)
            grad_prob = nt(v_ref[pl.ds(place, BLOCK), :], grad)
            grad_score = (prob * (grad_prob - delta)).astype(BF16)
            dv_acc[pl.ds(place, BLOCK), :] += nn(prob.astype(BF16), grad)
            dk_acc[pl.ds(place, BLOCK), :] += nn(grad_score, query)
            turned = keys.astype(F32).T.astype(BF16)
            part = jnp.concatenate(
                [nn(turned[:HEAD], grad_score[:, : 2 * BLOCK]), nn(turned[HEAD:], grad_score[:, 2 * BLOCK :])],
                axis=1,
            )
            if start:
                dq_acc[...] = part
            else:
                dq_acc[...] += part
            return grad_score

        grad_score = tile(0, True, True)
        if masked:
            near_ref[0] += grad_score.astype(F32)
            last = mine - first

            @pl.when(last >= 1)
            def _():
                near_ref[1] += tile(1, False, False).astype(F32)

            def advance(step, carry):
                wide = tile(step, False, False).astype(F32)
                far_ref[...] += jnp.sum(wide.reshape(BLOCK // 8, 8, 4 * BLOCK), axis=0)
                return carry

            lax.fori_loop(2, last + 1, advance, 0)
        else:

            def advance(step, carry):
                tile(step, False, False)
                return carry

            lax.fori_loop(1, steps, advance, 0)
        dq_ref[rows, :] = unpad_heads(dq_acc[...]).astype(BF16)
    dkv_ref[0] = dk_acc[...].astype(BF16)
    dkv_ref[1] = dv_acc[...].astype(BF16)
    if masked:
        rowid = lax.broadcasted_iota(jnp.int32, (BLOCK, SPAN), 0)
        lane = lax.broadcasted_iota(jnp.int32, (1, SPAN), 1)
        for head in range(4):
            lanes = slice(head * BLOCK, (head + 1) * BLOCK)
            wide = jnp.concatenate(
                [near_ref[0, :, lanes], near_ref[1, :, lanes], jnp.zeros((BLOCK, 2 * BLOCK), F32)], axis=1
            )
            bit = 1
            while bit < BLOCK:
                wide = jnp.where((rowid & bit) != 0, pltpu.roll(wide, SPAN - bit, 1), wide)
                bit = bit * 2
            sums = jnp.sum(wide, axis=0, keepdims=True)
            far = jnp.sum(far_ref[:, lanes])
            dvec_ref[0, head : head + 1, :] = sums + jnp.where(lane == BLOCK, far, 0.0)


def specs_of(rows, length, pairs, groups):
    cols = pl.BlockSpec((rows, 2 * BLOCK), lambda g, *_: (0, g))
    keys = pl.BlockSpec((length, BLOCK), lambda g, *_: (0, g))
    values = pl.BlockSpec((length, BLOCK), lambda g, *_: (0, groups + g))
    outs = pl.BlockSpec((1, pairs, HEAD, 4 * BLOCK), lambda g, *_: (g, 0, 0, 0))
    logs = pl.BlockSpec((1, pairs, 8, 4 * BLOCK), lambda g, *_: (g, 0, 0, 0))
    vecs = pl.BlockSpec((1, 4, SPAN), lambda g, *_: (g, 0, 0))
    lims = pl.BlockSpec((pairs, BLOCK), lambda g, *_: (0, 0))
    return cols, keys, values, outs, logs, vecs, lims


def attend(query, keys_values, table, extra, masked):
    rows, width = query.shape
    length = keys_values.shape[0]
    groups = width // (4 * HEAD)
    pairs = rows // BLOCK
    cols, kspec, vspec, outs, logs, vecs, lims = specs_of(rows, length, pairs, groups)
    scratch = [pltpu.VMEM((HEAD, 4 * BLOCK), F32)]
    if masked:
        scratch = [pltpu.VMEM((3, BLOCK, 4 * BLOCK), F32)] + scratch
    return pl.pallas_call(
        functools.partial(forward_kernel, masked),
        grid_spec=pltpu.PrefetchScalarGridSpec(
            num_scalar_prefetch=1,
            grid=(groups,),
            in_specs=[cols, kspec, vspec] + ([vecs, lims, lims] if masked else []),
            out_specs=[cols, outs, logs],
            scratch_shapes=scratch,
        ),
        out_shape=[
            jax.ShapeDtypeStruct((rows, width), BF16),
            jax.ShapeDtypeStruct((groups, pairs, HEAD, 4 * BLOCK), F32),
            jax.ShapeDtypeStruct((groups, pairs, 8, 4 * BLOCK), F32),
        ],
        cost_estimate=pl.CostEstimate(
            flops=4 * rows * length * width, bytes_accessed=4 * length * width, transcendentals=rows * length * 16
        ),
        name="attend_self" if masked else "attend_cross",
    )(table, query, keys_values, keys_values, *extra)


def attend_back(query, keys_values, grad, outs_in, logs_in, table, extra, masked):
    rows, width = query.shape
    length = keys_values.shape[0]
    groups = width // (4 * HEAD)
    pairs = rows // BLOCK
    cols, kspec, vspec, outs, logs, vecs, lims = specs_of(rows, length, pairs, groups)
    scratch = [pltpu.VMEM((length, BLOCK), F32), pltpu.VMEM((length, BLOCK), F32), pltpu.VMEM((HEAD, 4 * BLOCK), F32)]
    out_specs = [cols, pl.BlockSpec((2, length, BLOCK), lambda g, *_: (0, 0, g))]
    out_shape = [
        jax.ShapeDtypeStruct((rows, width), BF16),
        jax.ShapeDtypeStruct((2, length, width // 2), BF16),
    ]
    if masked:
        scratch = [pltpu.VMEM((3, BLOCK, 4 * BLOCK), F32)] + scratch
        scratch += [pltpu.VMEM((2, BLOCK, 4 * BLOCK), F32), pltpu.VMEM((8, 4 * BLOCK), F32)]
        out_specs = out_specs + [vecs]
        out_shape = out_shape + [jax.ShapeDtypeStruct((groups, 4, SPAN), F32)]
    return pl.pallas_call(
        functools.partial(backward_kernel, masked),
        grid_spec=pltpu.PrefetchScalarGridSpec(
            num_scalar_prefetch=1,
            grid=(groups,),
            in_specs=[cols, kspec, vspec, cols, outs, logs] + ([vecs, lims, lims] if masked else []),
            out_specs=out_specs,
            scratch_shapes=scratch,
        ),
        out_shape=out_shape,
        cost_estimate=pl.CostEstimate(
            flops=10 * rows * length * width, bytes_accessed=8 * length * width, transcendentals=rows * length * 16
        ),
        name="attend_self_back" if masked else "attend_cross_back",
    )(table, query, keys_values, keys_values, grad, outs_in, logs_in, *extra)


def offset_index(half):
    place = jnp.arange(SPAN, dtype=jnp.int32)
    behind = jnp.where(place >= 2 * BLOCK, place - SPAN, place)
    return behind, jnp.clip(half - behind, 0, 2 * half - 1)


D = 1024
HEADS = 16
KV_HEADS = 8
BUCKETS = 32
EPS = 1e-06
CTX = ("line", "core")


def tn(left, right):
    return lax.dot_general(left, right, (((0,), (0,)), ((), ())), preferred_element_type=F32)


def norm_rows(values, gain):
    scale = lax.rsqrt(jnp.mean(values * values, axis=-1, keepdims=True) + EPS)
    normed = values * scale
    return normed, scale, (normed * gain).astype(BF16)


def norm_back(grad_out, normed, scale, gain):
    grad_gain = jnp.sum(grad_out * normed, axis=0)
    inner = grad_out * gain
    grad_in = scale * (inner - normed * jnp.mean(inner * normed, axis=-1, keepdims=True))
    return grad_in, grad_gain


def gelu_tanh(value):
    return jax.nn.gelu(value, approximate=True)


def partners(size, bit):
    return [(index, index ^ bit) for index in range(size)]


def bits_of(size):
    return [1 << place for place in range(size.bit_length() - 1)]


def cross(value, axis, bit):
    return lax.ppermute(value, axis, partners(lax.axis_size(axis), bit))


def swap(value):
    return cross(value, "core", 1)


def add(left, right):
    return (left.astype(F32) + right.astype(F32)).astype(BF16)


def blank(shape):
    return pl.pallas_call(
        lambda out_ref: None,
        out_shape=jax.ShapeDtypeStruct(shape, BF16),
        out_specs=pl.BlockSpec(memory_space=pl.ANY),
        name="blank",
    )()


class Lane:
    def __init__(self, steps):
        self.steps = steps
        self.result = None
        self.pending = next(steps)

    def push(self, arrived):
        try:
            self.pending = self.steps.send(arrived)
        except StopIteration as end:
            self.pending, self.result = None, end.value

    def take(self):
        while self.pending is not None:
            tick([self], ())
        return self.result


def tick(lanes, live):
    active = [lane for lane in lanes if lane.pending is not None]
    live, arrived = lax.optimization_barrier((live, [lane.pending for lane in active]))
    for lane, value in zip(active, arrived):
        lane.push(value)
    return live


def swap_steps(*values):
    got = yield [swap(value) for value in values]
    return got


def sum_steps(value):
    for axis in ("core", "line", "fsdp"):
        for bit in bits_of(lax.axis_size(axis)):
            (got,) = yield [cross(value, axis, bit)]
            value = value + got
    return value


def small_steps(value):
    size = lax.axis_size("fsdp")
    me = lax.axis_index("fsdp")
    have = [(0, value)]
    for bit in bits_of(size):
        got = yield [cross(piece, "fsdp", bit) for _, piece in have]
        have = have + [(mask ^ bit, piece) for (mask, _), piece in zip(have, got)]
    whole = jnp.zeros((size, value.shape[0]), value.dtype)
    for mask, piece in have:
        whole = lax.dynamic_update_slice(whole, piece[None], (me ^ mask, 0))
    return whole


def columns_of(value, core):
    half = value.shape[1] // 2
    return lax.dynamic_slice_in_dim(value, core * half, half, axis=1)


def half_columns(parts):
    core = lax.axis_index("core")
    return jnp.concatenate([columns_of(part, core) for part in parts], axis=1)


def gather_steps(mine):
    size = lax.axis_size("fsdp")
    me = lax.axis_index("fsdp")
    rows, width = mine.shape
    bits = bits_of(size)
    half = rows // 2
    streams = [[(0, mine[stream * half : (stream + 1) * half])] for stream in range(2)]
    whole = lax.dynamic_update_slice(blank((size * rows, width)), mine, (me * rows, 0))
    for step in range(len(bits)):
        chosen = [(bits if stream == 0 else bits[::-1])[step] for stream in range(2)]
        got = yield [[cross(piece, "fsdp", chosen[stream]) for _, piece in streams[stream]] for stream in range(2)]
        for stream in range(2):
            fresh = [(mask ^ chosen[stream], piece) for (mask, _), piece in zip(streams[stream], got[stream])]
            streams[stream] = streams[stream] + fresh
            for mask, piece in fresh:
                whole = lax.dynamic_update_slice(whole, piece, ((me ^ mask) * rows + stream * half, 0))
    whole, other = yield whole, swap(whole)
    return whole, other


def by_core(mine, other):
    first = lax.axis_index("core") == 0
    return jnp.where(first, mine, other), jnp.where(first, other, mine)


def grad_halves(*grads):
    core = lax.axis_index("core")
    mine = jnp.concatenate([columns_of(item, core) for item in grads], axis=1)
    return mine, jnp.concatenate([columns_of(item, 1 - core) for item in grads], axis=1)


def weight_grad(hidden, hidden_swapped, mine, arrived):
    both_hidden = jnp.concatenate([hidden, hidden_swapped], axis=0)
    both_grad = jnp.concatenate([mine, arrived], axis=0)
    return tn(both_hidden, both_grad).astype(BF16)


def split(value, axis, bit, place):
    mine = (lax.axis_index(axis) // bit) % 2
    keep = lax.dynamic_index_in_dim(value, mine, place, keepdims=False)
    return keep, lax.dynamic_index_in_dim(value, 1 - mine, place, keepdims=False)


def reduce_steps(partial, widths):
    size = lax.axis_size("fsdp")
    lines = lax.axis_size("line")
    rows = partial.shape[0] // size
    width = partial.shape[1]
    bits = bits_of(size)
    folded = partial.reshape([2] * len(bits) + [2, rows // 2, width])
    values = [lax.index_in_dim(folded, stream, len(bits), keepdims=False) for stream in range(2)]
    left = [bits[::-1], bits[::-1]]
    for step in range(len(bits)):
        chosen = [(bits if stream == 0 else bits[::-1])[step] for stream in range(2)]
        parts = [
            split(values[stream], "fsdp", chosen[stream], left[stream].index(chosen[stream])) for stream in range(2)
        ]
        got = yield [cross(parts[stream][1], "fsdp", chosen[stream]) for stream in range(2)]
        values = [add(parts[stream][0], got[stream]) for stream in range(2)]
        left = [[item for item in left[stream] if item != chosen[stream]] for stream in range(2)]
    shard = jnp.stack(values)
    line_bits = bits_of(lines)
    value = shard.reshape([2] * len(line_bits) + [rows // lines, width])
    for bit in line_bits:
        keep, send = split(value, "line", bit, value.ndim - 3)
        (got,) = yield [cross(send, "line", bit)]
        value = add(keep, got)
    have = [(0, value)]
    for bit in line_bits[::-1]:
        got = yield [cross(piece, "line", bit) for _, piece in have]
        have = have + [(mask ^ bit, piece) for (mask, _), piece in zip(have, got)]
    have = [piece for _, piece in sorted(have, key=lambda item: item[0])]
    mine = jnp.stack(have)
    (other,) = yield [swap(mine)]
    me = lax.axis_index("line")
    outs = []
    start = 0
    for wide in widths:
        part = slice(start, start + wide // 2)
        both = jnp.concatenate(by_core(mine[..., part], other[..., part]), axis=2)
        ordered = [lax.dynamic_index_in_dim(both, me ^ index, 0, keepdims=False) for index in range(lines)]
        outs.append(jnp.concatenate(ordered, axis=0).astype(F32))
        start = start + wide // 2
    return outs


def gather_context_steps(value):
    have = [(0, value)]
    for bit in bits_of(lax.axis_size("line"))[::-1]:
        got = yield [cross(piece, "line", bit) for _, piece in have]
        have = have + [(mask ^ bit, piece) for (mask, _), piece in zip(have, got)]
    mine = jnp.concatenate([piece for _, piece in sorted(have, key=lambda item: item[0])], axis=0)
    (other,) = yield [swap(mine)]
    return jnp.concatenate([mine, other], axis=0)


def reduce_context_steps(value):
    lines = lax.axis_size("line")
    two, total, width = value.shape
    value = value.reshape(two, 2, lines, total // (2 * lines), width)
    (got,) = yield [swap(value[:, 1])]
    value = add(value[:, 0], got)
    for bit in bits_of(lines):
        value = value.reshape(two, value.shape[1] // 2, 2, value.shape[2], width)
        (got,) = yield [cross(value[:, :, 1], "line", bit)]
        value = add(value[:, :, 0], got)
    return value[:, 0]


def body(
    inputs, encoder, teacher, valid_mask, doc_ids, block_order, buckets,
    gain_self, w_query, w_key, w_value, w_out, gain_cross, c_query, c_key, c_value, c_out,
    gain_ffn, w_gate, w_up, w_down, bias_table,
):
    rows, width = inputs.shape[1:]
    lines = lax.axis_size("line")
    shards = lax.axis_size("fsdp")
    contexts = 2 * lines
    length = rows * contexts
    pair = rows // BLOCK
    token_total = length * shards
    key_width = KV_HEADS * HEAD
    context = lax.axis_index("line") * 2 + lax.axis_index("core")
    fsdp = lax.axis_index("fsdp")

    core = lax.axis_index("core")
    hidden_ff = w_gate.shape[1]
    joint = jnp.concatenate
    halves = D // 2
    share = gain_self.shape[0]

    def times(left, weight):
        return joint(by_core(nn(left, weight[0]), nn(left, weight[1])), axis=1)

    def times_back(grad, weight):
        return nt(columns_of(grad, core), weight[0]) + nt(columns_of(grad, 1 - core), weight[1])

    lane_qkv = Lane(gather_steps(half_columns([joint([w_query, w_key, w_value], axis=1)])))
    lane_small = Lane(small_steps(joint([gain_self, gain_cross, gain_ffn, bias_table.reshape(-1)])))
    mask_rows = valid_mask.reshape(rows).astype(F32)
    lane_count = Lane(sum_steps(jnp.broadcast_to(jnp.sum(mask_rows), (8, 128))))
    mid_shard = half_columns([w_out, c_query, joint([c_key, c_value], axis=1), c_out])
    mid_shard = tick([lane_qkv, lane_small], mid_shard)

    gu_shard = half_columns([joint([w_gate, w_up], axis=1)])
    wd_shard = half_columns([w_down])

    query_blocks = lax.dynamic_slice_in_dim(block_order, context * pair, pair)
    slots = jnp.arange(contexts * pair, dtype=jnp.int32)
    owner = slots // pair
    near = ((owner % 2) ^ core) * lines + ((owner // 2) ^ lax.axis_index("line"))
    slots_near = near * pair + slots % pair
    inverse = jnp.sum(jnp.where(block_order[None, :] == slots[:, None], slots_near[None, :], 0), axis=1)
    docs = doc_ids.reshape(length)
    query_docs = jnp.stack(
        [lax.dynamic_slice_in_dim(docs, query_blocks[index] * BLOCK, BLOCK) for index in range(pair)]
    )
    low = jnp.sum((docs[None, None, :] < query_docs[:, :, None]).astype(jnp.int32), axis=-1)
    high = jnp.sum((docs[None, None, :] <= query_docs[:, :, None]).astype(jnp.int32), axis=-1) - 1
    place_table = jnp.concatenate([query_blocks, low[:, 0] // BLOCK, inverse]).astype(jnp.int32)
    behind, index_of = offset_index(length)
    bucket_match = (jnp.take(buckets, index_of)[None, :] == jnp.arange(BUCKETS, dtype=jnp.int32)[:, None])

    gu_shard, wd_shard, low, high, place_table, bucket_match = tick(
        [lane_qkv, lane_small, lane_count], (gu_shard, wd_shard, low, high, place_table, bucket_match)
    )

    small = lane_small.take()
    gain_one, gain_two, gain_three = [
        small[:, index * share : (index + 1) * share].reshape(D).astype(F32) for index in range(3)
    ]
    table_whole = small[:, 3 * share :].reshape(BUCKETS, HEADS)
    vectors = tn(table_whole, bucket_match.astype(BF16)).reshape(HEADS // 4, 4, SPAN)
    flat_in = inputs.reshape(rows, width).astype(F32)
    normed_one, scale_one, hidden_one = norm_rows(flat_in, gain_one)
    hidden_one, vectors = tick([lane_qkv, lane_count], (hidden_one, vectors))
    extra = (vectors, low, high)

    qkv_mine, qkv_other = lane_qkv.take()
    lane_mid = Lane(gather_steps(mid_shard))
    query, pairs = by_core(nn(hidden_one, qkv_mine).astype(BF16), nn(hidden_one, qkv_other).astype(BF16))
    query, pairs = tick([lane_count], (query, pairs))

    lane_keys = Lane(gather_context_steps(pairs))
    gu_shard = tick([lane_keys, lane_mid, lane_count], gu_shard)
    lane_hidden_one = Lane(swap_steps(hidden_one))
    wd_shard = tick([lane_keys, lane_mid, lane_count, lane_hidden_one], wd_shard)
    lane_gu = Lane(gather_steps(gu_shard))
    tick([lane_keys, lane_mid], ())
    mid_mine, mid_other = lane_mid.take()
    wo, wcq, wckv, wco = [
        (mid_mine[:, index * halves : (index + 1) * halves], mid_other[:, index * halves : (index + 1) * halves])
        for index in range(4)
    ]
    encoder_rows = encoder.reshape(encoder.shape[1], width)
    encoder_pairs = times(encoder_rows, wckv).astype(BF16)
    pairs_whole, encoder_pairs = tick([], (lane_keys.take(), encoder_pairs))

    lane_encoder = Lane(gather_context_steps(encoder_pairs))
    lane_encoder_rows = Lane(swap_steps(encoder_rows))
    attention, outs_one, logs_one = attend(query, pairs_whole, place_table, extra, True)
    attention, outs_one, logs_one = tick([lane_gu, lane_encoder, lane_encoder_rows], (attention, outs_one, logs_one))

    lane_attention = Lane(swap_steps(attention))
    mid_one = flat_in + times(attention, wo)
    normed_two, scale_two, hidden_two = norm_rows(mid_one, gain_two)
    cross_q = times(hidden_two, wcq).astype(BF16)
    mid_one, normed_two, hidden_two, cross_q, scale_two = tick(
        [lane_encoder, lane_attention], (mid_one, normed_two, hidden_two, cross_q, scale_two)
    )
    tick([lane_encoder], ())
    encoder_whole = lane_encoder.take()

    lane_hidden_two = Lane(swap_steps(hidden_two))
    crossed, outs_two, logs_two = attend(cross_q, encoder_whole, place_table, (), False)
    crossed, outs_two, logs_two = tick([lane_gu, lane_hidden_two], (crossed, outs_two, logs_two))

    lane_wd = Lane(gather_steps(wd_shard))
    lane_crossed = Lane(swap_steps(crossed))
    mid_two = mid_one + times(crossed, wco)
    normed_three, scale_three, hidden_three = norm_rows(mid_two, gain_three)
    mid_two, normed_three, hidden_three, scale_three = tick(
        [lane_gu, lane_wd, lane_crossed], (mid_two, normed_three, hidden_three, scale_three)
    )

    gu_mine, gu_other = lane_gu.take()
    lane_hidden_three = Lane(swap_steps(hidden_three))
    gate, up = by_core(nn(hidden_three, gu_mine), nn(hidden_three, gu_other))
    active, gelu_pull = jax.vjp(gelu_tanh, gate)
    mixed = (active * up).astype(BF16)
    mixed, gate, up, active = tick([lane_wd, lane_hidden_three], (mixed, gate, up, active))
    lane_mixed = Lane(swap_steps(mixed))
    tick([lane_wd, lane_mixed], ())

    wd_mine, wd_other = lane_wd.take()
    count = jnp.maximum(lane_count.take()[0, 0], 1.0)
    result = mid_two + times(mixed, (wd_mine, wd_other))
    layer_out = result.astype(BF16)
    diff = result - teacher.reshape(rows, width).astype(F32)
    squared_local = jnp.sum(mask_rows[:, None] * diff * diff)
    grad_result = token_total / count * mask_rows[:, None] * diff

    e_three = grad_result.astype(BF16)
    down_mine, down_away = grad_halves(e_three)
    grad_result, e_three, down_mine, down_away, squared_local, layer_out = tick(
        [], (grad_result, e_three, down_mine, down_away, squared_local, layer_out)
    )
    lane_down = Lane(swap_steps(down_away))
    grad_mixed = times_back(e_three, (wd_mine, wd_other))
    (gelu_slope,) = gelu_pull(grad_mixed * up)
    grad_gate = gelu_slope.astype(BF16)
    grad_up = (grad_mixed * active).astype(BF16)
    wide_mine, wide_away = grad_halves(grad_gate, grad_up)
    grad_gate, grad_up, wide_mine, wide_away = tick([lane_down], (grad_gate, grad_up, wide_mine, wide_away))

    lane_wide = Lane(swap_steps(wide_away))
    partial_down = weight_grad(mixed, lane_mixed.take()[0], down_mine, lane_down.take()[0])
    partial_down = tick([lane_wide], partial_down)

    lane_down = Lane(reduce_steps(partial_down, (D,)))
    partial_wide = weight_grad(hidden_three, lane_hidden_three.take()[0], wide_mine, lane_wide.take()[0])
    grad_hidden_three = times_back(joint([grad_gate, grad_up], axis=1), (gu_mine, gu_other))
    partial_wide, grad_hidden_three = tick([lane_down], (partial_wide, grad_hidden_three))

    lane_wide = Lane(reduce_steps(partial_wide, (hidden_ff, hidden_ff)))
    grad_norm_three, grad_gain_three = norm_back(grad_hidden_three, normed_three, scale_three, gain_three)
    grad_mid_two = grad_result + grad_norm_three

    e_two = grad_mid_two.astype(BF16)
    grad_cross = times_back(e_two, wco).astype(BF16)
    grad_cross_q, encoder_grad = attend_back(
        cross_q, encoder_whole, grad_cross, outs_two, logs_two, place_table, (), False
    )
    out_mine, out_away = grad_halves(e_two, grad_cross_q)
    grad_mid_two, grad_cross_q, encoder_grad, out_mine, out_away = tick(
        [lane_down, lane_wide], (grad_mid_two, grad_cross_q, encoder_grad, out_mine, out_away)
    )

    lane_encoder = Lane(reduce_context_steps(encoder_grad))
    lane_out = Lane(swap_steps(out_away))
    grad_norm_two, grad_gain_two = norm_back(times_back(grad_cross_q, wcq), normed_two, scale_two, gain_two)
    grad_mid_one = grad_mid_two + grad_norm_two

    e_one = grad_mid_one.astype(BF16)
    one_mine, one_away = grad_halves(e_one)
    grad_attention = times_back(e_one, wo).astype(BF16)
    grad_mid_one, one_mine, one_away, grad_attention = tick(
        [lane_down, lane_encoder, lane_out], (grad_mid_one, one_mine, one_away, grad_attention)
    )
    lane_one = Lane(swap_steps(one_away))
    grad_query, grad_pairs, grad_vectors = attend_back(
        query, pairs_whole, grad_attention, outs_one, logs_one, place_table, extra, True
    )
    grad_query, grad_pairs, grad_vectors = tick(
        [lane_down, lane_wide, lane_encoder, lane_one], (grad_query, grad_pairs, grad_vectors)
    )

    lane_pairs = Lane(reduce_context_steps(grad_pairs))
    arrived = lane_out.take()[0]
    partial_out = weight_grad(crossed, lane_crossed.take()[0], out_mine[:, :halves], arrived[:, :halves])
    partial_query = weight_grad(hidden_two, lane_hidden_two.take()[0], out_mine[:, halves:], arrived[:, halves:])
    partial_one = weight_grad(attention, lane_attention.take()[0], one_mine, lane_one.take()[0])
    partial_mid = joint([partial_out, partial_query, partial_one], axis=1)
    partial_mid = tick([lane_pairs, lane_wide, lane_encoder], partial_mid)

    lane_mid = Lane(reduce_steps(partial_mid, (D, D, D)))
    encoder_mine = joint([lane_encoder.take()[0], lane_encoder.take()[1]], axis=1)
    grad_encoder = times_back(encoder_mine, wckv)
    keys_mine, keys_away = grad_halves(encoder_mine[:, :key_width], encoder_mine[:, key_width:])
    grad_encoder, keys_mine, keys_away = tick([lane_pairs, lane_mid, lane_wide], (grad_encoder, keys_mine, keys_away))

    lane_keys = Lane(swap_steps(keys_away))
    tick([lane_pairs, lane_mid, lane_keys], ())
    mine = lane_pairs.take()
    last_mine, last_away = grad_halves(grad_query, mine[0], mine[1])
    last_mine, last_away = tick([], (last_mine, last_away))

    lane_last = Lane(swap_steps(last_away))
    partial_keys = weight_grad(encoder_rows, lane_encoder_rows.take()[0], keys_mine, lane_keys.take()[0])
    partial_keys = tick([lane_last], partial_keys)
    partial_last = weight_grad(hidden_one, lane_hidden_one.take()[0], last_mine, lane_last.take()[0])
    partial_last = joint([partial_last, partial_keys], axis=1)
    partial_last = tick([lane_wide, lane_down], partial_last)

    lane_last = Lane(reduce_steps(partial_last, (D, key_width, key_width, key_width, key_width)))
    grad_packed = joint([grad_query, mine[0], mine[1]], axis=1)
    grad_norm_one, grad_gain_one = norm_back(
        times_back(grad_packed, (qkv_mine, qkv_other)), normed_one, scale_one, gain_one
    )
    grad_inputs = grad_mid_one + grad_norm_one

    grad_table = lax.dot_general(
        bucket_match.astype(F32) * ((behind >= 1 - BLOCK) & (behind < 2 * BLOCK)).astype(F32)[None, :],
        grad_vectors.reshape(HEADS, SPAN),
        (((1,), (1,)), ((), ())),
        precision=lax.Precision.HIGHEST,
        preferred_element_type=F32,
    )
    sums = jnp.concatenate(
        [
            grad_gain_one,
            grad_gain_two,
            grad_gain_three,
            grad_table.reshape(-1),
            jnp.broadcast_to(squared_local, (512,)),
        ]
    )
    sums, grad_inputs = tick([lane_last, lane_wide, lane_mid, lane_down], (sums.reshape(-1, 128), grad_inputs))
    lane_sums = Lane(sum_steps(sums))
    lanes = [lane_last, lane_wide, lane_mid, lane_down, lane_sums]
    while any(lane.pending is not None for lane in lanes):
        tick(lanes, ())
    sums = lane_sums.take().reshape(-1)
    (grad_down,) = lane_down.take()
    grad_gate_weight, grad_up_weight = lane_wide.take()
    grad_cross_out, grad_cross_query, grad_out_weight = lane_mid.take()
    grad_query_weight, grad_key_weight, grad_value_weight, grad_cross_key, grad_cross_value = lane_last.take()
    loss = sums[3 * D + 512] / (D * count)

    def shard_of(offset, amount):
        return lax.dynamic_slice_in_dim(sums, offset + fsdp * (amount // shards), amount // shards)

    return (
        layer_out.reshape(1, rows, width),
        loss,
        grad_inputs.reshape(1, rows, width),
        grad_encoder.reshape(1, encoder.shape[1], width),
        shard_of(0, D),
        grad_query_weight,
        grad_key_weight,
        grad_value_weight,
        grad_out_weight,
        shard_of(D, D),
        grad_cross_query,
        grad_cross_key,
        grad_cross_value,
        grad_cross_out,
        shard_of(2 * D, D),
        grad_gate_weight,
        grad_up_weight,
        grad_down,
        shard_of(3 * D, 512).reshape(BUCKETS // shards, HEADS),
    )


def solution(mesh):
    shape = mesh.devices.shape
    fine = Mesh(mesh.devices.reshape(shape[0] // 2, 2, shape[1]), ("line", "core", "fsdp"))
    tokens = P("fsdp", CTX, None)
    matrix = P("fsdp", None)
    vector = P("fsdp")
    weights = (vector, matrix, matrix, matrix, matrix, vector, matrix, matrix, matrix, matrix, vector)
    weights = weights + (matrix, matrix, matrix, matrix)
    in_specs = (tokens, tokens, tokens, P("fsdp", CTX), matrix, P(), P()) + weights
    out_specs = (tokens, P(), tokens, tokens) + weights
    return jax.shard_map(body, mesh=fine, in_specs=in_specs, out_specs=out_specs, check_vma=False)
```

```python
import functools
import jax
import jax.numpy as jnp
from jax import lax
from jax.experimental import pallas as pl
from jax.experimental.pallas import tpu as pltpu
from jax.sharding import Mesh
from jax.sharding import PartitionSpec as P

HEAD = 64
BLOCK = 128
NEGATIVE = -1e30
SPAN = 512
F32 = jnp.float32
BF16 = jnp.bfloat16


def nt(left, right):
    return lax.dot_general(left, right, (((1,), (1,)), ((), ())), preferred_element_type=F32)


def nn(left, right):
    return jnp.dot(left, right, preferred_element_type=F32)


def pad_heads(block):
    wide = block.astype(F32)
    lane = lax.broadcasted_iota(jnp.int32, (BLOCK, BLOCK), 1)
    parts = []
    for group in range(2):
        slab = wide[:, group * BLOCK : (group + 1) * BLOCK]
        turned = pltpu.roll(slab, HEAD, 1)
        keep = (lane < HEAD) if group == 0 else (lane >= HEAD)
        for part in range(2):
            source = slab if part == group else turned
            parts.append(jnp.where(keep, source, 0.0))
    return jnp.concatenate(parts, axis=0).astype(BF16)


def unpad_heads(turned):
    parts = [turned[:, index * BLOCK : (index + 1) * BLOCK].T for index in range(4)]
    return jnp.concatenate(parts, axis=1)


def fill_bias(vectors_ref, bias_ref):
    for head in range(4):
        row = jnp.broadcast_to(vectors_ref[0, head : head + 1, :], (BLOCK, SPAN))
        turned = pltpu.roll(row, 0, 1, stride=1, stride_axis=0)
        lanes = slice(head * BLOCK, (head + 1) * BLOCK)
        bias_ref[0, :, lanes] = turned[:, :BLOCK]
        bias_ref[1, :, lanes] = turned[:, BLOCK : 2 * BLOCK]
        bias_ref[2, :, lanes] = jnp.broadcast_to(row[:, BLOCK : BLOCK + 1], (BLOCK, BLOCK))


def four(tile):
    return jnp.concatenate([tile] * 4, axis=1)


def forward_kernel(masked, table, *refs):
    if masked:
        q_ref, k_ref, v_ref, vec_ref, low_ref, high_ref, a_ref, o_ref, l_ref, bias_ref, acc_ref = refs
        fill_bias(vec_ref, bias_ref)
    else:
        q_ref, k_ref, v_ref, a_ref, o_ref, l_ref, acc_ref = refs
    pairs = q_ref.shape[0] // BLOCK
    steps = k_ref.shape[0] // BLOCK
    row = lax.broadcasted_iota(jnp.int32, (BLOCK, BLOCK), 0)
    for index in range(pairs):
        rows = slice(index * BLOCK, (index + 1) * BLOCK)
        query = pad_heads(q_ref[rows, :])
        if masked:
            mine = table[index]
            first = table[pairs + index]
            low = low_ref[index : index + 1, :]
            high = high_ref[index : index + 1, :]

        def scores(step, near):
            if not masked:
                place = pl.multiple_of(step * BLOCK, BLOCK)
                return place, nt(k_ref[pl.ds(place, BLOCK), :], query)
            block = mine - step
            place = pl.multiple_of(table[2 * pairs + block] * BLOCK, BLOCK)
            raw = nt(k_ref[pl.ds(place, BLOCK), :], query)
            position = row + block * BLOCK
            allowed = position >= low
            if near:
                allowed = allowed & (position <= high)
                raw = raw + bias_ref[0]
            else:
                raw = raw + bias_ref[jnp.minimum(step, 2)]
            return place, jnp.where(four(allowed), raw, NEGATIVE)

        def gather(place, weight):
            turned = v_ref[pl.ds(place, BLOCK), :].astype(F32).T.astype(BF16)
            low_half = nn(turned[:HEAD], weight[:, : 2 * BLOCK])
            high_half = nn(turned[HEAD:], weight[:, 2 * BLOCK :])
            return jnp.concatenate([low_half, high_half], axis=1)

        place, raw = scores(0, True)
        top = jnp.max(raw, axis=0, keepdims=True)
        weight = jnp.exp(raw - top)
        total = jnp.sum(weight, axis=0, keepdims=True)
        acc_ref[...] = gather(place, weight.astype(BF16))

        def advance(step, carry):
            top, total = carry
            place, raw = scores(step, False)
            new_top = jnp.maximum(top, jnp.max(raw, axis=0, keepdims=True))
            factor = jnp.exp(top - new_top)
            weight = jnp.exp(raw - new_top)
            total = total * factor + jnp.sum(weight, axis=0, keepdims=True)
            acc_ref[...] = acc_ref[...] * factor + gather(place, weight.astype(BF16))
            return new_top, total

        count = mine - first + 1 if masked else steps
        top, total = lax.fori_loop(1, count, advance, (top, total))
        out = acc_ref[...] / total
        o_ref[0, index] = out
        l_ref[0, index] = jnp.broadcast_to(top + jnp.log(total), (8, 4 * BLOCK))
        a_ref[rows, :] = unpad_heads(out).astype(BF16)


def backward_kernel(masked, table, *refs):
    if masked:
        (q_ref, k_ref, v_ref, g_ref, o_ref, l_ref, vec_ref, low_ref, high_ref,
         dq_ref, dkv_ref, dvec_ref, bias_ref, dk_acc, dv_acc, dq_acc, near_ref, far_ref) = refs
        fill_bias(vec_ref, bias_ref)
        near_ref[...] = jnp.zeros_like(near_ref)
        far_ref[...] = jnp.zeros_like(far_ref)
    else:
        (q_ref, k_ref, v_ref, g_ref, o_ref, l_ref, dq_ref, dkv_ref, dk_acc, dv_acc, dq_acc) = refs
    pairs = q_ref.shape[0] // BLOCK
    steps = k_ref.shape[0] // BLOCK
    dk_acc[...] = jnp.zeros_like(dk_acc)
    dv_acc[...] = jnp.zeros_like(dv_acc)
    row = lax.broadcasted_iota(jnp.int32, (BLOCK, BLOCK), 0)
    for index in range(pairs):
        rows = slice(index * BLOCK, (index + 1) * BLOCK)
        query = pad_heads(q_ref[rows, :])
        grad = pad_heads(g_ref[rows, :])
        log_total = l_ref[0, index, :1, :]
        raw_grad = g_ref[rows, :].astype(F32)
        turned_grad = jnp.concatenate(
            [raw_grad[:, head * HEAD : (head + 1) * HEAD].T for head in range(4)], axis=1
        )
        delta = jnp.sum(turned_grad * o_ref[0, index], axis=0, keepdims=True)
        if masked:
            mine = table[index]
            first = table[pairs + index]
            low = low_ref[index : index + 1, :]
            high = high_ref[index : index + 1, :]

        def tile(step, near, start):
            if masked:
                block = mine - step
                place = pl.multiple_of(table[2 * pairs + block] * BLOCK, BLOCK)
            else:
                place = pl.multiple_of(step * BLOCK, BLOCK)
            keys = k_ref[pl.ds(place, BLOCK), :]
            raw = nt(keys, query)
            if masked:
                position = row + block * BLOCK
                allowed = position >= low
                if near:
                    allowed = allowed & (position <= high)
                    raw = raw + bias_ref[0]
                else:
                    raw = raw + bias_ref[jnp.minimum(step, 2)]
                raw = jnp.where(four(allowed), raw, NEGATIVE)
            prob = jnp.exp(raw - log_total)
            grad_prob = nt(v_ref[pl.ds(place, BLOCK), :], grad)
            grad_score = (prob * (grad_prob - delta)).astype(BF16)
            dv_acc[pl.ds(place, BLOCK), :] += nn(prob.astype(BF16), grad)
            dk_acc[pl.ds(place, BLOCK), :] += nn(grad_score, query)
            turned = keys.astype(F32).T.astype(BF16)
            part = jnp.concatenate(
                [nn(turned[:HEAD], grad_score[:, : 2 * BLOCK]), nn(turned[HEAD:], grad_score[:, 2 * BLOCK :])],
                axis=1,
            )
            if start:
                dq_acc[...] = part
            else:
                dq_acc[...] += part
            return grad_score

        grad_score = tile(0, True, True)
        if masked:
            near_ref[0] += grad_score.astype(F32)
            last = mine - first

            @pl.when(last >= 1)
            def _():
                near_ref[1] += tile(1, False, False).astype(F32)

            def advance(step, carry):
                wide = tile(step, False, False).astype(F32)
                far_ref[...] += jnp.sum(wide.reshape(BLOCK // 8, 8, 4 * BLOCK), axis=0)
                return carry

            lax.fori_loop(2, last + 1, advance, 0)
        else:

            def advance(step, carry):
                tile(step, False, False)
                return carry

            lax.fori_loop(1, steps, advance, 0)
        dq_ref[rows, :] = unpad_heads(dq_acc[...]).astype(BF16)
    dkv_ref[0] = dk_acc[...].astype(BF16)
    dkv_ref[1] = dv_acc[...].astype(BF16)
    if masked:
        rowid = lax.broadcasted_iota(jnp.int32, (BLOCK, SPAN), 0)
        lane = lax.broadcasted_iota(jnp.int32, (1, SPAN), 1)
        for head in range(4):
            lanes = slice(head * BLOCK, (head + 1) * BLOCK)
            wide = jnp.concatenate(
                [near_ref[0, :, lanes], near_ref[1, :, lanes], jnp.zeros((BLOCK, 2 * BLOCK), F32)], axis=1
            )
            bit = 1
            while bit < BLOCK:
                wide = jnp.where((rowid & bit) != 0, pltpu.roll(wide, SPAN - bit, 1), wide)
                bit = bit * 2
            sums = jnp.sum(wide, axis=0, keepdims=True)
            far = jnp.sum(far_ref[:, lanes])
            dvec_ref[0, head : head + 1, :] = sums + jnp.where(lane == BLOCK, far, 0.0)


def specs_of(rows, length, pairs, groups, first=0):
    cols = pl.BlockSpec((rows, 2 * BLOCK), lambda g, *_: (0, g + first))
    keys = pl.BlockSpec((length, BLOCK), lambda g, *_: (0, g + first))
    values = pl.BlockSpec((length, BLOCK), lambda g, *_: (0, groups + g + first))
    outs = pl.BlockSpec((1, pairs, HEAD, 4 * BLOCK), lambda g, *_: (g + first, 0, 0, 0))
    logs = pl.BlockSpec((1, pairs, 8, 4 * BLOCK), lambda g, *_: (g + first, 0, 0, 0))
    vecs = pl.BlockSpec((1, 4, SPAN), lambda g, *_: (g + first, 0, 0))
    lims = pl.BlockSpec((pairs, BLOCK), lambda g, *_: (0, 0))
    return cols, keys, values, outs, logs, vecs, lims


def attend(query, keys_values, table, extra, masked):
    rows, width = query.shape
    length = keys_values.shape[0]
    groups = width // (4 * HEAD)
    pairs = rows // BLOCK
    cols, kspec, vspec, outs, logs, vecs, lims = specs_of(rows, length, pairs, groups)
    scratch = [pltpu.VMEM((HEAD, 4 * BLOCK), F32)]
    if masked:
        scratch = [pltpu.VMEM((3, BLOCK, 4 * BLOCK), F32)] + scratch
    return pl.pallas_call(
        functools.partial(forward_kernel, masked),
        grid_spec=pltpu.PrefetchScalarGridSpec(
            num_scalar_prefetch=1,
            grid=(groups,),
            in_specs=[cols, kspec, vspec] + ([vecs, lims, lims] if masked else []),
            out_specs=[cols, outs, logs],
            scratch_shapes=scratch,
        ),
        out_shape=[
            jax.ShapeDtypeStruct((rows, width), BF16),
            jax.ShapeDtypeStruct((groups, pairs, HEAD, 4 * BLOCK), F32),
            jax.ShapeDtypeStruct((groups, pairs, 8, 4 * BLOCK), F32),
        ],
        cost_estimate=pl.CostEstimate(
            flops=4 * rows * length * width, bytes_accessed=4 * length * width, transcendentals=rows * length * 16
        ),
        name="attend_self" if masked else "attend_cross",
    )(table, query, keys_values, keys_values, *extra)


def attend_back(query, keys_values, grad, outs_in, logs_in, table, extra, masked, part=0, parts=1):
    rows, width = query.shape
    length = keys_values.shape[0]
    groups = width // (4 * HEAD)
    pairs = rows // BLOCK
    count = groups // parts
    cols, kspec, vspec, outs, logs, vecs, lims = specs_of(rows, length, pairs, groups, part * count)
    scratch = [pltpu.VMEM((length, BLOCK), F32), pltpu.VMEM((length, BLOCK), F32), pltpu.VMEM((HEAD, 4 * BLOCK), F32)]
    out_specs = [pl.BlockSpec((rows, 2 * BLOCK), lambda g, *_: (0, g)), pl.BlockSpec((2, length, BLOCK), lambda g, *_: (0, 0, g))]
    out_shape = [
        jax.ShapeDtypeStruct((rows, width // parts), BF16),
        jax.ShapeDtypeStruct((2, length, width // 2 // parts), BF16),
    ]
    if masked:
        scratch = [pltpu.VMEM((3, BLOCK, 4 * BLOCK), F32)] + scratch
        scratch += [pltpu.VMEM((2, BLOCK, 4 * BLOCK), F32), pltpu.VMEM((8, 4 * BLOCK), F32)]
        out_specs = out_specs + [pl.BlockSpec((1, 4, SPAN), lambda g, *_: (g, 0, 0))]
        out_shape = out_shape + [jax.ShapeDtypeStruct((count, 4, SPAN), F32)]
    return pl.pallas_call(
        functools.partial(backward_kernel, masked),
        grid_spec=pltpu.PrefetchScalarGridSpec(
            num_scalar_prefetch=1,
            grid=(count,),
            in_specs=[cols, kspec, vspec, cols, outs, logs] + ([vecs, lims, lims] if masked else []),
            out_specs=out_specs,
            scratch_shapes=scratch,
        ),
        out_shape=out_shape,
        cost_estimate=pl.CostEstimate(
            flops=10 * rows * length * width // parts, bytes_accessed=8 * length * width // parts,
            transcendentals=rows * length * 16 // parts
        ),
        name="attend_self_back" if masked else "attend_cross_back",
    )(table, query, keys_values, keys_values, grad, outs_in, logs_in, *extra)


def offset_index(half):
    place = jnp.arange(SPAN, dtype=jnp.int32)
    behind = jnp.where(place >= 2 * BLOCK, place - SPAN, place)
    return behind, jnp.clip(half - behind, 0, 2 * half - 1)


D = 1024
HEADS = 16
KV_HEADS = 8
BUCKETS = 32
EPS = 1e-06
CTX = ("line", "core")


def tn(left, right):
    return lax.dot_general(left, right, (((0,), (0,)), ((), ())), preferred_element_type=F32)


def norm_rows(values, gain):
    scale = lax.rsqrt(jnp.mean(values * values, axis=-1, keepdims=True) + EPS)
    normed = values * scale
    return normed, scale, (normed * gain).astype(BF16)


def norm_back(grad_out, normed, scale, gain):
    grad_gain = jnp.sum(grad_out * normed, axis=0)
    inner = grad_out * gain
    grad_in = scale * (inner - normed * jnp.mean(inner * normed, axis=-1, keepdims=True))
    return grad_in, grad_gain


def gelu_tanh(value):
    return jax.nn.gelu(value, approximate=True)


def partners(size, bit):
    return [(index, index ^ bit) for index in range(size)]


def bits_of(size):
    return [1 << place for place in range(size.bit_length() - 1)]


def cross(value, axis, bit):
    return lax.ppermute(value, axis, partners(lax.axis_size(axis), bit))


def swap(value):
    return cross(value, "core", 1)


def add(left, right):
    return (left.astype(F32) + right.astype(F32)).astype(BF16)


def place_kernel(spots, rows, me_ref, *refs):
    pieces, whole_ref, sems = refs[: len(spots)], refs[len(spots)], refs[len(spots) + 1]
    copies = []
    for index, (mask, offset) in enumerate(spots):
        count = pieces[index].shape[0]
        start = pl.multiple_of((me_ref[0] ^ mask) * rows + offset, count)
        copies.append(pltpu.make_async_copy(pieces[index], whole_ref.at[pl.ds(start, count), :], sems.at[index]))
    for copy in copies:
        copy.start()
    for copy in copies:
        copy.wait()


def place(me, pieces, spots, size, rows):
    anywhere = pl.BlockSpec(memory_space=pl.ANY)
    return pl.pallas_call(
        functools.partial(place_kernel, spots, rows),
        in_specs=[pl.BlockSpec(memory_space=pltpu.SMEM)] + [anywhere] * len(pieces),
        out_specs=anywhere,
        out_shape=jax.ShapeDtypeStruct((size * rows, pieces[0].shape[1]), BF16),
        scratch_shapes=[pltpu.SemaphoreType.DMA((len(pieces),))],
        name="place",
    )(me.reshape(1), *pieces)


class Lane:
    def __init__(self, steps):
        self.steps = steps
        self.result = None
        self.pending = next(steps)

    def push(self, arrived):
        try:
            self.pending = self.steps.send(arrived)
        except StopIteration as end:
            self.pending, self.result = None, end.value

    def take(self):
        while self.pending is not None:
            tick([self], ())
        return self.result

    def take(self):
        while self.pending is not None:
            tick([self], ())
        return self.result


def tick(lanes, live):
    active = [lane for lane in lanes if lane.pending is not None]
    live, arrived = lax.optimization_barrier((live, [lane.pending for lane in active]))
    for lane, value in zip(active, arrived):
        lane.push(value)
    return live


def swap_steps(*values):
    got = yield [swap(value) for value in values]
    return got


def sum_steps(value):
    for axis in ("core", "line", "fsdp"):
        for bit in bits_of(lax.axis_size(axis)):
            (got,) = yield [cross(value, axis, bit)]
            value = value + got
    return value


def small_steps(value):
    size = lax.axis_size("fsdp")
    me = lax.axis_index("fsdp")
    have = [(0, value)]
    for bit in bits_of(size):
        got = yield [cross(piece, "fsdp", bit) for _, piece in have]
        have = have + [(mask ^ bit, piece) for (mask, _), piece in zip(have, got)]
    whole = jnp.zeros((size, value.shape[0]), value.dtype)
    for mask, piece in have:
        whole = lax.dynamic_update_slice(whole, piece[None], (me ^ mask, 0))
    return whole


def columns_of(value, core):
    half = value.shape[1] // 2
    return lax.dynamic_slice_in_dim(value, core * half, half, axis=1)


def half_columns(parts):
    core = lax.axis_index("core")
    return jnp.concatenate([columns_of(part, core) for part in parts], axis=1)


def gather_steps(mine):
    size = lax.axis_size("fsdp")
    me = lax.axis_index("fsdp")
    rows, width = mine.shape
    bits = bits_of(size)
    half = rows // 2
    streams = [[(0, mine[stream * half : (stream + 1) * half])] for stream in range(2)]
    for step in range(len(bits)):
        chosen = [(bits if stream == 0 else bits[::-1])[step] for stream in range(2)]
        got = yield [[cross(piece, "fsdp", chosen[stream]) for _, piece in streams[stream]] for stream in range(2)]
        for stream in range(2):
            fresh = [(mask ^ chosen[stream], piece) for (mask, _), piece in zip(streams[stream], got[stream])]
            streams[stream] = streams[stream] + fresh
    spots = [(0, 0)] + [(mask, stream * half) for stream in range(2) for mask, _ in streams[stream][1:]]
    pieces = [mine] + [piece for stream in range(2) for _, piece in streams[stream][1:]]
    whole = place(me, pieces, spots, size, rows)
    whole, other = yield whole, swap(whole)
    return whole, other


def by_core(mine, other):
    first = lax.axis_index("core") == 0
    return jnp.where(first, mine, other), jnp.where(first, other, mine)


def grad_halves(*grads):
    core = lax.axis_index("core")
    mine = jnp.concatenate([columns_of(item, core) for item in grads], axis=1)
    return mine, jnp.concatenate([columns_of(item, 1 - core) for item in grads], axis=1)


def weight_grad(hidden, hidden_swapped, mine, arrived):
    both_hidden = jnp.concatenate([hidden, hidden_swapped], axis=0)
    both_grad = jnp.concatenate([mine, arrived], axis=0)
    return tn(both_hidden, both_grad).astype(BF16)


def split(value, axis, bit, place):
    mine = (lax.axis_index(axis) // bit) % 2
    keep = lax.dynamic_index_in_dim(value, mine, place, keepdims=False)
    return keep, lax.dynamic_index_in_dim(value, 1 - mine, place, keepdims=False)


def reduce_steps(partials, widths):
    size = lax.axis_size("fsdp")
    lines = lax.axis_size("line")
    rows = partials[0].shape[0] // size
    width = partials[0].shape[1]
    many = len(partials)
    bits = bits_of(size)
    folded = jnp.stack(partials).reshape([many] + [2] * len(bits) + [2, rows // 2, width])
    values = [lax.index_in_dim(folded, stream, 1 + len(bits), keepdims=False) for stream in range(2)]
    left = [bits[::-1], bits[::-1]]
    for step in range(len(bits)):
        chosen = [(bits if stream == 0 else bits[::-1])[step] for stream in range(2)]
        parts = [
            split(values[stream], "fsdp", chosen[stream], 1 + left[stream].index(chosen[stream]))
            for stream in range(2)
        ]
        got = yield [cross(parts[stream][1], "fsdp", chosen[stream]) for stream in range(2)]
        values = [add(parts[stream][0], got[stream]) for stream in range(2)]
        left = [[item for item in left[stream] if item != chosen[stream]] for stream in range(2)]
    shard = jnp.stack(values, axis=1)
    line_bits = bits_of(lines)
    value = shard.reshape([many] + [2] * len(line_bits) + [rows // lines, width])
    for bit in line_bits:
        keep, send = split(value, "line", bit, value.ndim - 3)
        (got,) = yield [cross(send, "line", bit)]
        value = add(keep, got)
    have = [(0, value)]
    for bit in line_bits[::-1]:
        got = yield [cross(piece, "line", bit) for _, piece in have]
        have = have + [(mask ^ bit, piece) for (mask, _), piece in zip(have, got)]
    have = [piece for _, piece in sorted(have, key=lambda item: item[0])]
    mine = jnp.stack(have)
    (other,) = yield [swap(mine)]
    me = lax.axis_index("line")
    outs = []
    for index in range(many):
        start = 0
        for wide in widths[index]:
            part = slice(start, start + wide // 2)
            both = jnp.concatenate(by_core(mine[:, index, :, part], other[:, index, :, part]), axis=2)
            ordered = [lax.dynamic_index_in_dim(both, me ^ entry, 0, keepdims=False) for entry in range(lines)]
            outs.append(jnp.concatenate(ordered, axis=0).astype(F32))
            start = start + wide // 2
    return outs


def gather_context_steps(value):
    have = [(0, value)]
    for bit in bits_of(lax.axis_size("line"))[::-1]:
        got = yield [cross(piece, "line", bit) for _, piece in have]
        have = have + [(mask ^ bit, piece) for (mask, _), piece in zip(have, got)]
    mine = jnp.concatenate([piece for _, piece in sorted(have, key=lambda item: item[0])], axis=0)
    (other,) = yield [swap(mine)]
    return jnp.concatenate([mine, other], axis=0)


def reduce_context_steps(value):
    lines = lax.axis_size("line")
    two, total, width = value.shape
    value = value.reshape(two, 2, lines, total // (2 * lines), width)
    (got,) = yield [swap(value[:, 1])]
    value = add(value[:, 0], got)
    for bit in bits_of(lines):
        value = value.reshape(two, value.shape[1] // 2, 2, value.shape[2], width)
        (got,) = yield [cross(value[:, :, 1], "line", bit)]
        value = add(value[:, :, 0], got)
    return value[:, 0]


def body(
    inputs, encoder, teacher, valid_mask, doc_ids, block_order, buckets,
    gain_self, w_query, w_key, w_value, w_out, gain_cross, c_query, c_key, c_value, c_out,
    gain_ffn, w_gate, w_up, w_down, bias_table,
):
    rows, width = inputs.shape[1:]
    lines = lax.axis_size("line")
    shards = lax.axis_size("fsdp")
    contexts = 2 * lines
    length = rows * contexts
    pair = rows // BLOCK
    token_total = length * shards
    key_width = KV_HEADS * HEAD
    context = lax.axis_index("line") * 2 + lax.axis_index("core")
    fsdp = lax.axis_index("fsdp")

    core = lax.axis_index("core")
    hidden_ff = w_gate.shape[1]
    joint = jnp.concatenate
    halves = D // 2
    share = gain_self.shape[0]

    def times(left, weight):
        return joint(by_core(nn(left, weight[0]), nn(left, weight[1])), axis=1)

    def times_back(grad, weight):
        return nt(columns_of(grad, core), weight[0]) + nt(columns_of(grad, 1 - core), weight[1])

    lane_qkv = Lane(gather_steps(half_columns([joint([w_query, w_key, w_value], axis=1)])))
    lane_small = Lane(small_steps(joint([gain_self, gain_cross, gain_ffn, bias_table.reshape(-1)])))
    mask_rows = valid_mask.reshape(rows).astype(F32)
    mid_shard = half_columns([w_out, c_query, joint([c_key, c_value], axis=1), c_out])
    mid_shard = tick([lane_qkv, lane_small], mid_shard)

    gu_shard = half_columns([joint([w_gate, w_up], axis=1)])
    wd_shard = half_columns([w_down])

    query_blocks = lax.dynamic_slice_in_dim(block_order, context * pair, pair)
    slots = jnp.arange(contexts * pair, dtype=jnp.int32)
    owner = slots // pair
    near = ((owner % 2) ^ core) * lines + ((owner // 2) ^ lax.axis_index("line"))
    slots_near = near * pair + slots % pair
    inverse = jnp.sum(jnp.where(block_order[None, :] == slots[:, None], slots_near[None, :], 0), axis=1)
    docs = doc_ids.reshape(length)
    query_docs = jnp.stack(
        [lax.dynamic_slice_in_dim(docs, query_blocks[index] * BLOCK, BLOCK) for index in range(pair)]
    )
    low = jnp.sum((docs[None, None, :] < query_docs[:, :, None]).astype(jnp.int32), axis=-1)
    high = jnp.sum((docs[None, None, :] <= query_docs[:, :, None]).astype(jnp.int32), axis=-1) - 1
    place_table = jnp.concatenate([query_blocks, low[:, 0] // BLOCK, inverse]).astype(jnp.int32)
    behind, index_of = offset_index(length)
    bucket_match = (jnp.take(buckets, index_of)[None, :] == jnp.arange(BUCKETS, dtype=jnp.int32)[:, None])

    gu_shard, wd_shard, low, high, place_table, bucket_match = tick(
        [lane_qkv, lane_small], (gu_shard, wd_shard, low, high, place_table, bucket_match)
    )

    small = lane_small.take()
    gain_one, gain_two, gain_three = [
        small[:, index * share : (index + 1) * share].reshape(D).astype(F32) for index in range(3)
    ]
    table_whole = small[:, 3 * share :].reshape(BUCKETS, HEADS)
    vectors = tn(table_whole, bucket_match.astype(BF16)).reshape(HEADS // 4, 4, SPAN)
    flat_in = inputs.reshape(rows, width).astype(F32)
    normed_one, scale_one, hidden_one = norm_rows(flat_in, gain_one)
    hidden_one, vectors = tick([lane_qkv], (hidden_one, vectors))
    extra = (vectors, low, high)

    qkv_mine, qkv_other = lane_qkv.take()
    lane_mid = Lane(gather_steps(mid_shard))
    query, pairs = by_core(nn(hidden_one, qkv_mine).astype(BF16), nn(hidden_one, qkv_other).astype(BF16))
    query, pairs = tick([], (query, pairs))

    lane_keys = Lane(gather_context_steps(pairs))
    gu_shard = tick([lane_keys, lane_mid], gu_shard)
    lane_hidden_one = Lane(swap_steps(hidden_one))
    wd_shard = tick([lane_keys, lane_mid, lane_hidden_one], wd_shard)
    lane_gu = Lane(gather_steps(gu_shard))
    tick([lane_keys, lane_mid], ())
    mid_mine, mid_other = lane_mid.take()
    wo, wcq, wckv, wco = [
        (mid_mine[:, index * halves : (index + 1) * halves], mid_other[:, index * halves : (index + 1) * halves])
        for index in range(4)
    ]
    encoder_rows = encoder.reshape(encoder.shape[1], width)
    encoder_pairs = times(encoder_rows, wckv).astype(BF16)
    pairs_whole, encoder_pairs = tick([], (lane_keys.take(), encoder_pairs))

    lane_encoder = Lane(gather_context_steps(encoder_pairs))
    lane_encoder_rows = Lane(swap_steps(encoder_rows))
    lane_count = Lane(sum_steps(jnp.broadcast_to(jnp.sum(mask_rows), (8, 128))))
    attention, outs_one, logs_one = attend(query, pairs_whole, place_table, extra, True)
    attention, outs_one, logs_one = tick([lane_gu, lane_encoder, lane_encoder_rows, lane_count], (attention, outs_one, logs_one))

    lane_attention = Lane(swap_steps(attention))
    mid_one = flat_in + times(attention, wo)
    normed_two, scale_two, hidden_two = norm_rows(mid_one, gain_two)
    cross_q = times(hidden_two, wcq).astype(BF16)
    mid_one, normed_two, hidden_two, cross_q, scale_two = tick(
        [lane_encoder, lane_attention, lane_count], (mid_one, normed_two, hidden_two, cross_q, scale_two)
    )
    tick([lane_encoder, lane_count], ())
    encoder_whole = lane_encoder.take()

    lane_hidden_two = Lane(swap_steps(hidden_two))
    crossed, outs_two, logs_two = attend(cross_q, encoder_whole, place_table, (), False)
    crossed, outs_two, logs_two = tick([lane_gu, lane_hidden_two, lane_count], (crossed, outs_two, logs_two))

    lane_wd = Lane(gather_steps(wd_shard))
    lane_crossed = Lane(swap_steps(crossed))
    mid_two = mid_one + times(crossed, wco)
    normed_three, scale_three, hidden_three = norm_rows(mid_two, gain_three)
    mid_two, normed_three, hidden_three, scale_three = tick(
        [lane_gu, lane_wd, lane_crossed, lane_count], (mid_two, normed_three, hidden_three, scale_three)
    )

    gu_mine, gu_other = lane_gu.take()
    lane_hidden_three = Lane(swap_steps(hidden_three))
    gate, up = by_core(nn(hidden_three, gu_mine), nn(hidden_three, gu_other))
    active, gelu_pull = jax.vjp(gelu_tanh, gate)
    mixed = (active * up).astype(BF16)
    mixed, gate, up, active = tick([lane_wd, lane_hidden_three], (mixed, gate, up, active))
    lane_mixed = Lane(swap_steps(mixed))
    tick([lane_wd, lane_mixed], ())

    wd_mine, wd_other = lane_wd.take()
    count = jnp.maximum(lane_count.take()[0, 0], 1.0)
    result = mid_two + times(mixed, (wd_mine, wd_other))
    layer_out = result.astype(BF16)
    diff = result - teacher.reshape(rows, width).astype(F32)
    squared_local = jnp.sum(mask_rows[:, None] * diff * diff)
    grad_result = token_total / count * mask_rows[:, None] * diff

    e_three = grad_result.astype(BF16)
    down_mine, down_away = grad_halves(e_three)
    grad_result, e_three, down_mine, down_away, squared_local, layer_out = tick(
        [], (grad_result, e_three, down_mine, down_away, squared_local, layer_out)
    )
    lane_down = Lane(swap_steps(down_away))
    grad_mixed = times_back(e_three, (wd_mine, wd_other))
    (gelu_slope,) = gelu_pull(grad_mixed * up)
    grad_gate = gelu_slope.astype(BF16)
    grad_up = (grad_mixed * active).astype(BF16)
    wide_mine, wide_away = grad_halves(grad_gate, grad_up)
    grad_gate, grad_up, wide_mine, wide_away = tick([lane_down], (grad_gate, grad_up, wide_mine, wide_away))

    lane_wide = Lane(swap_steps(wide_away))
    partial_down = weight_grad(mixed, lane_mixed.take()[0], down_mine, lane_down.take()[0])
    partial_down = tick([lane_wide], partial_down)

    lane_down = Lane(reduce_steps([partial_down], [(D,)]))
    partial_wide = weight_grad(hidden_three, lane_hidden_three.take()[0], wide_mine, lane_wide.take()[0])
    grad_hidden_three = times_back(joint([grad_gate, grad_up], axis=1), (gu_mine, gu_other))
    partial_wide, grad_hidden_three = tick([lane_down], (partial_wide, grad_hidden_three))

    lane_wide = Lane(reduce_steps([partial_wide], [(hidden_ff, hidden_ff)]))
    grad_norm_three, grad_gain_three = norm_back(grad_hidden_three, normed_three, scale_three, gain_three)
    grad_mid_two = grad_result + grad_norm_three

    e_two = grad_mid_two.astype(BF16)
    grad_cross = times_back(e_two, wco).astype(BF16)
    grad_cross_q, encoder_grad = attend_back(
        cross_q, encoder_whole, grad_cross, outs_two, logs_two, place_table, (), False
    )
    out_mine, out_away = grad_halves(e_two, grad_cross_q)
    grad_mid_two, grad_cross_q, encoder_grad, out_mine, out_away = tick(
        [lane_down, lane_wide], (grad_mid_two, grad_cross_q, encoder_grad, out_mine, out_away)
    )

    lane_encoder = Lane(reduce_context_steps(encoder_grad))
    lane_out = Lane(swap_steps(out_away))
    grad_norm_two, grad_gain_two = norm_back(times_back(grad_cross_q, wcq), normed_two, scale_two, gain_two)
    grad_mid_one = grad_mid_two + grad_norm_two

    e_one = grad_mid_one.astype(BF16)
    one_mine, one_away = grad_halves(e_one)
    grad_attention = times_back(e_one, wo).astype(BF16)
    grad_mid_one, one_mine, one_away, grad_attention = tick(
        [lane_down, lane_encoder, lane_out], (grad_mid_one, one_mine, one_away, grad_attention)
    )
    lane_one = Lane(swap_steps(one_away))

    def attend_part(part):
        return attend_back(
            query, pairs_whole, grad_attention, outs_one, logs_one, place_table, extra, True, part, 2
        )

    query_first, pairs_first, vectors_first = attend_part(0)
    query_first, pairs_first, vectors_first, grad_attention = tick(
        [lane_down, lane_wide, lane_encoder, lane_one], (query_first, pairs_first, vectors_first, grad_attention)
    )
    lane_first = Lane(reduce_context_steps(pairs_first))
    query_second, pairs_second, vectors_second = attend_part(1)
    grad_query = joint([query_first, query_second], axis=1)
    grad_vectors = joint([vectors_first, vectors_second], axis=0)
    query_mine, query_away = grad_halves(grad_query)
    pairs_second, grad_query, grad_vectors, query_mine, query_away = tick(
        [lane_down, lane_wide, lane_encoder, lane_first],
        (pairs_second, grad_query, grad_vectors, query_mine, query_away),
    )

    lane_second = Lane(reduce_context_steps(pairs_second))
    lane_query = Lane(swap_steps(query_away))
    arrived = lane_out.take()[0]
    partial_out = weight_grad(crossed, lane_crossed.take()[0], out_mine[:, :halves], arrived[:, :halves])
    partial_cross = weight_grad(hidden_two, lane_hidden_two.take()[0], out_mine[:, halves:], arrived[:, halves:])
    partial_one = weight_grad(attention, lane_attention.take()[0], one_mine, lane_one.take()[0])
    encoder_got = lane_encoder.take()
    encoder_mine = joint([encoder_got[0], encoder_got[1]], axis=1)
    keys_mine, keys_away = grad_halves(encoder_mine[:, :key_width], encoder_mine[:, key_width:])
    partial_out, partial_cross, partial_one, encoder_mine, keys_mine, keys_away = tick(
        [lane_first, lane_second, lane_down, lane_query],
        (partial_out, partial_cross, partial_one, encoder_mine, keys_mine, keys_away),
    )

    lane_keys = Lane(swap_steps(keys_away))
    partial_query = weight_grad(hidden_one, lane_hidden_one.take()[0], query_mine, lane_query.take()[0])
    lane_mid = Lane(reduce_steps([partial_out, partial_cross, partial_one, partial_query], [(D,)] * 4))
    grad_encoder = times_back(encoder_mine, wckv)
    grad_encoder = tick([lane_first, lane_second, lane_down, lane_wide, lane_keys], grad_encoder)

    partial_keys = weight_grad(encoder_rows, lane_encoder_rows.take()[0], keys_mine, lane_keys.take()[0])
    partial_keys = tick([lane_second, lane_mid], partial_keys)
    pairs_first, pairs_second = lane_first.take(), lane_second.take()
    mine = [joint([pairs_first[index], pairs_second[index]], axis=1) for index in range(2)]
    last_mine, last_away = grad_halves(mine[0], mine[1])
    mine, last_mine, last_away = tick([], (mine, last_mine, last_away))

    lane_last = Lane(swap_steps(last_away))
    tick([lane_last], ())
    partial_last = weight_grad(hidden_one, lane_hidden_one.take()[0], last_mine, lane_last.take()[0])
    partial_last = tick([lane_mid, lane_wide], partial_last)

    lane_last = Lane(reduce_steps([partial_last, partial_keys], [(key_width, key_width)] * 2))
    grad_packed = joint([grad_query, mine[0], mine[1]], axis=1)
    grad_norm_one, grad_gain_one = norm_back(
        times_back(grad_packed, (qkv_mine, qkv_other)), normed_one, scale_one, gain_one
    )
    grad_inputs = grad_mid_one + grad_norm_one

    grad_table = lax.dot_general(
        bucket_match.astype(F32) * ((behind >= 1 - BLOCK) & (behind < 2 * BLOCK)).astype(F32)[None, :],
        grad_vectors.reshape(HEADS, SPAN),
        (((1,), (1,)), ((), ())),
        precision=lax.Precision.HIGHEST,
        preferred_element_type=F32,
    )
    sums = jnp.concatenate(
        [
            grad_gain_one,
            grad_gain_two,
            grad_gain_three,
            grad_table.reshape(-1),
            jnp.broadcast_to(squared_local, (512,)),
        ]
    )
    sums, grad_inputs = tick([lane_last, lane_wide, lane_mid, lane_down], (sums.reshape(-1, 128), grad_inputs))
    lane_sums = Lane(sum_steps(sums))
    lanes = [lane_last, lane_wide, lane_mid, lane_down, lane_sums]
    while any(lane.pending is not None for lane in lanes):
        tick(lanes, ())
    sums = lane_sums.take().reshape(-1)
    (grad_down,) = lane_down.take()
    grad_gate_weight, grad_up_weight = lane_wide.take()
    grad_cross_out, grad_cross_query, grad_out_weight, grad_query_weight = lane_mid.take()
    grad_key_weight, grad_value_weight, grad_cross_key, grad_cross_value = lane_last.take()
    loss = sums[3 * D + 512] / (D * count)

    def shard_of(offset, amount):
        return lax.dynamic_slice_in_dim(sums, offset + fsdp * (amount // shards), amount // shards)

    return (
        layer_out.reshape(1, rows, width),
        loss,
        grad_inputs.reshape(1, rows, width),
        grad_encoder.reshape(1, encoder.shape[1], width),
        shard_of(0, D),
        grad_query_weight,
        grad_key_weight,
        grad_value_weight,
        grad_out_weight,
        shard_of(D, D),
        grad_cross_query,
        grad_cross_key,
        grad_cross_value,
        grad_cross_out,
        shard_of(2 * D, D),
        grad_gate_weight,
        grad_up_weight,
        grad_down,
        shard_of(3 * D, 512).reshape(BUCKETS // shards, HEADS),
    )


def solution(mesh):
    shape = mesh.devices.shape
    fine = Mesh(mesh.devices.reshape(shape[0] // 2, 2, shape[1]), ("line", "core", "fsdp"))
    tokens = P("fsdp", CTX, None)
    matrix = P("fsdp", None)
    vector = P("fsdp")
    weights = (vector, matrix, matrix, matrix, matrix, vector, matrix, matrix, matrix, matrix, vector)
    weights = weights + (matrix, matrix, matrix, matrix)
    in_specs = (tokens, tokens, tokens, P("fsdp", CTX), matrix, P(), P()) + weights
    out_specs = (tokens, P(), tokens, tokens) + weights
    return jax.shard_map(body, mesh=fine, in_specs=in_specs, out_specs=out_specs, check_vma=False)
```

```python
import functools
import jax
import jax.numpy as jnp
from jax import lax
from jax.experimental import pallas as pl
from jax.experimental.pallas import tpu as pltpu
from jax.sharding import Mesh
from jax.sharding import PartitionSpec as P

HEAD = 64
BLOCK = 128
NEGATIVE = -1e30
SPAN = 512
F32 = jnp.float32
BF16 = jnp.bfloat16


def nt(left, right):
    return lax.dot_general(left, right, (((1,), (1,)), ((), ())), preferred_element_type=F32)


def nn(left, right):
    return jnp.dot(left, right, preferred_element_type=F32)


def pad_heads(block):
    wide = block.astype(F32)
    lane = lax.broadcasted_iota(jnp.int32, (BLOCK, BLOCK), 1)
    parts = []
    for group in range(2):
        slab = wide[:, group * BLOCK : (group + 1) * BLOCK]
        turned = pltpu.roll(slab, HEAD, 1)
        keep = (lane < HEAD) if group == 0 else (lane >= HEAD)
        for part in range(2):
            source = slab if part == group else turned
            parts.append(jnp.where(keep, source, 0.0))
    return jnp.concatenate(parts, axis=0).astype(BF16)


def unpad_heads(turned):
    parts = [turned[:, index * BLOCK : (index + 1) * BLOCK].T for index in range(4)]
    return jnp.concatenate(parts, axis=1)


def fill_bias(vectors_ref, bias_ref):
    for head in range(4):
        row = jnp.broadcast_to(vectors_ref[0, head : head + 1, :], (BLOCK, SPAN))
        turned = pltpu.roll(row, 0, 1, stride=1, stride_axis=0)
        lanes = slice(head * BLOCK, (head + 1) * BLOCK)
        bias_ref[0, :, lanes] = turned[:, :BLOCK]
        bias_ref[1, :, lanes] = turned[:, BLOCK : 2 * BLOCK]
        bias_ref[2, :, lanes] = jnp.broadcast_to(row[:, BLOCK : BLOCK + 1], (BLOCK, BLOCK))


def four(tile):
    return jnp.concatenate([tile] * 4, axis=1)


def forward_kernel(masked, table, *refs):
    if masked:
        q_ref, k_ref, v_ref, vec_ref, low_ref, high_ref, a_ref, o_ref, l_ref, bias_ref, acc_ref = refs
        fill_bias(vec_ref, bias_ref)
    else:
        q_ref, k_ref, v_ref, a_ref, o_ref, l_ref, acc_ref = refs
    pairs = q_ref.shape[0] // BLOCK
    steps = k_ref.shape[0] // BLOCK
    row = lax.broadcasted_iota(jnp.int32, (BLOCK, BLOCK), 0)
    for index in range(pairs):
        rows = slice(index * BLOCK, (index + 1) * BLOCK)
        query = pad_heads(q_ref[rows, :])
        if masked:
            mine = table[index]
            first = table[pairs + index]
            low = low_ref[index : index + 1, :]
            high = high_ref[index : index + 1, :]

        def scores(step, near):
            if not masked:
                place = pl.multiple_of(step * BLOCK, BLOCK)
                return place, nt(k_ref[pl.ds(place, BLOCK), :], query)
            block = mine - step
            place = pl.multiple_of(table[2 * pairs + block] * BLOCK, BLOCK)
            raw = nt(k_ref[pl.ds(place, BLOCK), :], query)
            position = row + block * BLOCK
            allowed = position >= low
            if near:
                allowed = allowed & (position <= high)
                raw = raw + bias_ref[0]
            else:
                raw = raw + bias_ref[jnp.minimum(step, 2)]
            return place, jnp.where(four(allowed), raw, NEGATIVE)

        def gather(place, weight):
            turned = v_ref[pl.ds(place, BLOCK), :].astype(F32).T.astype(BF16)
            low_half = nn(turned[:HEAD], weight[:, : 2 * BLOCK])
            high_half = nn(turned[HEAD:], weight[:, 2 * BLOCK :])
            return jnp.concatenate([low_half, high_half], axis=1)

        place, raw = scores(0, True)
        top = jnp.max(raw, axis=0, keepdims=True)
        weight = jnp.exp(raw - top)
        total = jnp.sum(weight, axis=0, keepdims=True)
        acc_ref[...] = gather(place, weight.astype(BF16))

        def advance(step, carry):
            top, total = carry
            place, raw = scores(step, False)
            new_top = jnp.maximum(top, jnp.max(raw, axis=0, keepdims=True))
            factor = jnp.exp(top - new_top)
            weight = jnp.exp(raw - new_top)
            total = total * factor + jnp.sum(weight, axis=0, keepdims=True)
            acc_ref[...] = acc_ref[...] * factor + gather(place, weight.astype(BF16))
            return new_top, total

        count = mine - first + 1 if masked else steps
        top, total = lax.fori_loop(1, count, advance, (top, total))
        out = acc_ref[...] / total
        o_ref[0, index] = out
        l_ref[0, index] = jnp.broadcast_to(top + jnp.log(total), (8, 4 * BLOCK))
        a_ref[rows, :] = unpad_heads(out).astype(BF16)


def backward_kernel(masked, table, *refs):
    if masked:
        (q_ref, k_ref, v_ref, g_ref, o_ref, l_ref, vec_ref, low_ref, high_ref,
         dq_ref, dkv_ref, dvec_ref, bias_ref, dk_acc, dv_acc, dq_acc, near_ref, far_ref) = refs
        fill_bias(vec_ref, bias_ref)
        near_ref[...] = jnp.zeros_like(near_ref)
        far_ref[...] = jnp.zeros_like(far_ref)
    else:
        (q_ref, k_ref, v_ref, g_ref, o_ref, l_ref, dq_ref, dkv_ref, dk_acc, dv_acc, dq_acc) = refs
    pairs = q_ref.shape[0] // BLOCK
    steps = k_ref.shape[0] // BLOCK
    dk_acc[...] = jnp.zeros_like(dk_acc)
    dv_acc[...] = jnp.zeros_like(dv_acc)
    row = lax.broadcasted_iota(jnp.int32, (BLOCK, BLOCK), 0)
    for index in range(pairs):
        rows = slice(index * BLOCK, (index + 1) * BLOCK)
        query = pad_heads(q_ref[rows, :])
        grad = pad_heads(g_ref[rows, :])
        log_total = l_ref[0, index, :1, :]
        raw_grad = g_ref[rows, :].astype(F32)
        turned_grad = jnp.concatenate(
            [raw_grad[:, head * HEAD : (head + 1) * HEAD].T for head in range(4)], axis=1
        )
        delta = jnp.sum(turned_grad * o_ref[0, index], axis=0, keepdims=True)
        if masked:
            mine = table[index]
            first = table[pairs + index]
            low = low_ref[index : index + 1, :]
            high = high_ref[index : index + 1, :]

        def tile(step, near, start):
            if masked:
                block = mine - step
                place = pl.multiple_of(table[2 * pairs + block] * BLOCK, BLOCK)
            else:
                place = pl.multiple_of(step * BLOCK, BLOCK)
            keys = k_ref[pl.ds(place, BLOCK), :]
            raw = nt(keys, query)
            if masked:
                position = row + block * BLOCK
                allowed = position >= low
                if near:
                    allowed = allowed & (position <= high)
                    raw = raw + bias_ref[0]
                else:
                    raw = raw + bias_ref[jnp.minimum(step, 2)]
                raw = jnp.where(four(allowed), raw, NEGATIVE)
            prob = jnp.exp(raw - log_total)
            grad_prob = nt(v_ref[pl.ds(place, BLOCK), :], grad)
            grad_score = (prob * (grad_prob - delta)).astype(BF16)
            dv_acc[pl.ds(place, BLOCK), :] += nn(prob.astype(BF16), grad)
            dk_acc[pl.ds(place, BLOCK), :] += nn(grad_score, query)
            turned = keys.astype(F32).T.astype(BF16)
            part = jnp.concatenate(
                [nn(turned[:HEAD], grad_score[:, : 2 * BLOCK]), nn(turned[HEAD:], grad_score[:, 2 * BLOCK :])],
                axis=1,
            )
            if start:
                dq_acc[...] = part
            else:
                dq_acc[...] += part
            return grad_score

        grad_score = tile(0, True, True)
        if masked:
            near_ref[0] += grad_score.astype(F32)
            last = mine - first

            @pl.when(last >= 1)
            def _():
                near_ref[1] += tile(1, False, False).astype(F32)

            def advance(step, carry):
                wide = tile(step, False, False).astype(F32)
                far_ref[...] += jnp.sum(wide.reshape(BLOCK // 8, 8, 4 * BLOCK), axis=0)
                return carry

            lax.fori_loop(2, last + 1, advance, 0)
        else:

            def advance(step, carry):
                tile(step, False, False)
                return carry

            lax.fori_loop(1, steps, advance, 0)
        dq_ref[rows, :] = unpad_heads(dq_acc[...]).astype(BF16)
    dkv_ref[0] = dk_acc[...].astype(BF16)
    dkv_ref[1] = dv_acc[...].astype(BF16)
    if masked:
        rowid = lax.broadcasted_iota(jnp.int32, (BLOCK, SPAN), 0)
        lane = lax.broadcasted_iota(jnp.int32, (1, SPAN), 1)
        for head in range(4):
            lanes = slice(head * BLOCK, (head + 1) * BLOCK)
            wide = jnp.concatenate(
                [near_ref[0, :, lanes], near_ref[1, :, lanes], jnp.zeros((BLOCK, 2 * BLOCK), F32)], axis=1
            )
            bit = 1
            while bit < BLOCK:
                wide = jnp.where((rowid & bit) != 0, pltpu.roll(wide, SPAN - bit, 1), wide)
                bit = bit * 2
            sums = jnp.sum(wide, axis=0, keepdims=True)
            far = jnp.sum(far_ref[:, lanes])
            dvec_ref[0, head : head + 1, :] = sums + jnp.where(lane == BLOCK, far, 0.0)


def specs_of(rows, length, pairs, groups, first=0):
    cols = pl.BlockSpec((rows, 2 * BLOCK), lambda g, *_: (0, g + first))
    keys = pl.BlockSpec((length, BLOCK), lambda g, *_: (0, g + first))
    values = pl.BlockSpec((length, BLOCK), lambda g, *_: (0, groups + g + first))
    outs = pl.BlockSpec((1, pairs, HEAD, 4 * BLOCK), lambda g, *_: (g + first, 0, 0, 0))
    logs = pl.BlockSpec((1, pairs, 8, 4 * BLOCK), lambda g, *_: (g + first, 0, 0, 0))
    vecs = pl.BlockSpec((1, 4, SPAN), lambda g, *_: (g + first, 0, 0))
    lims = pl.BlockSpec((pairs, BLOCK), lambda g, *_: (0, 0))
    return cols, keys, values, outs, logs, vecs, lims


def attend(query, keys_values, table, extra, masked):
    rows, width = query.shape
    length = keys_values.shape[0]
    groups = width // (4 * HEAD)
    pairs = rows // BLOCK
    cols, kspec, vspec, outs, logs, vecs, lims = specs_of(rows, length, pairs, groups)
    scratch = [pltpu.VMEM((HEAD, 4 * BLOCK), F32)]
    if masked:
        scratch = [pltpu.VMEM((3, BLOCK, 4 * BLOCK), F32)] + scratch
    return pl.pallas_call(
        functools.partial(forward_kernel, masked),
        grid_spec=pltpu.PrefetchScalarGridSpec(
            num_scalar_prefetch=1,
            grid=(groups,),
            in_specs=[cols, kspec, vspec] + ([vecs, lims, lims] if masked else []),
            out_specs=[cols, outs, logs],
            scratch_shapes=scratch,
        ),
        out_shape=[
            jax.ShapeDtypeStruct((rows, width), BF16),
            jax.ShapeDtypeStruct((groups, pairs, HEAD, 4 * BLOCK), F32),
            jax.ShapeDtypeStruct((groups, pairs, 8, 4 * BLOCK), F32),
        ],
        cost_estimate=pl.CostEstimate(
            flops=4 * rows * length * width, bytes_accessed=4 * length * width, transcendentals=rows * length * 16
        ),
        name="attend_self" if masked else "attend_cross",
    )(table, query, keys_values, keys_values, *extra)


def attend_back(query, keys_values, grad, outs_in, logs_in, table, extra, masked, part=0, parts=1):
    rows, width = query.shape
    length = keys_values.shape[0]
    groups = width // (4 * HEAD)
    pairs = rows // BLOCK
    count = groups // parts
    cols, kspec, vspec, outs, logs, vecs, lims = specs_of(rows, length, pairs, groups, part * count)
    scratch = [pltpu.VMEM((length, BLOCK), F32), pltpu.VMEM((length, BLOCK), F32), pltpu.VMEM((HEAD, 4 * BLOCK), F32)]
    out_specs = [pl.BlockSpec((rows, 2 * BLOCK), lambda g, *_: (0, g)), pl.BlockSpec((2, length, BLOCK), lambda g, *_: (0, 0, g))]
    out_shape = [
        jax.ShapeDtypeStruct((rows, width // parts), BF16),
        jax.ShapeDtypeStruct((2, length, width // 2 // parts), BF16),
    ]
    if masked:
        scratch = [pltpu.VMEM((3, BLOCK, 4 * BLOCK), F32)] + scratch
        scratch += [pltpu.VMEM((2, BLOCK, 4 * BLOCK), F32), pltpu.VMEM((8, 4 * BLOCK), F32)]
        out_specs = out_specs + [pl.BlockSpec((1, 4, SPAN), lambda g, *_: (g, 0, 0))]
        out_shape = out_shape + [jax.ShapeDtypeStruct((count, 4, SPAN), F32)]
    return pl.pallas_call(
        functools.partial(backward_kernel, masked),
        grid_spec=pltpu.PrefetchScalarGridSpec(
            num_scalar_prefetch=1,
            grid=(count,),
            in_specs=[cols, kspec, vspec, cols, outs, logs] + ([vecs, lims, lims] if masked else []),
            out_specs=out_specs,
            scratch_shapes=scratch,
        ),
        out_shape=out_shape,
        cost_estimate=pl.CostEstimate(
            flops=10 * rows * length * width // parts, bytes_accessed=8 * length * width // parts,
            transcendentals=rows * length * 16 // parts
        ),
        name="attend_self_back" if masked else "attend_cross_back",
    )(table, query, keys_values, keys_values, grad, outs_in, logs_in, *extra)


def offset_index(half):
    place = jnp.arange(SPAN, dtype=jnp.int32)
    behind = jnp.where(place >= 2 * BLOCK, place - SPAN, place)
    return behind, jnp.clip(half - behind, 0, 2 * half - 1)


D = 1024
HEADS = 16
KV_HEADS = 8
BUCKETS = 32
EPS = 1e-06
CTX = ("line", "core")


def tn(left, right):
    return lax.dot_general(left, right, (((0,), (0,)), ((), ())), preferred_element_type=F32)


def norm_rows(values, gain):
    scale = lax.rsqrt(jnp.mean(values * values, axis=-1, keepdims=True) + EPS)
    normed = values * scale
    return normed, scale, (normed * gain).astype(BF16)


def norm_back(grad_out, normed, scale, gain):
    grad_gain = jnp.sum(grad_out * normed, axis=0)
    inner = grad_out * gain
    grad_in = scale * (inner - normed * jnp.mean(inner * normed, axis=-1, keepdims=True))
    return grad_in, grad_gain


def gelu_tanh(value):
    return jax.nn.gelu(value, approximate=True)


def partners(size, bit):
    return [(index, index ^ bit) for index in range(size)]


def bits_of(size):
    return [1 << place for place in range(size.bit_length() - 1)]


def cross(value, axis, bit):
    return lax.ppermute(value, axis, partners(lax.axis_size(axis), bit))


def swap(value):
    return cross(value, "core", 1)


def add(left, right):
    return (left.astype(F32) + right.astype(F32)).astype(BF16)


def place_kernel(spots, rows, me_ref, *refs):
    pieces, whole_ref, sems = refs[: len(spots)], refs[len(spots)], refs[len(spots) + 1]
    copies = []
    for index, (mask, offset) in enumerate(spots):
        count = pieces[index].shape[0]
        start = pl.multiple_of((me_ref[0] ^ mask) * rows + offset, count)
        copies.append(pltpu.make_async_copy(pieces[index], whole_ref.at[pl.ds(start, count), :], sems.at[index]))
    for copy in copies:
        copy.start()
    for copy in copies:
        copy.wait()


def place(me, pieces, spots, size, rows):
    anywhere = pl.BlockSpec(memory_space=pl.ANY)
    return pl.pallas_call(
        functools.partial(place_kernel, spots, rows),
        in_specs=[pl.BlockSpec(memory_space=pltpu.SMEM)] + [pl.BlockSpec(memory_space=pltpu.VMEM)] * len(pieces),
        out_specs=anywhere,
        out_shape=jax.ShapeDtypeStruct((size * rows, pieces[0].shape[1]), BF16),
        scratch_shapes=[pltpu.SemaphoreType.DMA((len(pieces),))],
        name="place",
    )(me.reshape(1), *pieces)


class Lane:
    def __init__(self, steps):
        self.steps = steps
        self.result = None
        self.pending = next(steps)

    def push(self, arrived):
        try:
            self.pending = self.steps.send(arrived)
        except StopIteration as end:
            self.pending, self.result = None, end.value

    def take(self):
        while self.pending is not None:
            tick([self], ())
        return self.result

    def take(self):
        while self.pending is not None:
            tick([self], ())
        return self.result


def tick(lanes, live):
    active = [lane for lane in lanes if lane.pending is not None]
    live, arrived = lax.optimization_barrier((live, [lane.pending for lane in active]))
    for lane, value in zip(active, arrived):
        lane.push(value)
    return live


def swap_steps(*values):
    got = yield [swap(value) for value in values]
    return got


def sum_steps(value):
    for axis in ("core", "line", "fsdp"):
        for bit in bits_of(lax.axis_size(axis)):
            (got,) = yield [cross(value, axis, bit)]
            value = value + got
    return value


def small_steps(value):
    size = lax.axis_size("fsdp")
    me = lax.axis_index("fsdp")
    have = [(0, value)]
    for bit in bits_of(size):
        got = yield [cross(piece, "fsdp", bit) for _, piece in have]
        have = have + [(mask ^ bit, piece) for (mask, _), piece in zip(have, got)]
    whole = jnp.zeros((size, value.shape[0]), value.dtype)
    for mask, piece in have:
        whole = lax.dynamic_update_slice(whole, piece[None], (me ^ mask, 0))
    return whole


def columns_of(value, core):
    half = value.shape[1] // 2
    return lax.dynamic_slice_in_dim(value, core * half, half, axis=1)


def half_columns(parts):
    core = lax.axis_index("core")
    return jnp.concatenate([columns_of(part, core) for part in parts], axis=1)


def gather_steps(mine):
    size = lax.axis_size("fsdp")
    me = lax.axis_index("fsdp")
    rows, width = mine.shape
    bits = bits_of(size)
    half = rows // 2
    streams = [[(0, mine[stream * half : (stream + 1) * half])] for stream in range(2)]
    for step in range(len(bits)):
        chosen = [(bits if stream == 0 else bits[::-1])[step] for stream in range(2)]
        got = yield [[cross(piece, "fsdp", chosen[stream]) for _, piece in streams[stream]] for stream in range(2)]
        for stream in range(2):
            fresh = [(mask ^ chosen[stream], piece) for (mask, _), piece in zip(streams[stream], got[stream])]
            streams[stream] = streams[stream] + fresh
    spots = [(0, 0)] + [(mask, stream * half) for stream in range(2) for mask, _ in streams[stream][1:]]
    pieces = [mine] + [piece for stream in range(2) for _, piece in streams[stream][1:]]
    whole = place(me, pieces, spots, size, rows)
    whole, other = yield whole, swap(whole)
    return whole, other


def by_core(mine, other):
    first = lax.axis_index("core") == 0
    return jnp.where(first, mine, other), jnp.where(first, other, mine)


def grad_halves(*grads):
    core = lax.axis_index("core")
    mine = jnp.concatenate([columns_of(item, core) for item in grads], axis=1)
    return mine, jnp.concatenate([columns_of(item, 1 - core) for item in grads], axis=1)


def weight_grad(hidden, hidden_swapped, mine, arrived):
    both_hidden = jnp.concatenate([hidden, hidden_swapped], axis=0)
    both_grad = jnp.concatenate([mine, arrived], axis=0)
    return tn(both_hidden, both_grad).astype(BF16)


def split(value, axis, bit, place):
    mine = (lax.axis_index(axis) // bit) % 2
    keep = lax.dynamic_index_in_dim(value, mine, place, keepdims=False)
    return keep, lax.dynamic_index_in_dim(value, 1 - mine, place, keepdims=False)


def reduce_steps(partials, widths):
    size = lax.axis_size("fsdp")
    lines = lax.axis_size("line")
    rows = partials[0].shape[0] // size
    width = partials[0].shape[1]
    many = len(partials)
    bits = bits_of(size)
    folded = jnp.stack(partials).reshape([many] + [2] * len(bits) + [2, rows // 2, width])
    values = [lax.index_in_dim(folded, stream, 1 + len(bits), keepdims=False) for stream in range(2)]
    left = [bits[::-1], bits[::-1]]
    for step in range(len(bits)):
        chosen = [(bits if stream == 0 else bits[::-1])[step] for stream in range(2)]
        parts = [
            split(values[stream], "fsdp", chosen[stream], 1 + left[stream].index(chosen[stream]))
            for stream in range(2)
        ]
        got = yield [cross(parts[stream][1], "fsdp", chosen[stream]) for stream in range(2)]
        values = [add(parts[stream][0], got[stream]) for stream in range(2)]
        left = [[item for item in left[stream] if item != chosen[stream]] for stream in range(2)]
    shard = jnp.stack(values, axis=1)
    line_bits = bits_of(lines)
    value = shard.reshape([many] + [2] * len(line_bits) + [rows // lines, width])
    for bit in line_bits:
        keep, send = split(value, "line", bit, value.ndim - 3)
        (got,) = yield [cross(send, "line", bit)]
        value = add(keep, got)
    have = [(0, value)]
    for bit in line_bits[::-1]:
        got = yield [cross(piece, "line", bit) for _, piece in have]
        have = have + [(mask ^ bit, piece) for (mask, _), piece in zip(have, got)]
    have = [piece for _, piece in sorted(have, key=lambda item: item[0])]
    mine = jnp.stack(have)
    (other,) = yield [swap(mine)]
    me = lax.axis_index("line")
    outs = []
    for index in range(many):
        start = 0
        for wide in widths[index]:
            part = slice(start, start + wide // 2)
            both = jnp.concatenate(by_core(mine[:, index, :, part], other[:, index, :, part]), axis=2)
            ordered = [lax.dynamic_index_in_dim(both, me ^ entry, 0, keepdims=False) for entry in range(lines)]
            outs.append(jnp.concatenate(ordered, axis=0).astype(F32))
            start = start + wide // 2
    return outs


def gather_context_steps(value):
    have = [(0, value)]
    for bit in bits_of(lax.axis_size("line"))[::-1]:
        got = yield [cross(piece, "line", bit) for _, piece in have]
        have = have + [(mask ^ bit, piece) for (mask, _), piece in zip(have, got)]
    mine = jnp.concatenate([piece for _, piece in sorted(have, key=lambda item: item[0])], axis=0)
    (other,) = yield [swap(mine)]
    return jnp.concatenate([mine, other], axis=0)


def reduce_context_steps(value):
    lines = lax.axis_size("line")
    two, total, width = value.shape
    value = value.reshape(two, 2, lines, total // (2 * lines), width)
    (got,) = yield [swap(value[:, 1])]
    value = add(value[:, 0], got)
    for bit in bits_of(lines):
        value = value.reshape(two, value.shape[1] // 2, 2, value.shape[2], width)
        (got,) = yield [cross(value[:, :, 1], "line", bit)]
        value = add(value[:, :, 0], got)
    return value[:, 0]


def body(
    inputs, encoder, teacher, valid_mask, doc_ids, block_order, buckets,
    gain_self, w_query, w_key, w_value, w_out, gain_cross, c_query, c_key, c_value, c_out,
    gain_ffn, w_gate, w_up, w_down, bias_table,
):
    rows, width = inputs.shape[1:]
    lines = lax.axis_size("line")
    shards = lax.axis_size("fsdp")
    contexts = 2 * lines
    length = rows * contexts
    pair = rows // BLOCK
    token_total = length * shards
    key_width = KV_HEADS * HEAD
    context = lax.axis_index("line") * 2 + lax.axis_index("core")
    fsdp = lax.axis_index("fsdp")

    core = lax.axis_index("core")
    hidden_ff = w_gate.shape[1]
    joint = jnp.concatenate
    halves = D // 2
    share = gain_self.shape[0]

    def times(left, weight):
        return joint(by_core(nn(left, weight[0]), nn(left, weight[1])), axis=1)

    def times_back(grad, weight):
        return nt(columns_of(grad, core), weight[0]) + nt(columns_of(grad, 1 - core), weight[1])

    lane_qkv = Lane(gather_steps(half_columns([joint([w_query, w_key, w_value], axis=1)])))
    lane_small = Lane(small_steps(joint([gain_self, gain_cross, gain_ffn, bias_table.reshape(-1)])))
    mask_rows = valid_mask.reshape(rows).astype(F32)
    mid_shard = half_columns([w_out, c_query, joint([c_key, c_value], axis=1), c_out])
    mid_shard = tick([lane_qkv, lane_small], mid_shard)

    gu_shard = half_columns([joint([w_gate, w_up], axis=1)])
    wd_shard = half_columns([w_down])

    query_blocks = lax.dynamic_slice_in_dim(block_order, context * pair, pair)
    slots = jnp.arange(contexts * pair, dtype=jnp.int32)
    owner = slots // pair
    near = ((owner % 2) ^ core) * lines + ((owner // 2) ^ lax.axis_index("line"))
    slots_near = near * pair + slots % pair
    inverse = jnp.sum(jnp.where(block_order[None, :] == slots[:, None], slots_near[None, :], 0), axis=1)
    docs = doc_ids.reshape(length)
    query_docs = jnp.stack(
        [lax.dynamic_slice_in_dim(docs, query_blocks[index] * BLOCK, BLOCK) for index in range(pair)]
    )
    low = jnp.sum((docs[None, None, :] < query_docs[:, :, None]).astype(jnp.int32), axis=-1)
    high = jnp.sum((docs[None, None, :] <= query_docs[:, :, None]).astype(jnp.int32), axis=-1) - 1
    place_table = jnp.concatenate([query_blocks, low[:, 0] // BLOCK, inverse]).astype(jnp.int32)
    behind, index_of = offset_index(length)
    bucket_match = (jnp.take(buckets, index_of)[None, :] == jnp.arange(BUCKETS, dtype=jnp.int32)[:, None])

    gu_shard, wd_shard, low, high, place_table, bucket_match = tick(
        [lane_qkv, lane_small], (gu_shard, wd_shard, low, high, place_table, bucket_match)
    )

    small = lane_small.take()
    gain_one, gain_two, gain_three = [
        small[:, index * share : (index + 1) * share].reshape(D).astype(F32) for index in range(3)
    ]
    table_whole = small[:, 3 * share :].reshape(BUCKETS, HEADS)
    vectors = tn(table_whole, bucket_match.astype(BF16)).reshape(HEADS // 4, 4, SPAN)
    flat_in = inputs.reshape(rows, width).astype(F32)
    normed_one, scale_one, hidden_one = norm_rows(flat_in, gain_one)
    hidden_one, vectors = tick([lane_qkv], (hidden_one, vectors))
    extra = (vectors, low, high)

    qkv_mine, qkv_other = lane_qkv.take()
    lane_mid = Lane(gather_steps(mid_shard))
    query, pairs = by_core(nn(hidden_one, qkv_mine).astype(BF16), nn(hidden_one, qkv_other).astype(BF16))
    query, pairs = tick([], (query, pairs))

    lane_keys = Lane(gather_context_steps(pairs))
    gu_shard = tick([lane_keys, lane_mid], gu_shard)
    lane_hidden_one = Lane(swap_steps(hidden_one))
    wd_shard = tick([lane_keys, lane_mid, lane_hidden_one], wd_shard)
    lane_gu = Lane(gather_steps(gu_shard))
    tick([lane_keys, lane_mid], ())
    mid_mine, mid_other = lane_mid.take()
    wo, wcq, wckv, wco = [
        (mid_mine[:, index * halves : (index + 1) * halves], mid_other[:, index * halves : (index + 1) * halves])
        for index in range(4)
    ]
    encoder_rows = encoder.reshape(encoder.shape[1], width)
    encoder_pairs = times(encoder_rows, wckv).astype(BF16)
    pairs_whole, encoder_pairs = tick([], (lane_keys.take(), encoder_pairs))

    lane_encoder = Lane(gather_context_steps(encoder_pairs))
    lane_encoder_rows = Lane(swap_steps(encoder_rows))
    lane_count = Lane(sum_steps(jnp.broadcast_to(jnp.sum(mask_rows), (8, 128))))
    attention, outs_one, logs_one = attend(query, pairs_whole, place_table, extra, True)
    attention, outs_one, logs_one = tick([lane_gu, lane_encoder, lane_encoder_rows, lane_count], (attention, outs_one, logs_one))

    lane_attention = Lane(swap_steps(attention))
    mid_one = flat_in + times(attention, wo)
    normed_two, scale_two, hidden_two = norm_rows(mid_one, gain_two)
    cross_q = times(hidden_two, wcq).astype(BF16)
    mid_one, normed_two, hidden_two, cross_q, scale_two = tick(
        [lane_encoder, lane_attention, lane_count], (mid_one, normed_two, hidden_two, cross_q, scale_two)
    )
    tick([lane_encoder, lane_count], ())
    encoder_whole = lane_encoder.take()

    lane_hidden_two = Lane(swap_steps(hidden_two))
    crossed, outs_two, logs_two = attend(cross_q, encoder_whole, place_table, (), False)
    crossed, outs_two, logs_two = tick([lane_gu, lane_hidden_two, lane_count], (crossed, outs_two, logs_two))

    lane_wd = Lane(gather_steps(wd_shard))
    lane_crossed = Lane(swap_steps(crossed))
    mid_two = mid_one + times(crossed, wco)
    normed_three, scale_three, hidden_three = norm_rows(mid_two, gain_three)
    mid_two, normed_three, hidden_three, scale_three = tick(
        [lane_gu, lane_wd, lane_crossed, lane_count], (mid_two, normed_three, hidden_three, scale_three)
    )

    gu_mine, gu_other = lane_gu.take()
    lane_hidden_three = Lane(swap_steps(hidden_three))
    gate, up = by_core(nn(hidden_three, gu_mine), nn(hidden_three, gu_other))
    active, gelu_pull = jax.vjp(gelu_tanh, gate)
    mixed = (active * up).astype(BF16)
    mixed, gate, up, active = tick([lane_wd, lane_hidden_three], (mixed, gate, up, active))
    lane_mixed = Lane(swap_steps(mixed))
    tick([lane_wd, lane_mixed], ())

    wd_mine, wd_other = lane_wd.take()
    count = jnp.maximum(lane_count.take()[0, 0], 1.0)
    result = mid_two + times(mixed, (wd_mine, wd_other))
    layer_out = result.astype(BF16)
    diff = result - teacher.reshape(rows, width).astype(F32)
    squared_local = jnp.sum(mask_rows[:, None] * diff * diff)
    grad_result = token_total / count * mask_rows[:, None] * diff

    e_three = grad_result.astype(BF16)
    down_mine, down_away = grad_halves(e_three)
    grad_result, e_three, down_mine, down_away, squared_local, layer_out = tick(
        [], (grad_result, e_three, down_mine, down_away, squared_local, layer_out)
    )
    lane_down = Lane(swap_steps(down_away))
    grad_mixed = times_back(e_three, (wd_mine, wd_other))
    (gelu_slope,) = gelu_pull(grad_mixed * up)
    grad_gate = gelu_slope.astype(BF16)
    grad_up = (grad_mixed * active).astype(BF16)
    wide_mine, wide_away = grad_halves(grad_gate, grad_up)
    grad_gate, grad_up, wide_mine, wide_away = tick([lane_down], (grad_gate, grad_up, wide_mine, wide_away))

    lane_wide = Lane(swap_steps(wide_away))
    partial_down = weight_grad(mixed, lane_mixed.take()[0], down_mine, lane_down.take()[0])
    partial_down = tick([lane_wide], partial_down)

    lane_down = Lane(reduce_steps([partial_down], [(D,)]))
    partial_wide = weight_grad(hidden_three, lane_hidden_three.take()[0], wide_mine, lane_wide.take()[0])
    grad_hidden_three = times_back(joint([grad_gate, grad_up], axis=1), (gu_mine, gu_other))
    partial_wide, grad_hidden_three = tick([lane_down], (partial_wide, grad_hidden_three))

    lane_wide = Lane(reduce_steps([partial_wide], [(hidden_ff, hidden_ff)]))
    grad_norm_three, grad_gain_three = norm_back(grad_hidden_three, normed_three, scale_three, gain_three)
    grad_mid_two = grad_result + grad_norm_three

    e_two = grad_mid_two.astype(BF16)
    grad_cross = times_back(e_two, wco).astype(BF16)
    grad_cross_q, encoder_grad = attend_back(
        cross_q, encoder_whole, grad_cross, outs_two, logs_two, place_table, (), False
    )
    out_mine, out_away = grad_halves(e_two, grad_cross_q)
    grad_mid_two, grad_cross_q, encoder_grad, out_mine, out_away = tick(
        [lane_down, lane_wide], (grad_mid_two, grad_cross_q, encoder_grad, out_mine, out_away)
    )

    lane_encoder = Lane(reduce_context_steps(encoder_grad))
    lane_out = Lane(swap_steps(out_away))
    grad_norm_two, grad_gain_two = norm_back(times_back(grad_cross_q, wcq), normed_two, scale_two, gain_two)
    grad_mid_one = grad_mid_two + grad_norm_two

    e_one = grad_mid_one.astype(BF16)
    one_mine, one_away = grad_halves(e_one)
    grad_attention = times_back(e_one, wo).astype(BF16)
    grad_mid_one, one_mine, one_away, grad_attention = tick(
        [lane_down, lane_encoder, lane_out], (grad_mid_one, one_mine, one_away, grad_attention)
    )
    lane_one = Lane(swap_steps(one_away))

    def attend_part(part):
        return attend_back(
            query, pairs_whole, grad_attention, outs_one, logs_one, place_table, extra, True, part, 2
        )

    query_first, pairs_first, vectors_first = attend_part(0)
    query_first, pairs_first, vectors_first, grad_attention = tick(
        [lane_down, lane_wide, lane_encoder, lane_one], (query_first, pairs_first, vectors_first, grad_attention)
    )
    lane_first = Lane(reduce_context_steps(pairs_first))
    query_second, pairs_second, vectors_second = attend_part(1)
    grad_query = joint([query_first, query_second], axis=1)
    grad_vectors = joint([vectors_first, vectors_second], axis=0)
    query_mine, query_away = grad_halves(grad_query)
    pairs_second, grad_query, grad_vectors, query_mine, query_away = tick(
        [lane_down, lane_wide, lane_encoder, lane_first],
        (pairs_second, grad_query, grad_vectors, query_mine, query_away),
    )

    lane_second = Lane(reduce_context_steps(pairs_second))
    lane_query = Lane(swap_steps(query_away))
    arrived = lane_out.take()[0]
    partial_out = weight_grad(crossed, lane_crossed.take()[0], out_mine[:, :halves], arrived[:, :halves])
    partial_cross = weight_grad(hidden_two, lane_hidden_two.take()[0], out_mine[:, halves:], arrived[:, halves:])
    partial_one = weight_grad(attention, lane_attention.take()[0], one_mine, lane_one.take()[0])
    encoder_got = lane_encoder.take()
    encoder_mine = joint([encoder_got[0], encoder_got[1]], axis=1)
    keys_mine, keys_away = grad_halves(encoder_mine[:, :key_width], encoder_mine[:, key_width:])
    partial_out, partial_cross, partial_one, encoder_mine, keys_mine, keys_away = tick(
        [lane_first, lane_second, lane_down, lane_query],
        (partial_out, partial_cross, partial_one, encoder_mine, keys_mine, keys_away),
    )

    lane_keys = Lane(swap_steps(keys_away))
    partial_query = weight_grad(hidden_one, lane_hidden_one.take()[0], query_mine, lane_query.take()[0])
    lane_mid = Lane(reduce_steps([partial_out, partial_cross, partial_one, partial_query], [(D,)] * 4))
    grad_encoder = times_back(encoder_mine, wckv)
    grad_encoder = tick([lane_first, lane_second, lane_down, lane_wide, lane_keys], grad_encoder)

    partial_keys = weight_grad(encoder_rows, lane_encoder_rows.take()[0], keys_mine, lane_keys.take()[0])
    partial_keys = tick([lane_second, lane_mid], partial_keys)
    pairs_first, pairs_second = lane_first.take(), lane_second.take()
    mine = [joint([pairs_first[index], pairs_second[index]], axis=1) for index in range(2)]
    last_mine, last_away = grad_halves(mine[0], mine[1])
    mine, last_mine, last_away = tick([], (mine, last_mine, last_away))

    lane_last = Lane(swap_steps(last_away))
    tick([lane_last], ())
    partial_last = weight_grad(hidden_one, lane_hidden_one.take()[0], last_mine, lane_last.take()[0])
    partial_last = tick([lane_mid, lane_wide], partial_last)

    lane_last = Lane(reduce_steps([partial_last, partial_keys], [(key_width, key_width)] * 2))
    grad_packed = joint([grad_query, mine[0], mine[1]], axis=1)
    grad_norm_one, grad_gain_one = norm_back(
        times_back(grad_packed, (qkv_mine, qkv_other)), normed_one, scale_one, gain_one
    )
    grad_inputs = grad_mid_one + grad_norm_one

    grad_table = lax.dot_general(
        bucket_match.astype(F32) * ((behind >= 1 - BLOCK) & (behind < 2 * BLOCK)).astype(F32)[None, :],
        grad_vectors.reshape(HEADS, SPAN),
        (((1,), (1,)), ((), ())),
        precision=lax.Precision.HIGHEST,
        preferred_element_type=F32,
    )
    sums = jnp.concatenate(
        [
            grad_gain_one,
            grad_gain_two,
            grad_gain_three,
            grad_table.reshape(-1),
            jnp.broadcast_to(squared_local, (512,)),
        ]
    )
    sums, grad_inputs = tick([lane_last, lane_wide, lane_mid, lane_down], (sums.reshape(-1, 128), grad_inputs))
    lane_sums = Lane(sum_steps(sums))
    lanes = [lane_last, lane_wide, lane_mid, lane_down, lane_sums]
    while any(lane.pending is not None for lane in lanes):
        tick(lanes, ())
    sums = lane_sums.take().reshape(-1)
    (grad_down,) = lane_down.take()
    grad_gate_weight, grad_up_weight = lane_wide.take()
    grad_cross_out, grad_cross_query, grad_out_weight, grad_query_weight = lane_mid.take()
    grad_key_weight, grad_value_weight, grad_cross_key, grad_cross_value = lane_last.take()
    loss = sums[3 * D + 512] / (D * count)

    def shard_of(offset, amount):
        return lax.dynamic_slice_in_dim(sums, offset + fsdp * (amount // shards), amount // shards)

    return (
        layer_out.reshape(1, rows, width),
        loss,
        grad_inputs.reshape(1, rows, width),
        grad_encoder.reshape(1, encoder.shape[1], width),
        shard_of(0, D),
        grad_query_weight,
        grad_key_weight,
        grad_value_weight,
        grad_out_weight,
        shard_of(D, D),
        grad_cross_query,
        grad_cross_key,
        grad_cross_value,
        grad_cross_out,
        shard_of(2 * D, D),
        grad_gate_weight,
        grad_up_weight,
        grad_down,
        shard_of(3 * D, 512).reshape(BUCKETS // shards, HEADS),
    )


def solution(mesh):
    shape = mesh.devices.shape
    fine = Mesh(mesh.devices.reshape(shape[0] // 2, 2, shape[1]), ("line", "core", "fsdp"))
    tokens = P("fsdp", CTX, None)
    matrix = P("fsdp", None)
    vector = P("fsdp")
    weights = (vector, matrix, matrix, matrix, matrix, vector, matrix, matrix, matrix, matrix, vector)
    weights = weights + (matrix, matrix, matrix, matrix)
    in_specs = (tokens, tokens, tokens, P("fsdp", CTX), matrix, P(), P()) + weights
    out_specs = (tokens, P(), tokens, tokens) + weights
    return jax.shard_map(body, mesh=fine, in_specs=in_specs, out_specs=out_specs, check_vma=False)
```

```python
import functools
import jax
import jax.numpy as jnp
from jax import lax
from jax.experimental import pallas as pl
from jax.experimental.pallas import tpu as pltpu
from jax.sharding import Mesh
from jax.sharding import PartitionSpec as P

HEAD = 64
BLOCK = 128
NEGATIVE = -1e30
SPAN = 512
F32 = jnp.float32
BF16 = jnp.bfloat16


def nt(left, right):
    return lax.dot_general(left, right, (((1,), (1,)), ((), ())), preferred_element_type=F32)


def nn(left, right):
    return jnp.dot(left, right, preferred_element_type=F32)


def pad_heads(block):
    wide = block.astype(F32)
    lane = lax.broadcasted_iota(jnp.int32, (BLOCK, BLOCK), 1)
    parts = []
    for group in range(2):
        slab = wide[:, group * BLOCK : (group + 1) * BLOCK]
        turned = pltpu.roll(slab, HEAD, 1)
        keep = (lane < HEAD) if group == 0 else (lane >= HEAD)
        for part in range(2):
            source = slab if part == group else turned
            parts.append(jnp.where(keep, source, 0.0))
    return jnp.concatenate(parts, axis=0).astype(BF16)


def unpad_heads(turned):
    parts = [turned[:, index * BLOCK : (index + 1) * BLOCK].T for index in range(4)]
    return jnp.concatenate(parts, axis=1)


def fill_bias(vectors_ref, bias_ref):
    for head in range(4):
        row = jnp.broadcast_to(vectors_ref[0, head : head + 1, :], (BLOCK, SPAN))
        turned = pltpu.roll(row, 0, 1, stride=1, stride_axis=0)
        lanes = slice(head * BLOCK, (head + 1) * BLOCK)
        bias_ref[0, :, lanes] = turned[:, :BLOCK]
        bias_ref[1, :, lanes] = turned[:, BLOCK : 2 * BLOCK]
        bias_ref[2, :, lanes] = jnp.broadcast_to(row[:, BLOCK : BLOCK + 1], (BLOCK, BLOCK))


def four(tile):
    return jnp.concatenate([tile] * 4, axis=1)


def forward_kernel(masked, table, *refs):
    if masked:
        q_ref, k_ref, v_ref, vec_ref, low_ref, high_ref, a_ref, o_ref, l_ref, bias_ref, acc_ref = refs
        fill_bias(vec_ref, bias_ref)
    else:
        q_ref, k_ref, v_ref, a_ref, o_ref, l_ref, acc_ref = refs
    pairs = q_ref.shape[0] // BLOCK
    steps = k_ref.shape[0] // BLOCK
    row = lax.broadcasted_iota(jnp.int32, (BLOCK, BLOCK), 0)
    for index in range(pairs):
        rows = slice(index * BLOCK, (index + 1) * BLOCK)
        query = pad_heads(q_ref[rows, :])
        if masked:
            mine = table[index]
            first = table[pairs + index]
            low = low_ref[index : index + 1, :]
            high = high_ref[index : index + 1, :]

        def scores(step, near):
            if not masked:
                place = pl.multiple_of(step * BLOCK, BLOCK)
                return place, nt(k_ref[pl.ds(place, BLOCK), :], query)
            block = mine - step
            place = pl.multiple_of(table[2 * pairs + block] * BLOCK, BLOCK)
            raw = nt(k_ref[pl.ds(place, BLOCK), :], query)
            position = row + block * BLOCK
            allowed = position >= low
            if near:
                allowed = allowed & (position <= high)
                raw = raw + bias_ref[0]
            else:
                raw = raw + bias_ref[jnp.minimum(step, 2)]
            return place, jnp.where(four(allowed), raw, NEGATIVE)

        def gather(place, weight):
            turned = v_ref[pl.ds(place, BLOCK), :].astype(F32).T.astype(BF16)
            low_half = nn(turned[:HEAD], weight[:, : 2 * BLOCK])
            high_half = nn(turned[HEAD:], weight[:, 2 * BLOCK :])
            return jnp.concatenate([low_half, high_half], axis=1)

        place, raw = scores(0, True)
        top = jnp.max(raw, axis=0, keepdims=True)
        weight = jnp.exp(raw - top)
        total = jnp.sum(weight, axis=0, keepdims=True)
        acc_ref[...] = gather(place, weight.astype(BF16))

        def advance(step, carry):
            top, total = carry
            place, raw = scores(step, False)
            new_top = jnp.maximum(top, jnp.max(raw, axis=0, keepdims=True))
            factor = jnp.exp(top - new_top)
            weight = jnp.exp(raw - new_top)
            total = total * factor + jnp.sum(weight, axis=0, keepdims=True)
            acc_ref[...] = acc_ref[...] * factor + gather(place, weight.astype(BF16))
            return new_top, total

        count = mine - first + 1 if masked else steps
        top, total = lax.fori_loop(1, count, advance, (top, total))
        out = acc_ref[...] / total
        o_ref[0, index] = out
        l_ref[0, index] = jnp.broadcast_to(top + jnp.log(total), (8, 4 * BLOCK))
        a_ref[rows, :] = unpad_heads(out).astype(BF16)


def backward_kernel(masked, table, *refs):
    if masked:
        (q_ref, k_ref, v_ref, g_ref, o_ref, l_ref, vec_ref, low_ref, high_ref,
         dq_ref, dkv_ref, dvec_ref, bias_ref, dk_acc, dv_acc, dq_acc, near_ref, far_ref) = refs
        fill_bias(vec_ref, bias_ref)
        near_ref[...] = jnp.zeros_like(near_ref)
        far_ref[...] = jnp.zeros_like(far_ref)
    else:
        (q_ref, k_ref, v_ref, g_ref, o_ref, l_ref, dq_ref, dkv_ref, dk_acc, dv_acc, dq_acc) = refs
    pairs = q_ref.shape[0] // BLOCK
    steps = k_ref.shape[0] // BLOCK
    dk_acc[...] = jnp.zeros_like(dk_acc)
    dv_acc[...] = jnp.zeros_like(dv_acc)
    row = lax.broadcasted_iota(jnp.int32, (BLOCK, BLOCK), 0)
    for index in range(pairs):
        rows = slice(index * BLOCK, (index + 1) * BLOCK)
        query = pad_heads(q_ref[rows, :])
        grad = pad_heads(g_ref[rows, :])
        log_total = l_ref[0, index, :1, :]
        raw_grad = g_ref[rows, :].astype(F32)
        turned_grad = jnp.concatenate(
            [raw_grad[:, head * HEAD : (head + 1) * HEAD].T for head in range(4)], axis=1
        )
        delta = jnp.sum(turned_grad * o_ref[0, index], axis=0, keepdims=True)
        if masked:
            mine = table[index]
            first = table[pairs + index]
            low = low_ref[index : index + 1, :]
            high = high_ref[index : index + 1, :]

        def tile(step, near, start):
            if masked:
                block = mine - step
                place = pl.multiple_of(table[2 * pairs + block] * BLOCK, BLOCK)
            else:
                place = pl.multiple_of(step * BLOCK, BLOCK)
            keys = k_ref[pl.ds(place, BLOCK), :]
            raw = nt(keys, query)
            if masked:
                position = row + block * BLOCK
                allowed = position >= low
                if near:
                    allowed = allowed & (position <= high)
                    raw = raw + bias_ref[0]
                else:
                    raw = raw + bias_ref[jnp.minimum(step, 2)]
                raw = jnp.where(four(allowed), raw, NEGATIVE)
            prob = jnp.exp(raw - log_total)
            grad_prob = nt(v_ref[pl.ds(place, BLOCK), :], grad)
            grad_score = (prob * (grad_prob - delta)).astype(BF16)
            dv_acc[pl.ds(place, BLOCK), :] += nn(prob.astype(BF16), grad)
            dk_acc[pl.ds(place, BLOCK), :] += nn(grad_score, query)
            turned = keys.astype(F32).T.astype(BF16)
            part = jnp.concatenate(
                [nn(turned[:HEAD], grad_score[:, : 2 * BLOCK]), nn(turned[HEAD:], grad_score[:, 2 * BLOCK :])],
                axis=1,
            )
            if start:
                dq_acc[...] = part
            else:
                dq_acc[...] += part
            return grad_score

        grad_score = tile(0, True, True)
        if masked:
            near_ref[0] += grad_score.astype(F32)
            last = mine - first

            @pl.when(last >= 1)
            def _():
                near_ref[1] += tile(1, False, False).astype(F32)

            def advance(step, carry):
                wide = tile(step, False, False).astype(F32)
                far_ref[...] += jnp.sum(wide.reshape(BLOCK // 8, 8, 4 * BLOCK), axis=0)
                return carry

            lax.fori_loop(2, last + 1, advance, 0)
        else:

            def advance(step, carry):
                tile(step, False, False)
                return carry

            lax.fori_loop(1, steps, advance, 0)
        dq_ref[rows, :] = unpad_heads(dq_acc[...]).astype(BF16)
    dkv_ref[0] = dk_acc[...].astype(BF16)
    dkv_ref[1] = dv_acc[...].astype(BF16)
    if masked:
        rowid = lax.broadcasted_iota(jnp.int32, (BLOCK, SPAN), 0)
        lane = lax.broadcasted_iota(jnp.int32, (1, SPAN), 1)
        for head in range(4):
            lanes = slice(head * BLOCK, (head + 1) * BLOCK)
            wide = jnp.concatenate(
                [near_ref[0, :, lanes], near_ref[1, :, lanes], jnp.zeros((BLOCK, 2 * BLOCK), F32)], axis=1
            )
            bit = 1
            while bit < BLOCK:
                wide = jnp.where((rowid & bit) != 0, pltpu.roll(wide, SPAN - bit, 1), wide)
                bit = bit * 2
            sums = jnp.sum(wide, axis=0, keepdims=True)
            far = jnp.sum(far_ref[:, lanes])
            dvec_ref[0, head : head + 1, :] = sums + jnp.where(lane == BLOCK, far, 0.0)


def specs_of(rows, length, pairs, groups, first=0):
    cols = pl.BlockSpec((rows, 2 * BLOCK), lambda g, *_: (0, g + first))
    keys = pl.BlockSpec((length, BLOCK), lambda g, *_: (0, g + first))
    values = pl.BlockSpec((length, BLOCK), lambda g, *_: (0, groups + g + first))
    outs = pl.BlockSpec((1, pairs, HEAD, 4 * BLOCK), lambda g, *_: (g + first, 0, 0, 0))
    logs = pl.BlockSpec((1, pairs, 8, 4 * BLOCK), lambda g, *_: (g + first, 0, 0, 0))
    vecs = pl.BlockSpec((1, 4, SPAN), lambda g, *_: (g + first, 0, 0))
    lims = pl.BlockSpec((pairs, BLOCK), lambda g, *_: (0, 0))
    return cols, keys, values, outs, logs, vecs, lims


def attend(query, keys_values, table, extra, masked):
    rows, width = query.shape
    length = keys_values.shape[0]
    groups = width // (4 * HEAD)
    pairs = rows // BLOCK
    cols, kspec, vspec, outs, logs, vecs, lims = specs_of(rows, length, pairs, groups)
    scratch = [pltpu.VMEM((HEAD, 4 * BLOCK), F32)]
    if masked:
        scratch = [pltpu.VMEM((3, BLOCK, 4 * BLOCK), F32)] + scratch
    return pl.pallas_call(
        functools.partial(forward_kernel, masked),
        grid_spec=pltpu.PrefetchScalarGridSpec(
            num_scalar_prefetch=1,
            grid=(groups,),
            in_specs=[cols, kspec, vspec] + ([vecs, lims, lims] if masked else []),
            out_specs=[cols, outs, logs],
            scratch_shapes=scratch,
        ),
        out_shape=[
            jax.ShapeDtypeStruct((rows, width), BF16),
            jax.ShapeDtypeStruct((groups, pairs, HEAD, 4 * BLOCK), F32),
            jax.ShapeDtypeStruct((groups, pairs, 8, 4 * BLOCK), F32),
        ],
        cost_estimate=pl.CostEstimate(
            flops=4 * rows * length * width, bytes_accessed=4 * length * width, transcendentals=rows * length * 16
        ),
        name="attend_self" if masked else "attend_cross",
    )(table, query, keys_values, keys_values, *extra)


def attend_back(query, keys_values, grad, outs_in, logs_in, table, extra, masked, part=0, parts=1):
    rows, width = query.shape
    length = keys_values.shape[0]
    groups = width // (4 * HEAD)
    pairs = rows // BLOCK
    count = groups // parts
    cols, kspec, vspec, outs, logs, vecs, lims = specs_of(rows, length, pairs, groups, part * count)
    scratch = [pltpu.VMEM((length, BLOCK), F32), pltpu.VMEM((length, BLOCK), F32), pltpu.VMEM((HEAD, 4 * BLOCK), F32)]
    out_specs = [pl.BlockSpec((rows, 2 * BLOCK), lambda g, *_: (0, g)), pl.BlockSpec((2, length, BLOCK), lambda g, *_: (0, 0, g))]
    out_shape = [
        jax.ShapeDtypeStruct((rows, width // parts), BF16),
        jax.ShapeDtypeStruct((2, length, width // 2 // parts), BF16),
    ]
    if masked:
        scratch = [pltpu.VMEM((3, BLOCK, 4 * BLOCK), F32)] + scratch
        scratch += [pltpu.VMEM((2, BLOCK, 4 * BLOCK), F32), pltpu.VMEM((8, 4 * BLOCK), F32)]
        out_specs = out_specs + [pl.BlockSpec((1, 4, SPAN), lambda g, *_: (g, 0, 0))]
        out_shape = out_shape + [jax.ShapeDtypeStruct((count, 4, SPAN), F32)]
    return pl.pallas_call(
        functools.partial(backward_kernel, masked),
        grid_spec=pltpu.PrefetchScalarGridSpec(
            num_scalar_prefetch=1,
            grid=(count,),
            in_specs=[cols, kspec, vspec, cols, outs, logs] + ([vecs, lims, lims] if masked else []),
            out_specs=out_specs,
            scratch_shapes=scratch,
        ),
        out_shape=out_shape,
        cost_estimate=pl.CostEstimate(
            flops=10 * rows * length * width // parts, bytes_accessed=8 * length * width // parts,
            transcendentals=rows * length * 16 // parts
        ),
        name="attend_self_back" if masked else "attend_cross_back",
    )(table, query, keys_values, keys_values, grad, outs_in, logs_in, *extra)


def offset_index(half):
    place = jnp.arange(SPAN, dtype=jnp.int32)
    behind = jnp.where(place >= 2 * BLOCK, place - SPAN, place)
    return behind, jnp.clip(half - behind, 0, 2 * half - 1)


D = 1024
HEADS = 16
KV_HEADS = 8
BUCKETS = 32
EPS = 1e-06
CTX = ("line", "core")


def tn(left, right):
    return lax.dot_general(left, right, (((0,), (0,)), ((), ())), preferred_element_type=F32)


def norm_rows(values, gain):
    scale = lax.rsqrt(jnp.mean(values * values, axis=-1, keepdims=True) + EPS)
    normed = values * scale
    return normed, scale, (normed * gain).astype(BF16)


def norm_back(grad_out, normed, scale, gain):
    grad_gain = jnp.sum(grad_out * normed, axis=0)
    inner = grad_out * gain
    grad_in = scale * (inner - normed * jnp.mean(inner * normed, axis=-1, keepdims=True))
    return grad_in, grad_gain


def gelu_tanh(value):
    return jax.nn.gelu(value, approximate=True)


def partners(size, bit):
    return [(index, index ^ bit) for index in range(size)]


def bits_of(size):
    return [1 << place for place in range(size.bit_length() - 1)]


def cross(value, axis, bit):
    return lax.ppermute(value, axis, partners(lax.axis_size(axis), bit))


def swap(value):
    return cross(value, "core", 1)


def add(left, right):
    return (left.astype(F32) + right.astype(F32)).astype(BF16)


def place_kernel(spots, rows, me_ref, *refs):
    pieces, whole_ref, sems = refs[: len(spots)], refs[len(spots)], refs[len(spots) + 1]
    copies = []
    for index, (mask, offset) in enumerate(spots):
        count = pieces[index].shape[0]
        start = pl.multiple_of((me_ref[0] ^ mask) * rows + offset, count)
        copies.append(pltpu.make_async_copy(pieces[index], whole_ref.at[pl.ds(start, count), :], sems.at[index]))
    for copy in copies:
        copy.start()
    for copy in copies:
        copy.wait()


def place(me, pieces, spots, size, rows):
    anywhere = pl.BlockSpec(memory_space=pl.ANY)
    return pl.pallas_call(
        functools.partial(place_kernel, spots, rows),
        in_specs=[pl.BlockSpec(memory_space=pltpu.SMEM)] + [pl.BlockSpec(memory_space=pltpu.VMEM)] * len(pieces),
        out_specs=anywhere,
        out_shape=jax.ShapeDtypeStruct((size * rows, pieces[0].shape[1]), BF16),
        scratch_shapes=[pltpu.SemaphoreType.DMA((len(pieces),))],
        name="place",
    )(me.reshape(1), *pieces)


class Lane:
    def __init__(self, steps):
        self.steps = steps
        self.result = None
        self.pending = next(steps)

    def push(self, arrived):
        try:
            self.pending = self.steps.send(arrived)
        except StopIteration as end:
            self.pending, self.result = None, end.value

    def take(self):
        while self.pending is not None:
            tick([self], ())
        return self.result

    def take(self):
        while self.pending is not None:
            tick([self], ())
        return self.result


def tick(lanes, live):
    active = [lane for lane in lanes if lane.pending is not None]
    live, arrived = lax.optimization_barrier((live, [lane.pending for lane in active]))
    for lane, value in zip(active, arrived):
        lane.push(value)
    return live


def swap_steps(*values):
    got = yield [swap(value) for value in values]
    return got


def sum_steps(value):
    for axis in ("core", "fsdp", "line"):
        for bit in bits_of(lax.axis_size(axis)):
            (got,) = yield [cross(value, axis, bit)]
            value = value + got
    return value


def count_steps(value):
    (got,) = yield [swap(value)]
    value = value + got
    got = yield [cross(value, "line", mask) for mask in range(1, lax.axis_size("line"))]
    return value + sum(got)


def small_steps(value):
    size = lax.axis_size("fsdp")
    me = lax.axis_index("fsdp")
    have = [(0, value)]
    for bit in bits_of(size):
        got = yield [cross(piece, "fsdp", bit) for _, piece in have]
        have = have + [(mask ^ bit, piece) for (mask, _), piece in zip(have, got)]
    whole = jnp.zeros((size, value.shape[0]), value.dtype)
    for mask, piece in have:
        whole = lax.dynamic_update_slice(whole, piece[None], (me ^ mask, 0))
    return whole


def columns_of(value, core):
    half = value.shape[1] // 2
    return lax.dynamic_slice_in_dim(value, core * half, half, axis=1)


def half_columns(parts):
    core = lax.axis_index("core")
    return jnp.concatenate([columns_of(part, core) for part in parts], axis=1)


def gather_steps(mine):
    size = lax.axis_size("fsdp")
    me = lax.axis_index("fsdp")
    rows, width = mine.shape
    bits = bits_of(size)
    half = rows // 2
    streams = [[(0, mine[stream * half : (stream + 1) * half])] for stream in range(2)]
    for step in range(len(bits)):
        chosen = [(bits if stream == 0 else bits[::-1])[step] for stream in range(2)]
        got = yield [[cross(piece, "fsdp", chosen[stream]) for _, piece in streams[stream]] for stream in range(2)]
        for stream in range(2):
            fresh = [(mask ^ chosen[stream], piece) for (mask, _), piece in zip(streams[stream], got[stream])]
            streams[stream] = streams[stream] + fresh
    spots = [(0, 0)] + [(mask, stream * half) for stream in range(2) for mask, _ in streams[stream][1:]]
    pieces = [mine] + [piece for stream in range(2) for _, piece in streams[stream][1:]]
    whole = place(me, pieces, spots, size, rows)
    whole, other = yield whole, swap(whole)
    return whole, other


def by_core(mine, other):
    first = lax.axis_index("core") == 0
    return jnp.where(first, mine, other), jnp.where(first, other, mine)


def grad_halves(*grads):
    core = lax.axis_index("core")
    mine = jnp.concatenate([columns_of(item, core) for item in grads], axis=1)
    return mine, jnp.concatenate([columns_of(item, 1 - core) for item in grads], axis=1)


def weight_grad(hidden, hidden_swapped, mine, arrived):
    both_hidden = jnp.concatenate([hidden, hidden_swapped], axis=0)
    both_grad = jnp.concatenate([mine, arrived], axis=0)
    return tn(both_hidden, both_grad).astype(BF16)


def split(value, axis, bit, place):
    mine = (lax.axis_index(axis) // bit) % 2
    keep = lax.dynamic_index_in_dim(value, mine, place, keepdims=False)
    return keep, lax.dynamic_index_in_dim(value, 1 - mine, place, keepdims=False)


def reduce_steps(partials, widths):
    size = lax.axis_size("fsdp")
    lines = lax.axis_size("line")
    rows = partials[0].shape[0] // size
    width = partials[0].shape[1]
    many = len(partials)
    bits = bits_of(size)
    folded = jnp.stack(partials).reshape([many] + [2] * len(bits) + [2, rows // 2, width])
    values = [lax.index_in_dim(folded, stream, 1 + len(bits), keepdims=False) for stream in range(2)]
    left = [bits[::-1], bits[::-1]]
    for step in range(len(bits)):
        chosen = [(bits if stream == 0 else bits[::-1])[step] for stream in range(2)]
        parts = [
            split(values[stream], "fsdp", chosen[stream], 1 + left[stream].index(chosen[stream]))
            for stream in range(2)
        ]
        got = yield [cross(parts[stream][1], "fsdp", chosen[stream]) for stream in range(2)]
        values = [add(parts[stream][0], got[stream]) for stream in range(2)]
        left = [[item for item in left[stream] if item != chosen[stream]] for stream in range(2)]
    shard = jnp.stack(values, axis=1)
    line_bits = bits_of(lines)
    value = shard.reshape([many] + [2] * len(line_bits) + [rows // lines, width])
    for bit in line_bits:
        keep, send = split(value, "line", bit, value.ndim - 3)
        (got,) = yield [cross(send, "line", bit)]
        value = add(keep, got)
    have = [(0, value)]
    for bit in line_bits[::-1]:
        got = yield [cross(piece, "line", bit) for _, piece in have]
        have = have + [(mask ^ bit, piece) for (mask, _), piece in zip(have, got)]
    have = [piece for _, piece in sorted(have, key=lambda item: item[0])]
    mine = jnp.stack(have)
    (other,) = yield [swap(mine)]
    me = lax.axis_index("line")
    outs = []
    for index in range(many):
        start = 0
        for wide in widths[index]:
            part = slice(start, start + wide // 2)
            both = jnp.concatenate(by_core(mine[:, index, :, part], other[:, index, :, part]), axis=2)
            ordered = [lax.dynamic_index_in_dim(both, me ^ entry, 0, keepdims=False) for entry in range(lines)]
            outs.append(jnp.concatenate(ordered, axis=0).astype(F32))
            start = start + wide // 2
    return outs


def gather_context_steps(value):
    have = [(0, value)]
    for bit in bits_of(lax.axis_size("line"))[::-1]:
        got = yield [cross(piece, "line", bit) for _, piece in have]
        have = have + [(mask ^ bit, piece) for (mask, _), piece in zip(have, got)]
    mine = jnp.concatenate([piece for _, piece in sorted(have, key=lambda item: item[0])], axis=0)
    (other,) = yield [swap(mine)]
    return jnp.concatenate([mine, other], axis=0)


def reduce_context_steps(value):
    lines = lax.axis_size("line")
    two, total, width = value.shape
    value = value.reshape(two, 2, lines, total // (2 * lines), width)
    (got,) = yield [swap(value[:, 1])]
    value = add(value[:, 0], got)
    for bit in bits_of(lines):
        value = value.reshape(two, value.shape[1] // 2, 2, value.shape[2], width)
        (got,) = yield [cross(value[:, :, 1], "line", bit)]
        value = add(value[:, :, 0], got)
    return value[:, 0]


def body(
    inputs, encoder, teacher, valid_mask, doc_ids, block_order, buckets,
    gain_self, w_query, w_key, w_value, w_out, gain_cross, c_query, c_key, c_value, c_out,
    gain_ffn, w_gate, w_up, w_down, bias_table,
):
    rows, width = inputs.shape[1:]
    lines = lax.axis_size("line")
    shards = lax.axis_size("fsdp")
    contexts = 2 * lines
    length = rows * contexts
    pair = rows // BLOCK
    token_total = length * shards
    key_width = KV_HEADS * HEAD
    context = lax.axis_index("line") * 2 + lax.axis_index("core")
    fsdp = lax.axis_index("fsdp")

    core = lax.axis_index("core")
    hidden_ff = w_gate.shape[1]
    joint = jnp.concatenate
    halves = D // 2
    share = gain_self.shape[0]

    def times(left, weight):
        return joint(by_core(nn(left, weight[0]), nn(left, weight[1])), axis=1)

    def times_back(grad, weight):
        return nt(columns_of(grad, core), weight[0]) + nt(columns_of(grad, 1 - core), weight[1])

    mask_rows = valid_mask.reshape(rows).astype(F32)
    assert rows <= 256
    local_count = jnp.broadcast_to(jnp.sum(mask_rows), (128,)).astype(BF16)
    lane_qkv = Lane(gather_steps(half_columns([joint([w_query, w_key, w_value], axis=1)])))
    lane_small = Lane(small_steps(joint([gain_self, gain_cross, gain_ffn, bias_table.reshape(-1), local_count])))
    mid_parts = tick([lane_qkv, lane_small], (w_out, c_query, c_key, c_value, c_out))

    mid_shard = half_columns([mid_parts[0], mid_parts[1], joint(mid_parts[2:4], axis=1), mid_parts[4]])
    mid_shard = tick([lane_qkv, lane_small], mid_shard)

    small = lane_small.take()
    gain_one, gain_two, gain_three = [
        small[:, index * share : (index + 1) * share].reshape(D).astype(F32) for index in range(3)
    ]
    table_whole = small[:, 3 * share : -128].reshape(BUCKETS, HEADS)
    lane_count = Lane(count_steps(jnp.broadcast_to(jnp.sum(small[:, -128:].astype(F32), axis=0), (8, 128))))
    flat_in = inputs.reshape(rows, width).astype(F32)
    normed_one, scale_one, hidden_one = norm_rows(flat_in, gain_one)
    hidden_one = tick([lane_qkv, lane_count], hidden_one)

    qkv_mine, qkv_other = lane_qkv.take()
    lane_mid = Lane(gather_steps(mid_shard))
    query, pairs = by_core(nn(hidden_one, qkv_mine).astype(BF16), nn(hidden_one, qkv_other).astype(BF16))
    query, pairs, late = tick(
        [lane_mid, lane_count], (query, pairs, (w_gate, w_up, w_down, doc_ids, block_order, buckets, table_whole))
    )
    gate_part, up_part, down_part, doc_ids, block_order, buckets, table_whole = late

    lane_keys = Lane(gather_context_steps(pairs))
    gu_shard = half_columns([joint([gate_part, up_part], axis=1)])
    wd_shard = half_columns([down_part])

    query_blocks = lax.dynamic_slice_in_dim(block_order, context * pair, pair)
    slots = jnp.arange(contexts * pair, dtype=jnp.int32)
    owner = slots // pair
    near = ((owner % 2) ^ core) * lines + ((owner // 2) ^ lax.axis_index("line"))
    slots_near = near * pair + slots % pair
    inverse = jnp.sum(jnp.where(block_order[None, :] == slots[:, None], slots_near[None, :], 0), axis=1)
    docs = doc_ids.reshape(length)
    query_docs = jnp.stack(
        [lax.dynamic_slice_in_dim(docs, query_blocks[index] * BLOCK, BLOCK) for index in range(pair)]
    )
    low = jnp.sum((docs[None, None, :] < query_docs[:, :, None]).astype(jnp.int32), axis=-1)
    high = jnp.sum((docs[None, None, :] <= query_docs[:, :, None]).astype(jnp.int32), axis=-1) - 1
    place_table = jnp.concatenate([query_blocks, low[:, 0] // BLOCK, inverse]).astype(jnp.int32)
    behind, index_of = offset_index(length)
    bucket_match = (jnp.take(buckets, index_of)[None, :] == jnp.arange(BUCKETS, dtype=jnp.int32)[:, None])

    vectors = tn(table_whole, bucket_match.astype(BF16)).reshape(HEADS // 4, 4, SPAN)
    gu_shard, wd_shard, low, high, place_table, bucket_match, vectors = tick(
        [lane_keys, lane_mid], (gu_shard, wd_shard, low, high, place_table, bucket_match, vectors)
    )
    extra = (vectors, low, high)

    lane_gu = Lane(gather_steps(gu_shard))
    lane_hidden_one = Lane(swap_steps(hidden_one))
    tick([lane_keys, lane_mid, lane_hidden_one], ())
    mid_mine, mid_other = lane_mid.take()
    wo, wcq, wckv, wco = [
        (mid_mine[:, index * halves : (index + 1) * halves], mid_other[:, index * halves : (index + 1) * halves])
        for index in range(4)
    ]
    encoder_rows = encoder.reshape(encoder.shape[1], width)
    encoder_pairs = times(encoder_rows, wckv).astype(BF16)
    encoder_pairs = tick([lane_keys, lane_gu], encoder_pairs)
    pairs_whole = lane_keys.take()

    lane_encoder = Lane(gather_context_steps(encoder_pairs))
    lane_encoder_rows = Lane(swap_steps(encoder_rows))
    attention, outs_one, logs_one = attend(query, pairs_whole, place_table, extra, True)
    attention, outs_one, logs_one, wd_shard = tick(
        [lane_encoder, lane_encoder_rows], (attention, outs_one, logs_one, wd_shard)
    )

    lane_attention = Lane(swap_steps(attention))
    lane_wd = Lane(gather_steps(wd_shard))
    mid_one = flat_in + times(attention, wo)
    normed_two, scale_two, hidden_two = norm_rows(mid_one, gain_two)
    cross_q = times(hidden_two, wcq).astype(BF16)
    mid_one, normed_two, hidden_two, cross_q, scale_two = tick(
        [lane_encoder, lane_attention, lane_gu], (mid_one, normed_two, hidden_two, cross_q, scale_two)
    )
    tick([lane_encoder, lane_wd], ())
    encoder_whole = lane_encoder.take()

    lane_hidden_two = Lane(swap_steps(hidden_two))
    crossed, outs_two, logs_two = attend(cross_q, encoder_whole, place_table, (), False)
    crossed, outs_two, logs_two = tick([lane_gu, lane_wd, lane_hidden_two], (crossed, outs_two, logs_two))

    lane_crossed = Lane(swap_steps(crossed))
    mid_two = mid_one + times(crossed, wco)
    normed_three, scale_three, hidden_three = norm_rows(mid_two, gain_three)
    mid_two, normed_three, hidden_three, scale_three = tick(
        [lane_wd, lane_crossed], (mid_two, normed_three, hidden_three, scale_three)
    )

    gu_mine, gu_other = lane_gu.take()
    lane_hidden_three = Lane(swap_steps(hidden_three))
    gate, up = by_core(nn(hidden_three, gu_mine), nn(hidden_three, gu_other))
    active, gelu_pull = jax.vjp(gelu_tanh, gate)
    mixed = (active * up).astype(BF16)
    mixed, gate, up, active = tick([lane_hidden_three], (mixed, gate, up, active))
    lane_mixed = Lane(swap_steps(mixed))

    wd_mine, wd_other = lane_wd.take()
    count = jnp.maximum(lane_count.take()[0, 0], 1.0)
    result = mid_two + times(mixed, (wd_mine, wd_other))
    layer_out = result.astype(BF16)
    diff = result - teacher.reshape(rows, width).astype(F32)
    squared_local = jnp.sum(mask_rows[:, None] * diff * diff)
    grad_result = token_total / count * mask_rows[:, None] * diff

    e_three = grad_result.astype(BF16)
    down_mine, down_away = grad_halves(e_three)
    grad_result, e_three, down_mine, down_away, squared_local, layer_out = tick(
        [lane_mixed], (grad_result, e_three, down_mine, down_away, squared_local, layer_out)
    )
    lane_down = Lane(swap_steps(down_away))
    grad_mixed = times_back(e_three, (wd_mine, wd_other))
    (gelu_slope,) = gelu_pull(grad_mixed * up)
    grad_gate = gelu_slope.astype(BF16)
    grad_up = (grad_mixed * active).astype(BF16)
    wide_mine, wide_away = grad_halves(grad_gate, grad_up)
    grad_gate, grad_up, wide_mine, wide_away = tick([lane_down], (grad_gate, grad_up, wide_mine, wide_away))

    lane_wide = Lane(swap_steps(wide_away))
    partial_down = weight_grad(mixed, lane_mixed.take()[0], down_mine, lane_down.take()[0])
    partial_down = tick([lane_wide], partial_down)

    lane_down = Lane(reduce_steps([partial_down], [(D,)]))
    partial_wide = weight_grad(hidden_three, lane_hidden_three.take()[0], wide_mine, lane_wide.take()[0])
    grad_hidden_three = times_back(joint([grad_gate, grad_up], axis=1), (gu_mine, gu_other))
    partial_wide, grad_hidden_three = tick([lane_down], (partial_wide, grad_hidden_three))

    lane_wide = Lane(reduce_steps([partial_wide], [(hidden_ff, hidden_ff)]))
    grad_norm_three, grad_gain_three = norm_back(grad_hidden_three, normed_three, scale_three, gain_three)
    grad_mid_two = grad_result + grad_norm_three

    e_two = grad_mid_two.astype(BF16)
    grad_cross = times_back(e_two, wco).astype(BF16)
    grad_cross_q, encoder_grad = attend_back(
        cross_q, encoder_whole, grad_cross, outs_two, logs_two, place_table, (), False
    )
    out_mine, out_away = grad_halves(e_two, grad_cross_q)
    grad_mid_two, grad_cross_q, encoder_grad, out_mine, out_away = tick(
        [lane_down, lane_wide], (grad_mid_two, grad_cross_q, encoder_grad, out_mine, out_away)
    )

    lane_encoder = Lane(reduce_context_steps(encoder_grad))
    lane_out = Lane(swap_steps(out_away))
    grad_norm_two, grad_gain_two = norm_back(times_back(grad_cross_q, wcq), normed_two, scale_two, gain_two)
    grad_mid_one = grad_mid_two + grad_norm_two

    e_one = grad_mid_one.astype(BF16)
    one_mine, one_away = grad_halves(e_one)
    grad_attention = times_back(e_one, wo).astype(BF16)
    grad_mid_one, one_mine, one_away, grad_attention = tick(
        [lane_down, lane_wide, lane_encoder, lane_out], (grad_mid_one, one_mine, one_away, grad_attention)
    )
    lane_one = Lane(swap_steps(one_away))

    def attend_part(part):
        return attend_back(
            query, pairs_whole, grad_attention, outs_one, logs_one, place_table, extra, True, part, 2
        )

    query_first, pairs_first, vectors_first = attend_part(0)
    query_first, pairs_first, vectors_first, grad_attention = tick(
        [lane_down, lane_wide, lane_encoder, lane_one], (query_first, pairs_first, vectors_first, grad_attention)
    )
    lane_first = Lane(reduce_context_steps(pairs_first))
    query_second, pairs_second, vectors_second = attend_part(1)
    grad_query = joint([query_first, query_second], axis=1)
    grad_vectors = joint([vectors_first, vectors_second], axis=0)
    query_mine, query_away = grad_halves(grad_query)
    pairs_second, grad_query, grad_vectors, query_mine, query_away = tick(
        [lane_down, lane_wide, lane_encoder, lane_first],
        (pairs_second, grad_query, grad_vectors, query_mine, query_away),
    )

    lane_second = Lane(reduce_context_steps(pairs_second))
    lane_query = Lane(swap_steps(query_away))
    arrived = lane_out.take()[0]
    partial_out = weight_grad(crossed, lane_crossed.take()[0], out_mine[:, :halves], arrived[:, :halves])
    partial_cross = weight_grad(hidden_two, lane_hidden_two.take()[0], out_mine[:, halves:], arrived[:, halves:])
    partial_one = weight_grad(attention, lane_attention.take()[0], one_mine, lane_one.take()[0])
    encoder_got = lane_encoder.take()
    encoder_mine = joint([encoder_got[0], encoder_got[1]], axis=1)
    keys_mine, keys_away = grad_halves(encoder_mine[:, :key_width], encoder_mine[:, key_width:])
    partial_out, partial_cross, partial_one, encoder_mine, keys_mine, keys_away = tick(
        [lane_first, lane_second, lane_down, lane_wide, lane_query],
        (partial_out, partial_cross, partial_one, encoder_mine, keys_mine, keys_away),
    )

    lane_keys = Lane(swap_steps(keys_away))
    partial_query = weight_grad(hidden_one, lane_hidden_one.take()[0], query_mine, lane_query.take()[0])
    lane_mid = Lane(reduce_steps([partial_out, partial_cross, partial_one, partial_query], [(D,)] * 4))
    grad_encoder = times_back(encoder_mine, wckv)
    grad_encoder = tick([lane_first, lane_second, lane_down, lane_keys], grad_encoder)

    partial_keys = weight_grad(encoder_rows, lane_encoder_rows.take()[0], keys_mine, lane_keys.take()[0])
    partial_keys = tick([lane_second, lane_mid, lane_wide], partial_keys)
    pairs_first, pairs_second = lane_first.take(), lane_second.take()
    mine = [joint([pairs_first[index], pairs_second[index]], axis=1) for index in range(2)]
    last_mine, last_away = grad_halves(mine[0], mine[1])
    mine, last_mine, last_away = tick([], (mine, last_mine, last_away))

    lane_last = Lane(swap_steps(last_away))
    tick([lane_last], ())
    partial_last = weight_grad(hidden_one, lane_hidden_one.take()[0], last_mine, lane_last.take()[0])
    partial_last = tick([lane_mid, lane_wide], partial_last)

    lane_last = Lane(reduce_steps([partial_last, partial_keys], [(key_width, key_width)] * 2))
    grad_packed = joint([grad_query, mine[0], mine[1]], axis=1)
    grad_norm_one, grad_gain_one = norm_back(
        times_back(grad_packed, (qkv_mine, qkv_other)), normed_one, scale_one, gain_one
    )
    grad_inputs = grad_mid_one + grad_norm_one

    grad_table = lax.dot_general(
        bucket_match.astype(F32) * ((behind >= 1 - BLOCK) & (behind < 2 * BLOCK)).astype(F32)[None, :],
        grad_vectors.reshape(HEADS, SPAN),
        (((1,), (1,)), ((), ())),
        precision=lax.Precision.HIGHEST,
        preferred_element_type=F32,
    )
    sums = jnp.concatenate(
        [
            grad_gain_one,
            grad_gain_two,
            grad_gain_three,
            grad_table.reshape(-1),
            jnp.broadcast_to(squared_local, (512,)),
        ]
    )
    sums, grad_inputs = tick([lane_last, lane_wide, lane_mid, lane_down], (sums.reshape(-1, 128), grad_inputs))
    lane_sums = Lane(sum_steps(sums))
    lanes = [lane_last, lane_wide, lane_mid, lane_down, lane_sums]
    while any(lane.pending is not None for lane in lanes):
        tick(lanes, ())
    sums = lane_sums.take().reshape(-1)
    (grad_down,) = lane_down.take()
    grad_gate_weight, grad_up_weight = lane_wide.take()
    grad_cross_out, grad_cross_query, grad_out_weight, grad_query_weight = lane_mid.take()
    grad_key_weight, grad_value_weight, grad_cross_key, grad_cross_value = lane_last.take()
    loss = sums[3 * D + 512] / (D * count)

    def shard_of(offset, amount):
        return lax.dynamic_slice_in_dim(sums, offset + fsdp * (amount // shards), amount // shards)

    return (
        layer_out.reshape(1, rows, width),
        loss,
        grad_inputs.reshape(1, rows, width),
        grad_encoder.reshape(1, encoder.shape[1], width),
        shard_of(0, D),
        grad_query_weight,
        grad_key_weight,
        grad_value_weight,
        grad_out_weight,
        shard_of(D, D),
        grad_cross_query,
        grad_cross_key,
        grad_cross_value,
        grad_cross_out,
        shard_of(2 * D, D),
        grad_gate_weight,
        grad_up_weight,
        grad_down,
        shard_of(3 * D, 512).reshape(BUCKETS // shards, HEADS),
    )


def solution(mesh):
    shape = mesh.devices.shape
    fine = Mesh(mesh.devices.reshape(shape[0] // 2, 2, shape[1]), ("line", "core", "fsdp"))
    tokens = P("fsdp", CTX, None)
    matrix = P("fsdp", None)
    vector = P("fsdp")
    weights = (vector, matrix, matrix, matrix, matrix, vector, matrix, matrix, matrix, matrix, vector)
    weights = weights + (matrix, matrix, matrix, matrix)
    in_specs = (tokens, tokens, tokens, P("fsdp", CTX), matrix, P(), P()) + weights
    out_specs = (tokens, P(), tokens, tokens) + weights
    return jax.shard_map(body, mesh=fine, in_specs=in_specs, out_specs=out_specs, check_vma=False)
```

```python
import functools
import jax
import jax.numpy as jnp
from jax import lax
from jax.experimental import pallas as pl
from jax.experimental.pallas import tpu as pltpu
from jax.sharding import Mesh
from jax.sharding import PartitionSpec as P

HEAD = 64
BLOCK = 128
NEGATIVE = -1e30
SPAN = 512
F32 = jnp.float32
BF16 = jnp.bfloat16


def nt(left, right):
    return lax.dot_general(left, right, (((1,), (1,)), ((), ())), preferred_element_type=F32)


def nn(left, right):
    return jnp.dot(left, right, preferred_element_type=F32)


def pad_heads(block):
    wide = block.astype(F32)
    lane = lax.broadcasted_iota(jnp.int32, (BLOCK, BLOCK), 1)
    parts = []
    for group in range(2):
        slab = wide[:, group * BLOCK : (group + 1) * BLOCK]
        turned = pltpu.roll(slab, HEAD, 1)
        keep = (lane < HEAD) if group == 0 else (lane >= HEAD)
        for part in range(2):
            source = slab if part == group else turned
            parts.append(jnp.where(keep, source, 0.0))
    return jnp.concatenate(parts, axis=0).astype(BF16)


def unpad_heads(turned):
    parts = [turned[:, index * BLOCK : (index + 1) * BLOCK].T for index in range(4)]
    return jnp.concatenate(parts, axis=1)


def fill_bias(vectors_ref, bias_ref):
    for head in range(4):
        row = jnp.broadcast_to(vectors_ref[0, head : head + 1, :], (BLOCK, SPAN))
        turned = pltpu.roll(row, 0, 1, stride=1, stride_axis=0)
        lanes = slice(head * BLOCK, (head + 1) * BLOCK)
        bias_ref[0, :, lanes] = turned[:, :BLOCK]
        bias_ref[1, :, lanes] = turned[:, BLOCK : 2 * BLOCK]
        bias_ref[2, :, lanes] = jnp.broadcast_to(row[:, BLOCK : BLOCK + 1], (BLOCK, BLOCK))


def four(tile):
    return jnp.concatenate([tile] * 4, axis=1)


def forward_kernel(masked, table, *refs):
    if masked:
        q_ref, k_ref, v_ref, vec_ref, low_ref, high_ref, a_ref, o_ref, l_ref, bias_ref, acc_ref = refs
        fill_bias(vec_ref, bias_ref)
    else:
        q_ref, k_ref, v_ref, a_ref, o_ref, l_ref, acc_ref = refs
    pairs = q_ref.shape[0] // BLOCK
    steps = k_ref.shape[0] // BLOCK
    row = lax.broadcasted_iota(jnp.int32, (BLOCK, BLOCK), 0)
    for index in range(pairs):
        rows = slice(index * BLOCK, (index + 1) * BLOCK)
        query = pad_heads(q_ref[rows, :])
        if masked:
            mine = table[index]
            first = table[pairs + index]
            low = low_ref[index : index + 1, :]
            high = high_ref[index : index + 1, :]

        def scores(step, near):
            if not masked:
                place = pl.multiple_of(step * BLOCK, BLOCK)
                return place, nt(k_ref[pl.ds(place, BLOCK), :], query)
            block = mine - step
            place = pl.multiple_of(table[2 * pairs + block] * BLOCK, BLOCK)
            raw = nt(k_ref[pl.ds(place, BLOCK), :], query)
            position = row + block * BLOCK
            allowed = position >= low
            if near:
                allowed = allowed & (position <= high)
                raw = raw + bias_ref[0]
            else:
                raw = raw + bias_ref[jnp.minimum(step, 2)]
            return place, jnp.where(four(allowed), raw, NEGATIVE)

        def gather(place, weight):
            turned = v_ref[pl.ds(place, BLOCK), :].astype(F32).T.astype(BF16)
            low_half = nn(turned[:HEAD], weight[:, : 2 * BLOCK])
            high_half = nn(turned[HEAD:], weight[:, 2 * BLOCK :])
            return jnp.concatenate([low_half, high_half], axis=1)

        place, raw = scores(0, True)
        top = jnp.max(raw, axis=0, keepdims=True)
        weight = jnp.exp(raw - top)
        total = jnp.sum(weight, axis=0, keepdims=True)
        acc_ref[...] = gather(place, weight.astype(BF16))

        def advance(step, carry):
            top, total = carry
            place, raw = scores(step, False)
            new_top = jnp.maximum(top, jnp.max(raw, axis=0, keepdims=True))
            factor = jnp.exp(top - new_top)
            weight = jnp.exp(raw - new_top)
            total = total * factor + jnp.sum(weight, axis=0, keepdims=True)
            acc_ref[...] = acc_ref[...] * factor + gather(place, weight.astype(BF16))
            return new_top, total

        count = mine - first + 1 if masked else steps
        top, total = lax.fori_loop(1, count, advance, (top, total))
        out = acc_ref[...] / total
        o_ref[0, index] = out
        l_ref[0, index] = jnp.broadcast_to(top + jnp.log(total), (8, 4 * BLOCK))
        a_ref[rows, :] = unpad_heads(out).astype(BF16)


def backward_kernel(masked, table, *refs):
    if masked:
        (q_ref, k_ref, v_ref, g_ref, o_ref, l_ref, vec_ref, low_ref, high_ref,
         dq_ref, dkv_ref, dvec_ref, bias_ref, dk_acc, dv_acc, dq_acc, near_ref, far_ref) = refs
        fill_bias(vec_ref, bias_ref)
        near_ref[...] = jnp.zeros_like(near_ref)
        far_ref[...] = jnp.zeros_like(far_ref)
    else:
        (q_ref, k_ref, v_ref, g_ref, o_ref, l_ref, dq_ref, dkv_ref, dk_acc, dv_acc, dq_acc) = refs
    pairs = q_ref.shape[0] // BLOCK
    steps = k_ref.shape[0] // BLOCK
    dk_acc[...] = jnp.zeros_like(dk_acc)
    dv_acc[...] = jnp.zeros_like(dv_acc)
    row = lax.broadcasted_iota(jnp.int32, (BLOCK, BLOCK), 0)
    for index in range(pairs):
        rows = slice(index * BLOCK, (index + 1) * BLOCK)
        query = pad_heads(q_ref[rows, :])
        grad = pad_heads(g_ref[rows, :])
        log_total = l_ref[0, index, :1, :]
        raw_grad = g_ref[rows, :].astype(F32)
        turned_grad = jnp.concatenate(
            [raw_grad[:, head * HEAD : (head + 1) * HEAD].T for head in range(4)], axis=1
        )
        delta = jnp.sum(turned_grad * o_ref[0, index], axis=0, keepdims=True)
        if masked:
            mine = table[index]
            first = table[pairs + index]
            low = low_ref[index : index + 1, :]
            high = high_ref[index : index + 1, :]

        def tile(step, near, start):
            if masked:
                block = mine - step
                place = pl.multiple_of(table[2 * pairs + block] * BLOCK, BLOCK)
            else:
                place = pl.multiple_of(step * BLOCK, BLOCK)
            keys = k_ref[pl.ds(place, BLOCK), :]
            raw = nt(keys, query)
            if masked:
                position = row + block * BLOCK
                allowed = position >= low
                if near:
                    allowed = allowed & (position <= high)
                    raw = raw + bias_ref[0]
                else:
                    raw = raw + bias_ref[jnp.minimum(step, 2)]
                raw = jnp.where(four(allowed), raw, NEGATIVE)
            prob = jnp.exp(raw - log_total)
            grad_prob = nt(v_ref[pl.ds(place, BLOCK), :], grad)
            grad_score = (prob * (grad_prob - delta)).astype(BF16)
            dv_acc[pl.ds(place, BLOCK), :] += nn(prob.astype(BF16), grad)
            dk_acc[pl.ds(place, BLOCK), :] += nn(grad_score, query)
            turned = keys.astype(F32).T.astype(BF16)
            part = jnp.concatenate(
                [nn(turned[:HEAD], grad_score[:, : 2 * BLOCK]), nn(turned[HEAD:], grad_score[:, 2 * BLOCK :])],
                axis=1,
            )
            if start:
                dq_acc[...] = part
            else:
                dq_acc[...] += part
            return grad_score

        grad_score = tile(0, True, True)
        if masked:
            near_ref[0] += grad_score.astype(F32)
            last = mine - first

            @pl.when(last >= 1)
            def _():
                near_ref[1] += tile(1, False, False).astype(F32)

            def advance(step, carry):
                wide = tile(step, False, False).astype(F32)
                far_ref[...] += jnp.sum(wide.reshape(BLOCK // 8, 8, 4 * BLOCK), axis=0)
                return carry

            lax.fori_loop(2, last + 1, advance, 0)
        else:

            def advance(step, carry):
                tile(step, False, False)
                return carry

            lax.fori_loop(1, steps, advance, 0)
        dq_ref[rows, :] = unpad_heads(dq_acc[...]).astype(BF16)
    dkv_ref[0] = dk_acc[...].astype(BF16)
    dkv_ref[1] = dv_acc[...].astype(BF16)
    if masked:
        rowid = lax.broadcasted_iota(jnp.int32, (BLOCK, SPAN), 0)
        lane = lax.broadcasted_iota(jnp.int32, (1, SPAN), 1)
        for head in range(4):
            lanes = slice(head * BLOCK, (head + 1) * BLOCK)
            wide = jnp.concatenate(
                [near_ref[0, :, lanes], near_ref[1, :, lanes], jnp.zeros((BLOCK, 2 * BLOCK), F32)], axis=1
            )
            bit = 1
            while bit < BLOCK:
                wide = jnp.where((rowid & bit) != 0, pltpu.roll(wide, SPAN - bit, 1), wide)
                bit = bit * 2
            sums = jnp.sum(wide, axis=0, keepdims=True)
            far = jnp.sum(far_ref[:, lanes])
            dvec_ref[0, head : head + 1, :] = sums + jnp.where(lane == BLOCK, far, 0.0)


def specs_of(rows, length, pairs, groups, first=0):
    cols = pl.BlockSpec((rows, 2 * BLOCK), lambda g, *_: (0, g + first))
    keys = pl.BlockSpec((length, BLOCK), lambda g, *_: (0, g + first))
    values = pl.BlockSpec((length, BLOCK), lambda g, *_: (0, groups + g + first))
    outs = pl.BlockSpec((1, pairs, HEAD, 4 * BLOCK), lambda g, *_: (g + first, 0, 0, 0))
    logs = pl.BlockSpec((1, pairs, 8, 4 * BLOCK), lambda g, *_: (g + first, 0, 0, 0))
    vecs = pl.BlockSpec((1, 4, SPAN), lambda g, *_: (g + first, 0, 0))
    lims = pl.BlockSpec((pairs, BLOCK), lambda g, *_: (0, 0))
    return cols, keys, values, outs, logs, vecs, lims


def attend(query, keys_values, table, extra, masked):
    rows, width = query.shape
    length = keys_values.shape[0]
    groups = width // (4 * HEAD)
    pairs = rows // BLOCK
    cols, kspec, vspec, outs, logs, vecs, lims = specs_of(rows, length, pairs, groups)
    scratch = [pltpu.VMEM((HEAD, 4 * BLOCK), F32)]
    if masked:
        scratch = [pltpu.VMEM((3, BLOCK, 4 * BLOCK), F32)] + scratch
    return pl.pallas_call(
        functools.partial(forward_kernel, masked),
        grid_spec=pltpu.PrefetchScalarGridSpec(
            num_scalar_prefetch=1,
            grid=(groups,),
            in_specs=[cols, kspec, vspec] + ([vecs, lims, lims] if masked else []),
            out_specs=[cols, outs, logs],
            scratch_shapes=scratch,
        ),
        out_shape=[
            jax.ShapeDtypeStruct((rows, width), BF16),
            jax.ShapeDtypeStruct((groups, pairs, HEAD, 4 * BLOCK), F32),
            jax.ShapeDtypeStruct((groups, pairs, 8, 4 * BLOCK), F32),
        ],
        cost_estimate=pl.CostEstimate(
            flops=4 * rows * length * width, bytes_accessed=4 * length * width, transcendentals=rows * length * 16
        ),
        name="attend_self" if masked else "attend_cross",
    )(table, query, keys_values, keys_values, *extra)


def attend_back(query, keys_values, grad, outs_in, logs_in, table, extra, masked, part=0, parts=1):
    rows, width = query.shape
    length = keys_values.shape[0]
    groups = width // (4 * HEAD)
    pairs = rows // BLOCK
    count = groups // parts
    cols, kspec, vspec, outs, logs, vecs, lims = specs_of(rows, length, pairs, groups, part * count)
    scratch = [pltpu.VMEM((length, BLOCK), F32), pltpu.VMEM((length, BLOCK), F32), pltpu.VMEM((HEAD, 4 * BLOCK), F32)]
    out_specs = [pl.BlockSpec((rows, 2 * BLOCK), lambda g, *_: (0, g)), pl.BlockSpec((2, length, BLOCK), lambda g, *_: (0, 0, g))]
    out_shape = [
        jax.ShapeDtypeStruct((rows, width // parts), BF16),
        jax.ShapeDtypeStruct((2, length, width // 2 // parts), BF16),
    ]
    if masked:
        scratch = [pltpu.VMEM((3, BLOCK, 4 * BLOCK), F32)] + scratch
        scratch += [pltpu.VMEM((2, BLOCK, 4 * BLOCK), F32), pltpu.VMEM((8, 4 * BLOCK), F32)]
        out_specs = out_specs + [pl.BlockSpec((1, 4, SPAN), lambda g, *_: (g, 0, 0))]
        out_shape = out_shape + [jax.ShapeDtypeStruct((count, 4, SPAN), F32)]
    return pl.pallas_call(
        functools.partial(backward_kernel, masked),
        grid_spec=pltpu.PrefetchScalarGridSpec(
            num_scalar_prefetch=1,
            grid=(count,),
            in_specs=[cols, kspec, vspec, cols, outs, logs] + ([vecs, lims, lims] if masked else []),
            out_specs=out_specs,
            scratch_shapes=scratch,
        ),
        out_shape=out_shape,
        cost_estimate=pl.CostEstimate(
            flops=10 * rows * length * width // parts, bytes_accessed=8 * length * width // parts,
            transcendentals=rows * length * 16 // parts
        ),
        name="attend_self_back" if masked else "attend_cross_back",
    )(table, query, keys_values, keys_values, grad, outs_in, logs_in, *extra)


def offset_index(half):
    place = jnp.arange(SPAN, dtype=jnp.int32)
    behind = jnp.where(place >= 2 * BLOCK, place - SPAN, place)
    return behind, jnp.clip(half - behind, 0, 2 * half - 1)


D = 1024
HEADS = 16
KV_HEADS = 8
BUCKETS = 32
EPS = 1e-06
CTX = ("line", "core")


def tn(left, right):
    return lax.dot_general(left, right, (((0,), (0,)), ((), ())), preferred_element_type=F32)


def norm_rows(values, gain):
    scale = lax.rsqrt(jnp.mean(values * values, axis=-1, keepdims=True) + EPS)
    normed = values * scale
    return normed, scale, (normed * gain).astype(BF16)


def norm_back(grad_out, normed, scale, gain):
    grad_gain = jnp.sum(grad_out * normed, axis=0)
    inner = grad_out * gain
    grad_in = scale * (inner - normed * jnp.mean(inner * normed, axis=-1, keepdims=True))
    return grad_in, grad_gain


def gelu_tanh(value):
    return jax.nn.gelu(value, approximate=True)


def partners(size, bit):
    return [(index, index ^ bit) for index in range(size)]


def bits_of(size):
    return [1 << place for place in range(size.bit_length() - 1)]


def cross(value, axis, bit):
    return lax.ppermute(value, axis, partners(lax.axis_size(axis), bit))


def swap(value):
    return cross(value, "core", 1)


def add(left, right):
    return (left.astype(F32) + right.astype(F32)).astype(BF16)


def place_kernel(spots, rows, me_ref, *refs):
    pieces, whole_ref, sems = refs[: len(spots)], refs[len(spots)], refs[len(spots) + 1]
    copies = []
    for index, (mask, offset) in enumerate(spots):
        count = pieces[index].shape[0]
        start = pl.multiple_of((me_ref[0] ^ mask) * rows + offset, count)
        copies.append(pltpu.make_async_copy(pieces[index], whole_ref.at[pl.ds(start, count), :], sems.at[index]))
    for copy in copies:
        copy.start()
    for copy in copies:
        copy.wait()


def place(me, pieces, spots, size, rows):
    anywhere = pl.BlockSpec(memory_space=pl.ANY)
    return pl.pallas_call(
        functools.partial(place_kernel, spots, rows),
        in_specs=[pl.BlockSpec(memory_space=pltpu.SMEM)] + [pl.BlockSpec(memory_space=pltpu.VMEM)] * len(pieces),
        out_specs=anywhere,
        out_shape=jax.ShapeDtypeStruct((size * rows, pieces[0].shape[1]), BF16),
        scratch_shapes=[pltpu.SemaphoreType.DMA((len(pieces),))],
        name="place",
    )(me.reshape(1), *pieces)


class Lane:
    def __init__(self, steps):
        self.steps = steps
        self.result = None
        self.pending = next(steps)

    def push(self, arrived):
        try:
            self.pending = self.steps.send(arrived)
        except StopIteration as end:
            self.pending, self.result = None, end.value

    def take(self):
        while self.pending is not None:
            tick([self], ())
        return self.result

    def take(self):
        while self.pending is not None:
            tick([self], ())
        return self.result


def tick(lanes, live):
    active = [lane for lane in lanes if lane.pending is not None]
    live, arrived = lax.optimization_barrier((live, [lane.pending for lane in active]))
    for lane, value in zip(active, arrived):
        lane.push(value)
    return live


def swap_steps(*values):
    got = yield [swap(value) for value in values]
    return got


def sum_steps(value):
    for axis in ("core", "fsdp", "line"):
        for bit in bits_of(lax.axis_size(axis)):
            (got,) = yield [cross(value, axis, bit)]
            value = value + got
    return value


def count_steps(value):
    (got,) = yield [swap(value)]
    value = value + got
    got = yield [cross(value, "line", mask) for mask in range(1, lax.axis_size("line"))]
    return value + sum(got)


def small_steps(value):
    size = lax.axis_size("fsdp")
    me = lax.axis_index("fsdp")
    have = [(0, value)]
    for bit in bits_of(size):
        got = yield [cross(piece, "fsdp", bit) for _, piece in have]
        have = have + [(mask ^ bit, piece) for (mask, _), piece in zip(have, got)]
    whole = jnp.zeros((size, value.shape[0]), value.dtype)
    for mask, piece in have:
        whole = lax.dynamic_update_slice(whole, piece[None], (me ^ mask, 0))
    return whole


def columns_of(value, core):
    half = value.shape[1] // 2
    return lax.dynamic_slice_in_dim(value, core * half, half, axis=1)


def half_columns(parts):
    core = lax.axis_index("core")
    return jnp.concatenate([columns_of(part, core) for part in parts], axis=1)


def gather_steps(mine, fine=False):
    size = lax.axis_size("fsdp")
    me = lax.axis_index("fsdp")
    rows, width = mine.shape
    bits = bits_of(size)
    half = rows // 2
    streams = [[(0, mine[stream * half : (stream + 1) * half])] for stream in range(2)]
    for step in range(len(bits)):
        chosen = [(bits if stream == 0 else bits[::-1])[step] for stream in range(2)]
        have = len(streams[0])
        got = [[], []]
        for spot in range(have) if fine else [slice(0, have)]:
            spot = spot if isinstance(spot, slice) else slice(spot, spot + 1)
            arrived = yield [
                [cross(piece, "fsdp", chosen[stream]) for _, piece in streams[stream][spot]] for stream in range(2)
            ]
            got = [got[stream] + arrived[stream] for stream in range(2)]
        for stream in range(2):
            fresh = [(mask ^ chosen[stream], piece) for (mask, _), piece in zip(streams[stream], got[stream])]
            streams[stream] = streams[stream] + fresh
    spots = [(0, 0)] + [(mask, stream * half) for stream in range(2) for mask, _ in streams[stream][1:]]
    pieces = [mine] + [piece for stream in range(2) for _, piece in streams[stream][1:]]
    whole = place(me, pieces, spots, size, rows)
    whole, other = yield whole, swap(whole)
    return whole, other


def by_core(mine, other):
    first = lax.axis_index("core") == 0
    return jnp.where(first, mine, other), jnp.where(first, other, mine)


def grad_halves(*grads):
    core = lax.axis_index("core")
    mine = jnp.concatenate([columns_of(item, core) for item in grads], axis=1)
    return mine, jnp.concatenate([columns_of(item, 1 - core) for item in grads], axis=1)


def weight_grad(hidden, hidden_swapped, mine, arrived):
    both_hidden = jnp.concatenate([hidden, hidden_swapped], axis=0)
    both_grad = jnp.concatenate([mine, arrived], axis=0)
    return tn(both_hidden, both_grad).astype(BF16)


def split(value, axis, bit, place):
    mine = (lax.axis_index(axis) // bit) % 2
    keep = lax.dynamic_index_in_dim(value, mine, place, keepdims=False)
    return keep, lax.dynamic_index_in_dim(value, 1 - mine, place, keepdims=False)


def reduce_steps(partials, widths):
    size = lax.axis_size("fsdp")
    lines = lax.axis_size("line")
    rows = partials[0].shape[0] // size
    width = partials[0].shape[1]
    many = len(partials)
    bits = bits_of(size)
    folded = jnp.stack(partials).reshape([many] + [2] * len(bits) + [2, rows // 2, width])
    values = [lax.index_in_dim(folded, stream, 1 + len(bits), keepdims=False) for stream in range(2)]
    left = [bits[::-1], bits[::-1]]
    for step in range(len(bits)):
        chosen = [(bits if stream == 0 else bits[::-1])[step] for stream in range(2)]
        parts = [
            split(values[stream], "fsdp", chosen[stream], 1 + left[stream].index(chosen[stream]))
            for stream in range(2)
        ]
        got = yield [cross(parts[stream][1], "fsdp", chosen[stream]) for stream in range(2)]
        values = [add(parts[stream][0], got[stream]) for stream in range(2)]
        left = [[item for item in left[stream] if item != chosen[stream]] for stream in range(2)]
    shard = jnp.stack(values, axis=1)
    line_bits = bits_of(lines)
    value = shard.reshape([many] + [2] * len(line_bits) + [rows // lines, width])
    for bit in line_bits:
        keep, send = split(value, "line", bit, value.ndim - 3)
        (got,) = yield [cross(send, "line", bit)]
        value = add(keep, got)
    mine = value[None]
    for bit in line_bits[::-1]:
        (got,) = yield [cross(mine, "line", bit)]
        mine = jnp.concatenate([mine, got], axis=0)
    (other,) = yield [swap(mine)]
    me = lax.axis_index("line")

    def spot(entry):
        mask = me ^ entry
        return sum(((mask // bit) % 2) * (lines // (2 * bit)) for bit in line_bits)

    outs = []
    for index in range(many):
        start = 0
        for wide in widths[index]:
            part = slice(start, start + wide // 2)
            both = jnp.concatenate(by_core(mine[:, index, :, part], other[:, index, :, part]), axis=2)
            ordered = [lax.dynamic_index_in_dim(both, spot(entry), 0, keepdims=False) for entry in range(lines)]
            outs.append(jnp.concatenate(ordered, axis=0).astype(F32))
            start = start + wide // 2
    return outs


def gather_context_steps(value):
    rows = value.shape[0]
    mine = value
    masks = [0]
    for bit in bits_of(lax.axis_size("line"))[::-1]:
        (got,) = yield [cross(mine, "line", bit)]
        mine = jnp.concatenate([mine, got], axis=0)
        masks = masks + [mask ^ bit for mask in masks]
    order = [masks.index(mask) for mask in range(len(masks))]
    mine = jnp.concatenate([mine[at * rows : (at + 1) * rows] for at in order], axis=0)
    (other,) = yield [swap(mine)]
    return jnp.concatenate([mine, other], axis=0)


def reduce_context_steps(value):
    lines = lax.axis_size("line")
    two, total, width = value.shape
    value = value.reshape(two, 2, lines, total // (2 * lines), width)
    (got,) = yield [swap(value[:, 1])]
    value = add(value[:, 0], got)
    for bit in bits_of(lines):
        value = value.reshape(two, value.shape[1] // 2, 2, value.shape[2], width)
        (got,) = yield [cross(value[:, :, 1], "line", bit)]
        value = add(value[:, :, 0], got)
    return value[:, 0]


def body(
    inputs, encoder, teacher, valid_mask, doc_ids, block_order, buckets,
    gain_self, w_query, w_key, w_value, w_out, gain_cross, c_query, c_key, c_value, c_out,
    gain_ffn, w_gate, w_up, w_down, bias_table,
):
    rows, width = inputs.shape[1:]
    lines = lax.axis_size("line")
    shards = lax.axis_size("fsdp")
    contexts = 2 * lines
    length = rows * contexts
    pair = rows // BLOCK
    token_total = length * shards
    key_width = KV_HEADS * HEAD
    context = lax.axis_index("line") * 2 + lax.axis_index("core")
    fsdp = lax.axis_index("fsdp")

    core = lax.axis_index("core")
    hidden_ff = w_gate.shape[1]
    joint = jnp.concatenate
    halves = D // 2
    share = gain_self.shape[0]

    def times(left, weight):
        return joint(by_core(nn(left, weight[0]), nn(left, weight[1])), axis=1)

    def times_back(grad, weight):
        return nt(columns_of(grad, core), weight[0]) + nt(columns_of(grad, 1 - core), weight[1])

    mask_rows = valid_mask.reshape(rows).astype(F32)
    assert rows <= 256
    local_count = jnp.broadcast_to(jnp.sum(mask_rows), (128,)).astype(BF16)
    lane_qkv = Lane(gather_steps(half_columns([joint([w_query, w_key, w_value], axis=1)])))
    lane_small = Lane(small_steps(joint([gain_self, gain_cross, gain_ffn, bias_table.reshape(-1), local_count])))
    mid_parts = tick([lane_qkv, lane_small], (w_out, c_query, c_key, c_value, c_out))

    mid_shard = half_columns([mid_parts[0], mid_parts[1], joint(mid_parts[2:4], axis=1), mid_parts[4]])
    mid_shard = tick([lane_qkv, lane_small], mid_shard)

    small = lane_small.take()
    gain_one, gain_two, gain_three = [
        small[:, index * share : (index + 1) * share].reshape(D).astype(F32) for index in range(3)
    ]
    table_whole = small[:, 3 * share : -128].reshape(BUCKETS, HEADS)
    lane_count = Lane(count_steps(jnp.broadcast_to(jnp.sum(small[:, -128:].astype(F32), axis=0), (8, 128))))
    flat_in = inputs.reshape(rows, width).astype(F32)
    normed_one, scale_one, hidden_one = norm_rows(flat_in, gain_one)
    hidden_one = tick([lane_qkv, lane_count], hidden_one)

    qkv_mine, qkv_other = lane_qkv.take()
    lane_mid = Lane(gather_steps(mid_shard))
    query, pairs = by_core(nn(hidden_one, qkv_mine).astype(BF16), nn(hidden_one, qkv_other).astype(BF16))
    query, pairs, late = tick(
        [lane_mid, lane_count], (query, pairs, (w_gate, w_up, w_down, doc_ids, block_order, buckets, table_whole))
    )
    gate_part, up_part, down_part, doc_ids, block_order, buckets, table_whole = late

    lane_keys = Lane(gather_context_steps(pairs))
    gu_shard = half_columns([joint([gate_part, up_part], axis=1)])
    wd_shard = half_columns([down_part])

    query_blocks = lax.dynamic_slice_in_dim(block_order, context * pair, pair)
    slots = jnp.arange(contexts * pair, dtype=jnp.int32)
    owner = slots // pair
    near = ((owner % 2) ^ core) * lines + ((owner // 2) ^ lax.axis_index("line"))
    slots_near = near * pair + slots % pair
    inverse = jnp.sum(jnp.where(block_order[None, :] == slots[:, None], slots_near[None, :], 0), axis=1)
    docs = doc_ids.reshape(length)
    query_docs = jnp.stack(
        [lax.dynamic_slice_in_dim(docs, query_blocks[index] * BLOCK, BLOCK) for index in range(pair)]
    )
    low = jnp.sum((docs[None, None, :] < query_docs[:, :, None]).astype(jnp.int32), axis=-1)
    high = jnp.sum((docs[None, None, :] <= query_docs[:, :, None]).astype(jnp.int32), axis=-1) - 1
    place_table = jnp.concatenate([query_blocks, low[:, 0] // BLOCK, inverse]).astype(jnp.int32)
    behind, index_of = offset_index(length)
    bucket_match = (jnp.take(buckets, index_of)[None, :] == jnp.arange(BUCKETS, dtype=jnp.int32)[:, None])

    vectors = tn(table_whole, bucket_match.astype(BF16)).reshape(HEADS // 4, 4, SPAN)
    gu_shard, wd_shard, low, high, place_table, bucket_match, vectors = tick(
        [lane_keys, lane_mid], (gu_shard, wd_shard, low, high, place_table, bucket_match, vectors)
    )
    extra = (vectors, low, high)

    lane_gu = Lane(gather_steps(gu_shard, True))
    tick([lane_keys, lane_mid, lane_gu], ())
    mid_mine, mid_other = lane_mid.take()
    wo, wcq, wckv, wco = [
        (mid_mine[:, index * halves : (index + 1) * halves], mid_other[:, index * halves : (index + 1) * halves])
        for index in range(4)
    ]
    encoder_rows = encoder.reshape(encoder.shape[1], width)
    encoder_pairs = times(encoder_rows, wckv).astype(BF16)
    encoder_pairs, wd_shard = tick([lane_keys], (encoder_pairs, wd_shard))
    pairs_whole = lane_keys.take()

    lane_encoder = Lane(gather_context_steps(encoder_pairs))
    lane_encoder_rows = Lane(swap_steps(encoder_rows))
    lane_wd = Lane(gather_steps(wd_shard))
    lane_hidden_one = Lane(swap_steps(hidden_one))
    attention, outs_one, logs_one = attend(query, pairs_whole, place_table, extra, True)
    attention, outs_one, logs_one = tick(
        [lane_encoder, lane_encoder_rows, lane_gu, lane_wd, lane_hidden_one], (attention, outs_one, logs_one)
    )

    lane_attention = Lane(swap_steps(attention))
    mid_one = flat_in + times(attention, wo)
    normed_two, scale_two, hidden_two = norm_rows(mid_one, gain_two)
    cross_q = times(hidden_two, wcq).astype(BF16)
    mid_one, normed_two, hidden_two, cross_q, scale_two = tick(
        [lane_encoder, lane_attention, lane_gu], (mid_one, normed_two, hidden_two, cross_q, scale_two)
    )
    tick([lane_encoder], ())
    encoder_whole = lane_encoder.take()

    lane_hidden_two = Lane(swap_steps(hidden_two))
    crossed, outs_two, logs_two = attend(cross_q, encoder_whole, place_table, (), False)
    crossed, outs_two, logs_two = tick([lane_gu, lane_wd, lane_hidden_two], (crossed, outs_two, logs_two))

    lane_crossed = Lane(swap_steps(crossed))
    mid_two = mid_one + times(crossed, wco)
    normed_three, scale_three, hidden_three = norm_rows(mid_two, gain_three)
    mid_two, normed_three, hidden_three, scale_three = tick(
        [lane_wd, lane_crossed], (mid_two, normed_three, hidden_three, scale_three)
    )

    gu_mine, gu_other = lane_gu.take()
    lane_hidden_three = Lane(swap_steps(hidden_three))
    gate, up = by_core(nn(hidden_three, gu_mine), nn(hidden_three, gu_other))
    active, gelu_pull = jax.vjp(gelu_tanh, gate)
    mixed = (active * up).astype(BF16)
    mixed, gate, up, active = tick([lane_hidden_three], (mixed, gate, up, active))
    lane_mixed = Lane(swap_steps(mixed))

    wd_mine, wd_other = lane_wd.take()
    count = jnp.maximum(lane_count.take()[0, 0], 1.0)
    result = mid_two + times(mixed, (wd_mine, wd_other))
    layer_out = result.astype(BF16)
    diff = result - teacher.reshape(rows, width).astype(F32)
    squared_local = jnp.sum(mask_rows[:, None] * diff * diff)
    grad_result = token_total / count * mask_rows[:, None] * diff

    e_three = grad_result.astype(BF16)
    down_mine, down_away = grad_halves(e_three)
    grad_result, e_three, down_mine, down_away, squared_local, layer_out = tick(
        [lane_mixed], (grad_result, e_three, down_mine, down_away, squared_local, layer_out)
    )
    lane_down = Lane(swap_steps(down_away))
    grad_mixed = times_back(e_three, (wd_mine, wd_other))
    (gelu_slope,) = gelu_pull(grad_mixed * up)
    grad_gate = gelu_slope.astype(BF16)
    grad_up = (grad_mixed * active).astype(BF16)
    wide_mine, wide_away = grad_halves(grad_gate, grad_up)
    grad_gate, grad_up, wide_mine, wide_away = tick([lane_down], (grad_gate, grad_up, wide_mine, wide_away))

    lane_wide = Lane(swap_steps(wide_away))
    partial_down = weight_grad(mixed, lane_mixed.take()[0], down_mine, lane_down.take()[0])
    partial_down = tick([lane_wide], partial_down)

    lane_down = Lane(reduce_steps([partial_down], [(D,)]))
    partial_wide = weight_grad(hidden_three, lane_hidden_three.take()[0], wide_mine, lane_wide.take()[0])
    grad_hidden_three = times_back(joint([grad_gate, grad_up], axis=1), (gu_mine, gu_other))
    partial_wide, grad_hidden_three = tick([lane_down], (partial_wide, grad_hidden_three))

    lane_wide = Lane(reduce_steps([partial_wide], [(hidden_ff, hidden_ff)]))
    grad_norm_three, grad_gain_three = norm_back(grad_hidden_three, normed_three, scale_three, gain_three)
    grad_mid_two = grad_result + grad_norm_three

    e_two = grad_mid_two.astype(BF16)
    grad_cross = times_back(e_two, wco).astype(BF16)
    grad_cross_q, encoder_grad = attend_back(
        cross_q, encoder_whole, grad_cross, outs_two, logs_two, place_table, (), False
    )
    out_mine, out_away = grad_halves(e_two, grad_cross_q)
    grad_mid_two, grad_cross_q, encoder_grad, out_mine, out_away = tick(
        [lane_down, lane_wide], (grad_mid_two, grad_cross_q, encoder_grad, out_mine, out_away)
    )

    lane_encoder = Lane(reduce_context_steps(encoder_grad))
    lane_out = Lane(swap_steps(out_away))
    grad_norm_two, grad_gain_two = norm_back(times_back(grad_cross_q, wcq), normed_two, scale_two, gain_two)
    grad_mid_one = grad_mid_two + grad_norm_two

    e_one = grad_mid_one.astype(BF16)
    one_mine, one_away = grad_halves(e_one)
    grad_attention = times_back(e_one, wo).astype(BF16)
    grad_mid_one, one_mine, one_away, grad_attention = tick(
        [lane_down, lane_wide, lane_encoder, lane_out], (grad_mid_one, one_mine, one_away, grad_attention)
    )
    lane_one = Lane(swap_steps(one_away))

    def attend_part(part):
        return attend_back(
            query, pairs_whole, grad_attention, outs_one, logs_one, place_table, extra, True, part, 2
        )

    query_first, pairs_first, vectors_first = attend_part(0)
    query_first, pairs_first, vectors_first, grad_attention = tick(
        [lane_down, lane_wide, lane_encoder, lane_one], (query_first, pairs_first, vectors_first, grad_attention)
    )
    lane_first = Lane(reduce_context_steps(pairs_first))
    query_second, pairs_second, vectors_second = attend_part(1)
    grad_query = joint([query_first, query_second], axis=1)
    grad_vectors = joint([vectors_first, vectors_second], axis=0)
    query_mine, query_away = grad_halves(grad_query)
    pairs_second, grad_query, grad_vectors, query_mine, query_away = tick(
        [lane_down, lane_wide, lane_encoder, lane_first],
        (pairs_second, grad_query, grad_vectors, query_mine, query_away),
    )

    lane_second = Lane(reduce_context_steps(pairs_second))
    lane_query = Lane(swap_steps(query_away))
    arrived = lane_out.take()[0]
    partial_out = weight_grad(crossed, lane_crossed.take()[0], out_mine[:, :halves], arrived[:, :halves])
    partial_cross = weight_grad(hidden_two, lane_hidden_two.take()[0], out_mine[:, halves:], arrived[:, halves:])
    partial_one = weight_grad(attention, lane_attention.take()[0], one_mine, lane_one.take()[0])
    encoder_got = lane_encoder.take()
    encoder_mine = joint([encoder_got[0], encoder_got[1]], axis=1)
    keys_mine, keys_away = grad_halves(encoder_mine[:, :key_width], encoder_mine[:, key_width:])
    partial_out, partial_cross, partial_one, encoder_mine, keys_mine, keys_away = tick(
        [lane_first, lane_second, lane_down, lane_wide, lane_query],
        (partial_out, partial_cross, partial_one, encoder_mine, keys_mine, keys_away),
    )

    lane_keys = Lane(swap_steps(keys_away))
    partial_query = weight_grad(hidden_one, lane_hidden_one.take()[0], query_mine, lane_query.take()[0])
    lane_mid = Lane(reduce_steps([partial_out, partial_cross, partial_one, partial_query], [(D,)] * 4))
    grad_encoder = times_back(encoder_mine, wckv)
    grad_encoder = tick([lane_first, lane_second, lane_down, lane_keys], grad_encoder)

    partial_keys = weight_grad(encoder_rows, lane_encoder_rows.take()[0], keys_mine, lane_keys.take()[0])
    partial_keys = tick([lane_second, lane_mid, lane_wide], partial_keys)
    pairs_first, pairs_second = lane_first.take(), lane_second.take()
    mine = [joint([pairs_first[index], pairs_second[index]], axis=1) for index in range(2)]
    last_mine, last_away = grad_halves(mine[0], mine[1])
    mine, last_mine, last_away = tick([], (mine, last_mine, last_away))

    lane_last = Lane(swap_steps(last_away))
    tick([lane_last], ())
    partial_last = weight_grad(hidden_one, lane_hidden_one.take()[0], last_mine, lane_last.take()[0])
    partial_last = tick([lane_mid, lane_wide], partial_last)

    lane_last = Lane(reduce_steps([partial_last, partial_keys], [(key_width, key_width)] * 2))
    grad_packed = joint([grad_query, mine[0], mine[1]], axis=1)
    grad_norm_one, grad_gain_one = norm_back(
        times_back(grad_packed, (qkv_mine, qkv_other)), normed_one, scale_one, gain_one
    )
    grad_inputs = grad_mid_one + grad_norm_one

    grad_table = lax.dot_general(
        bucket_match.astype(F32) * ((behind >= 1 - BLOCK) & (behind < 2 * BLOCK)).astype(F32)[None, :],
        grad_vectors.reshape(HEADS, SPAN),
        (((1,), (1,)), ((), ())),
        precision=lax.Precision.HIGHEST,
        preferred_element_type=F32,
    )
    sums = jnp.concatenate(
        [
            grad_gain_one,
            grad_gain_two,
            grad_gain_three,
            grad_table.reshape(-1),
            jnp.broadcast_to(squared_local, (512,)),
        ]
    )
    sums, grad_inputs = tick([lane_last, lane_wide, lane_mid, lane_down], (sums.reshape(-1, 128), grad_inputs))
    lane_sums = Lane(sum_steps(sums))
    lanes = [lane_last, lane_wide, lane_mid, lane_down, lane_sums]
    while any(lane.pending is not None for lane in lanes):
        tick(lanes, ())
    sums = lane_sums.take().reshape(-1)
    (grad_down,) = lane_down.take()
    grad_gate_weight, grad_up_weight = lane_wide.take()
    grad_cross_out, grad_cross_query, grad_out_weight, grad_query_weight = lane_mid.take()
    grad_key_weight, grad_value_weight, grad_cross_key, grad_cross_value = lane_last.take()
    loss = sums[3 * D + 512] / (D * count)

    def shard_of(offset, amount):
        return lax.dynamic_slice_in_dim(sums, offset + fsdp * (amount // shards), amount // shards)

    return (
        layer_out.reshape(1, rows, width),
        loss,
        grad_inputs.reshape(1, rows, width),
        grad_encoder.reshape(1, encoder.shape[1], width),
        shard_of(0, D),
        grad_query_weight,
        grad_key_weight,
        grad_value_weight,
        grad_out_weight,
        shard_of(D, D),
        grad_cross_query,
        grad_cross_key,
        grad_cross_value,
        grad_cross_out,
        shard_of(2 * D, D),
        grad_gate_weight,
        grad_up_weight,
        grad_down,
        shard_of(3 * D, 512).reshape(BUCKETS // shards, HEADS),
    )


def solution(mesh):
    shape = mesh.devices.shape
    fine = Mesh(mesh.devices.reshape(shape[0] // 2, 2, shape[1]), ("line", "core", "fsdp"))
    tokens = P("fsdp", CTX, None)
    matrix = P("fsdp", None)
    vector = P("fsdp")
    weights = (vector, matrix, matrix, matrix, matrix, vector, matrix, matrix, matrix, matrix, vector)
    weights = weights + (matrix, matrix, matrix, matrix)
    in_specs = (tokens, tokens, tokens, P("fsdp", CTX), matrix, P(), P()) + weights
    out_specs = (tokens, P(), tokens, tokens) + weights
    return jax.shard_map(body, mesh=fine, in_specs=in_specs, out_specs=out_specs, check_vma=False)
```

```python
import functools
import jax
import jax.numpy as jnp
from jax import lax
from jax.experimental import pallas as pl
from jax.experimental.pallas import tpu as pltpu
from jax.sharding import Mesh
from jax.sharding import PartitionSpec as P

HEAD = 64
BLOCK = 128
NEGATIVE = -1e30
SPAN = 512
F32 = jnp.float32
BF16 = jnp.bfloat16


def nt(left, right):
    return lax.dot_general(left, right, (((1,), (1,)), ((), ())), preferred_element_type=F32)


def nn(left, right):
    return jnp.dot(left, right, preferred_element_type=F32)


def pad_heads(block):
    wide = block.astype(F32)
    lane = lax.broadcasted_iota(jnp.int32, (BLOCK, BLOCK), 1)
    parts = []
    for group in range(2):
        slab = wide[:, group * BLOCK : (group + 1) * BLOCK]
        turned = pltpu.roll(slab, HEAD, 1)
        keep = (lane < HEAD) if group == 0 else (lane >= HEAD)
        for part in range(2):
            source = slab if part == group else turned
            parts.append(jnp.where(keep, source, 0.0))
    return jnp.concatenate(parts, axis=0).astype(BF16)


def unpad_heads(turned):
    parts = [turned[:, index * BLOCK : (index + 1) * BLOCK].T for index in range(4)]
    return jnp.concatenate(parts, axis=1)


def fill_bias(vectors_ref, bias_ref):
    for head in range(4):
        row = jnp.broadcast_to(vectors_ref[0, head : head + 1, :], (BLOCK, SPAN))
        turned = pltpu.roll(row, 0, 1, stride=1, stride_axis=0)
        lanes = slice(head * BLOCK, (head + 1) * BLOCK)
        bias_ref[0, :, lanes] = turned[:, :BLOCK]
        bias_ref[1, :, lanes] = turned[:, BLOCK : 2 * BLOCK]
        bias_ref[2, :, lanes] = jnp.broadcast_to(row[:, BLOCK : BLOCK + 1], (BLOCK, BLOCK))


def four(tile):
    return jnp.concatenate([tile] * 4, axis=1)


def forward_kernel(masked, table, *refs):
    if masked:
        q_ref, k_ref, v_ref, vec_ref, low_ref, high_ref, a_ref, o_ref, l_ref, bias_ref, acc_ref = refs
        fill_bias(vec_ref, bias_ref)
    else:
        q_ref, k_ref, v_ref, a_ref, o_ref, l_ref, acc_ref = refs
    pairs = q_ref.shape[0] // BLOCK
    steps = k_ref.shape[0] // BLOCK
    row = lax.broadcasted_iota(jnp.int32, (BLOCK, BLOCK), 0)
    for index in range(pairs):
        rows = slice(index * BLOCK, (index + 1) * BLOCK)
        query = pad_heads(q_ref[rows, :])
        if masked:
            mine = table[index]
            first = table[pairs + index]
            low = low_ref[index : index + 1, :]
            high = high_ref[index : index + 1, :]

        def scores(step, near):
            if not masked:
                place = pl.multiple_of(step * BLOCK, BLOCK)
                return place, nt(k_ref[pl.ds(place, BLOCK), :], query)
            block = mine - step
            place = pl.multiple_of(table[2 * pairs + block] * BLOCK, BLOCK)
            raw = nt(k_ref[pl.ds(place, BLOCK), :], query)
            position = row + block * BLOCK
            allowed = position >= low
            if near:
                allowed = allowed & (position <= high)
                raw = raw + bias_ref[0]
            else:
                raw = raw + bias_ref[jnp.minimum(step, 2)]
            return place, jnp.where(four(allowed), raw, NEGATIVE)

        def gather(place, weight):
            turned = v_ref[pl.ds(place, BLOCK), :].astype(F32).T.astype(BF16)
            low_half = nn(turned[:HEAD], weight[:, : 2 * BLOCK])
            high_half = nn(turned[HEAD:], weight[:, 2 * BLOCK :])
            return jnp.concatenate([low_half, high_half], axis=1)

        place, raw = scores(0, True)
        top = jnp.max(raw, axis=0, keepdims=True)
        weight = jnp.exp(raw - top)
        total = jnp.sum(weight, axis=0, keepdims=True)
        acc_ref[...] = gather(place, weight.astype(BF16))

        def advance(step, carry):
            top, total = carry
            place, raw = scores(step, False)
            new_top = jnp.maximum(top, jnp.max(raw, axis=0, keepdims=True))
            factor = jnp.exp(top - new_top)
            weight = jnp.exp(raw - new_top)
            total = total * factor + jnp.sum(weight, axis=0, keepdims=True)
            acc_ref[...] = acc_ref[...] * factor + gather(place, weight.astype(BF16))
            return new_top, total

        count = mine - first + 1 if masked else steps
        top, total = lax.fori_loop(1, count, advance, (top, total))
        out = acc_ref[...] / total
        o_ref[0, index] = out
        l_ref[0, index] = jnp.broadcast_to(top + jnp.log(total), (8, 4 * BLOCK))
        a_ref[rows, :] = unpad_heads(out).astype(BF16)


def backward_kernel(masked, table, *refs):
    if masked:
        (q_ref, k_ref, v_ref, g_ref, o_ref, l_ref, vec_ref, low_ref, high_ref,
         dq_ref, dkv_ref, dvec_ref, bias_ref, dk_acc, dv_acc, dq_acc, near_ref, far_ref) = refs
        fill_bias(vec_ref, bias_ref)
        near_ref[...] = jnp.zeros_like(near_ref)
        far_ref[...] = jnp.zeros_like(far_ref)
    else:
        (q_ref, k_ref, v_ref, g_ref, o_ref, l_ref, dq_ref, dkv_ref, dk_acc, dv_acc, dq_acc) = refs
    pairs = q_ref.shape[0] // BLOCK
    steps = k_ref.shape[0] // BLOCK
    dk_acc[...] = jnp.zeros_like(dk_acc)
    dv_acc[...] = jnp.zeros_like(dv_acc)
    row = lax.broadcasted_iota(jnp.int32, (BLOCK, BLOCK), 0)
    for index in range(pairs):
        rows = slice(index * BLOCK, (index + 1) * BLOCK)
        query = pad_heads(q_ref[rows, :])
        grad = pad_heads(g_ref[rows, :])
        log_total = l_ref[0, index, :1, :]
        raw_grad = g_ref[rows, :].astype(F32)
        turned_grad = jnp.concatenate(
            [raw_grad[:, head * HEAD : (head + 1) * HEAD].T for head in range(4)], axis=1
        )
        delta = jnp.sum(turned_grad * o_ref[0, index], axis=0, keepdims=True)
        if masked:
            mine = table[index]
            first = table[pairs + index]
            low = low_ref[index : index + 1, :]
            high = high_ref[index : index + 1, :]

        def tile(step, near, start):
            if masked:
                block = mine - step
                place = pl.multiple_of(table[2 * pairs + block] * BLOCK, BLOCK)
            else:
                place = pl.multiple_of(step * BLOCK, BLOCK)
            keys = k_ref[pl.ds(place, BLOCK), :]
            raw = nt(keys, query)
            if masked:
                position = row + block * BLOCK
                allowed = position >= low
                if near:
                    allowed = allowed & (position <= high)
                    raw = raw + bias_ref[0]
                else:
                    raw = raw + bias_ref[jnp.minimum(step, 2)]
                raw = jnp.where(four(allowed), raw, NEGATIVE)
            prob = jnp.exp(raw - log_total)
            grad_prob = nt(v_ref[pl.ds(place, BLOCK), :], grad)
            grad_score = (prob * (grad_prob - delta)).astype(BF16)
            dv_acc[pl.ds(place, BLOCK), :] += nn(prob.astype(BF16), grad)
            dk_acc[pl.ds(place, BLOCK), :] += nn(grad_score, query)
            turned = keys.astype(F32).T.astype(BF16)
            part = jnp.concatenate(
                [nn(turned[:HEAD], grad_score[:, : 2 * BLOCK]), nn(turned[HEAD:], grad_score[:, 2 * BLOCK :])],
                axis=1,
            )
            if start:
                dq_acc[...] = part
            else:
                dq_acc[...] += part
            return grad_score

        grad_score = tile(0, True, True)
        if masked:
            near_ref[0] += grad_score.astype(F32)
            last = mine - first

            @pl.when(last >= 1)
            def _():
                near_ref[1] += tile(1, False, False).astype(F32)

            def advance(step, carry):
                wide = tile(step, False, False).astype(F32)
                far_ref[...] += jnp.sum(wide.reshape(BLOCK // 8, 8, 4 * BLOCK), axis=0)
                return carry

            lax.fori_loop(2, last + 1, advance, 0)
        else:

            def advance(step, carry):
                tile(step, False, False)
                return carry

            lax.fori_loop(1, steps, advance, 0)
        dq_ref[rows, :] = unpad_heads(dq_acc[...]).astype(BF16)
    dkv_ref[0] = dk_acc[...].astype(BF16)
    dkv_ref[1] = dv_acc[...].astype(BF16)
    if masked:
        rowid = lax.broadcasted_iota(jnp.int32, (BLOCK, SPAN), 0)
        lane = lax.broadcasted_iota(jnp.int32, (1, SPAN), 1)
        for head in range(4):
            lanes = slice(head * BLOCK, (head + 1) * BLOCK)
            wide = jnp.concatenate(
                [near_ref[0, :, lanes], near_ref[1, :, lanes], jnp.zeros((BLOCK, 2 * BLOCK), F32)], axis=1
            )
            bit = 1
            while bit < BLOCK:
                wide = jnp.where((rowid & bit) != 0, pltpu.roll(wide, SPAN - bit, 1), wide)
                bit = bit * 2
            sums = jnp.sum(wide, axis=0, keepdims=True)
            far = jnp.sum(far_ref[:, lanes])
            dvec_ref[0, head : head + 1, :] = sums + jnp.where(lane == BLOCK, far, 0.0)


def specs_of(rows, length, pairs, groups, first=0):
    cols = pl.BlockSpec((rows, 2 * BLOCK), lambda g, *_: (0, g + first))
    keys = pl.BlockSpec((length, BLOCK), lambda g, *_: (0, g + first))
    values = pl.BlockSpec((length, BLOCK), lambda g, *_: (0, groups + g + first))
    outs = pl.BlockSpec((1, pairs, HEAD, 4 * BLOCK), lambda g, *_: (g + first, 0, 0, 0))
    logs = pl.BlockSpec((1, pairs, 8, 4 * BLOCK), lambda g, *_: (g + first, 0, 0, 0))
    vecs = pl.BlockSpec((1, 4, SPAN), lambda g, *_: (g + first, 0, 0))
    lims = pl.BlockSpec((pairs, BLOCK), lambda g, *_: (0, 0))
    return cols, keys, values, outs, logs, vecs, lims


def attend(query, keys_values, table, extra, masked):
    rows, width = query.shape
    length = keys_values.shape[0]
    groups = width // (4 * HEAD)
    pairs = rows // BLOCK
    cols, kspec, vspec, outs, logs, vecs, lims = specs_of(rows, length, pairs, groups)
    scratch = [pltpu.VMEM((HEAD, 4 * BLOCK), F32)]
    if masked:
        scratch = [pltpu.VMEM((3, BLOCK, 4 * BLOCK), F32)] + scratch
    return pl.pallas_call(
        functools.partial(forward_kernel, masked),
        grid_spec=pltpu.PrefetchScalarGridSpec(
            num_scalar_prefetch=1,
            grid=(groups,),
            in_specs=[cols, kspec, vspec] + ([vecs, lims, lims] if masked else []),
            out_specs=[cols, outs, logs],
            scratch_shapes=scratch,
        ),
        out_shape=[
            jax.ShapeDtypeStruct((rows, width), BF16),
            jax.ShapeDtypeStruct((groups, pairs, HEAD, 4 * BLOCK), F32),
            jax.ShapeDtypeStruct((groups, pairs, 8, 4 * BLOCK), F32),
        ],
        cost_estimate=pl.CostEstimate(
            flops=4 * rows * length * width, bytes_accessed=4 * length * width, transcendentals=rows * length * 16
        ),
        name="attend_self" if masked else "attend_cross",
    )(table, query, keys_values, keys_values, *extra)


def attend_back(query, keys_values, grad, outs_in, logs_in, table, extra, masked, part=0, parts=1):
    rows, width = query.shape
    length = keys_values.shape[0]
    groups = width // (4 * HEAD)
    pairs = rows // BLOCK
    count = groups // parts
    cols, kspec, vspec, outs, logs, vecs, lims = specs_of(rows, length, pairs, groups, part * count)
    scratch = [pltpu.VMEM((length, BLOCK), F32), pltpu.VMEM((length, BLOCK), F32), pltpu.VMEM((HEAD, 4 * BLOCK), F32)]
    out_specs = [pl.BlockSpec((rows, 2 * BLOCK), lambda g, *_: (0, g)), pl.BlockSpec((2, length, BLOCK), lambda g, *_: (0, 0, g))]
    out_shape = [
        jax.ShapeDtypeStruct((rows, width // parts), BF16),
        jax.ShapeDtypeStruct((2, length, width // 2 // parts), BF16),
    ]
    if masked:
        scratch = [pltpu.VMEM((3, BLOCK, 4 * BLOCK), F32)] + scratch
        scratch += [pltpu.VMEM((2, BLOCK, 4 * BLOCK), F32), pltpu.VMEM((8, 4 * BLOCK), F32)]
        out_specs = out_specs + [pl.BlockSpec((1, 4, SPAN), lambda g, *_: (g, 0, 0))]
        out_shape = out_shape + [jax.ShapeDtypeStruct((count, 4, SPAN), F32)]
    return pl.pallas_call(
        functools.partial(backward_kernel, masked),
        grid_spec=pltpu.PrefetchScalarGridSpec(
            num_scalar_prefetch=1,
            grid=(count,),
            in_specs=[cols, kspec, vspec, cols, outs, logs] + ([vecs, lims, lims] if masked else []),
            out_specs=out_specs,
            scratch_shapes=scratch,
        ),
        out_shape=out_shape,
        cost_estimate=pl.CostEstimate(
            flops=10 * rows * length * width // parts, bytes_accessed=8 * length * width // parts,
            transcendentals=rows * length * 16 // parts
        ),
        name="attend_self_back" if masked else "attend_cross_back",
    )(table, query, keys_values, keys_values, grad, outs_in, logs_in, *extra)


def offset_index(half):
    place = jnp.arange(SPAN, dtype=jnp.int32)
    behind = jnp.where(place >= 2 * BLOCK, place - SPAN, place)
    return behind, jnp.clip(half - behind, 0, 2 * half - 1)


D = 1024
HEADS = 16
KV_HEADS = 8
BUCKETS = 32
EPS = 1e-06
CTX = ("line", "core")


def tn(left, right):
    return lax.dot_general(left, right, (((0,), (0,)), ((), ())), preferred_element_type=F32)


def norm_rows(values, gain):
    scale = lax.rsqrt(jnp.mean(values * values, axis=-1, keepdims=True) + EPS)
    normed = values * scale
    return normed, scale, (normed * gain).astype(BF16)


def norm_back(grad_out, normed, scale, gain):
    grad_gain = jnp.sum(grad_out * normed, axis=0)
    inner = grad_out * gain
    grad_in = scale * (inner - normed * jnp.mean(inner * normed, axis=-1, keepdims=True))
    return grad_in, grad_gain


def gelu_tanh(value):
    return jax.nn.gelu(value, approximate=True)


def partners(size, bit):
    return [(index, index ^ bit) for index in range(size)]


def bits_of(size):
    return [1 << place for place in range(size.bit_length() - 1)]


def cross(value, axis, bit):
    return lax.ppermute(value, axis, partners(lax.axis_size(axis), bit))


def swap(value):
    return cross(value, "core", 1)


def add(left, right):
    return (left.astype(F32) + right.astype(F32)).astype(BF16)


def place_kernel(spots, rows, me_ref, *refs):
    pieces, whole_ref, sems = refs[: len(spots)], refs[len(spots)], refs[len(spots) + 1]
    copies = []
    for index, (mask, offset) in enumerate(spots):
        count = pieces[index].shape[0]
        start = pl.multiple_of((me_ref[0] ^ mask) * rows + offset, count)
        copies.append(pltpu.make_async_copy(pieces[index], whole_ref.at[pl.ds(start, count), :], sems.at[index]))
    for copy in copies:
        copy.start()
    for copy in copies:
        copy.wait()


def place(me, pieces, spots, size, rows):
    anywhere = pl.BlockSpec(memory_space=pl.ANY)
    return pl.pallas_call(
        functools.partial(place_kernel, spots, rows),
        in_specs=[pl.BlockSpec(memory_space=pltpu.SMEM)] + [pl.BlockSpec(memory_space=pltpu.VMEM)] * len(pieces),
        out_specs=anywhere,
        out_shape=jax.ShapeDtypeStruct((size * rows, pieces[0].shape[1]), BF16),
        scratch_shapes=[pltpu.SemaphoreType.DMA((len(pieces),))],
        name="place",
    )(me.reshape(1), *pieces)


class Lane:
    def __init__(self, steps):
        self.steps = steps
        self.result = None
        self.pending = next(steps)

    def push(self, arrived):
        try:
            self.pending = self.steps.send(arrived)
        except StopIteration as end:
            self.pending, self.result = None, end.value

    def take(self):
        while self.pending is not None:
            tick([self], ())
        return self.result

    def take(self):
        while self.pending is not None:
            tick([self], ())
        return self.result


def tick(lanes, live):
    active = [lane for lane in lanes if lane.pending is not None]
    live, arrived = lax.optimization_barrier((live, [lane.pending for lane in active]))
    for lane, value in zip(active, arrived):
        lane.push(value)
    return live


def swap_steps(*values):
    got = yield [swap(value) for value in values]
    return got


def sum_steps(value):
    for axis in ("core", "fsdp", "line"):
        for bit in bits_of(lax.axis_size(axis)):
            (got,) = yield [cross(value, axis, bit)]
            value = value + got
    return value


def count_steps(value):
    (got,) = yield [swap(value)]
    value = value + got
    got = yield [cross(value, "line", mask) for mask in range(1, lax.axis_size("line"))]
    return value + sum(got)


def small_steps(value):
    size = lax.axis_size("fsdp")
    me = lax.axis_index("fsdp")
    have = [(0, value)]
    for bit in bits_of(size):
        got = yield [cross(piece, "fsdp", bit) for _, piece in have]
        have = have + [(mask ^ bit, piece) for (mask, _), piece in zip(have, got)]
    whole = jnp.zeros((size, value.shape[0]), value.dtype)
    for mask, piece in have:
        whole = lax.dynamic_update_slice(whole, piece[None], (me ^ mask, 0))
    return whole


def columns_of(value, core):
    half = value.shape[1] // 2
    return lax.dynamic_slice_in_dim(value, core * half, half, axis=1)


def half_columns(parts):
    core = lax.axis_index("core")
    return jnp.concatenate([columns_of(part, core) for part in parts], axis=1)


def gather_steps(mine, fine=False):
    size = lax.axis_size("fsdp")
    me = lax.axis_index("fsdp")
    rows, width = mine.shape
    bits = bits_of(size)
    half = rows // 2
    streams = [[(0, mine[stream * half : (stream + 1) * half])] for stream in range(2)]
    for step in range(len(bits)):
        chosen = [(bits if stream == 0 else bits[::-1])[step] for stream in range(2)]
        have = len(streams[0])
        got = [[], []]
        for spot in range(have) if fine else [slice(0, have)]:
            spot = spot if isinstance(spot, slice) else slice(spot, spot + 1)
            arrived = yield [
                [cross(piece, "fsdp", chosen[stream]) for _, piece in streams[stream][spot]] for stream in range(2)
            ]
            got = [got[stream] + arrived[stream] for stream in range(2)]
        for stream in range(2):
            fresh = [(mask ^ chosen[stream], piece) for (mask, _), piece in zip(streams[stream], got[stream])]
            streams[stream] = streams[stream] + fresh
    spots = [(0, 0)] + [(mask, stream * half) for stream in range(2) for mask, _ in streams[stream][1:]]
    pieces = [mine] + [piece for stream in range(2) for _, piece in streams[stream][1:]]
    whole = place(me, pieces, spots, size, rows)
    whole, other = yield whole, swap(whole)
    return whole, other


def by_core(mine, other):
    first = lax.axis_index("core") == 0
    return jnp.where(first, mine, other), jnp.where(first, other, mine)


def grad_halves(*grads):
    core = lax.axis_index("core")
    mine = jnp.concatenate([columns_of(item, core) for item in grads], axis=1)
    return mine, jnp.concatenate([columns_of(item, 1 - core) for item in grads], axis=1)


def weight_grad(hidden, hidden_swapped, mine, arrived):
    both_hidden = jnp.concatenate([hidden, hidden_swapped], axis=0)
    both_grad = jnp.concatenate([mine, arrived], axis=0)
    return tn(both_hidden, both_grad).astype(BF16)


def split(value, axis, bit, place):
    mine = (lax.axis_index(axis) // bit) % 2
    keep = lax.dynamic_index_in_dim(value, mine, place, keepdims=False)
    return keep, lax.dynamic_index_in_dim(value, 1 - mine, place, keepdims=False)


def reduce_steps(partials, widths):
    size = lax.axis_size("fsdp")
    lines = lax.axis_size("line")
    rows = partials[0].shape[0] // size
    width = partials[0].shape[1]
    many = len(partials)
    bits = bits_of(size)
    folded = jnp.stack(partials).reshape([many] + [2] * len(bits) + [2, rows // 2, width])
    values = [lax.index_in_dim(folded, stream, 1 + len(bits), keepdims=False) for stream in range(2)]
    left = [bits[::-1], bits[::-1]]
    for step in range(len(bits)):
        chosen = [(bits if stream == 0 else bits[::-1])[step] for stream in range(2)]
        parts = [
            split(values[stream], "fsdp", chosen[stream], 1 + left[stream].index(chosen[stream]))
            for stream in range(2)
        ]
        got = yield [cross(parts[stream][1], "fsdp", chosen[stream]) for stream in range(2)]
        values = [add(parts[stream][0], got[stream]) for stream in range(2)]
        left = [[item for item in left[stream] if item != chosen[stream]] for stream in range(2)]
    shard = jnp.stack(values, axis=1)
    line_bits = bits_of(lines)
    value = shard.reshape([many] + [2] * len(line_bits) + [rows // lines, width])
    for bit in line_bits:
        keep, send = split(value, "line", bit, value.ndim - 3)
        (got,) = yield [cross(send, "line", bit)]
        value = add(keep, got)
    mine = value[None]
    for bit in line_bits[::-1]:
        (got,) = yield [cross(mine, "line", bit)]
        mine = jnp.concatenate([mine, got], axis=0)
    (other,) = yield [swap(mine)]
    me = lax.axis_index("line")

    def spot(entry):
        mask = me ^ entry
        return sum(((mask // bit) % 2) * (lines // (2 * bit)) for bit in line_bits)

    outs = []
    for index in range(many):
        start = 0
        for wide in widths[index]:
            part = slice(start, start + wide // 2)
            both = jnp.concatenate(by_core(mine[:, index, :, part], other[:, index, :, part]), axis=2)
            ordered = [lax.dynamic_index_in_dim(both, spot(entry), 0, keepdims=False) for entry in range(lines)]
            outs.append(jnp.concatenate(ordered, axis=0).astype(F32))
            start = start + wide // 2
    return outs


def gather_context_steps(value):
    rows = value.shape[0]
    mine = value
    masks = [0]
    for bit in bits_of(lax.axis_size("line"))[::-1]:
        (got,) = yield [cross(mine, "line", bit)]
        mine = jnp.concatenate([mine, got], axis=0)
        masks = masks + [mask ^ bit for mask in masks]
    order = [masks.index(mask) for mask in range(len(masks))]
    mine = jnp.concatenate([mine[at * rows : (at + 1) * rows] for at in order], axis=0)
    (other,) = yield [swap(mine)]
    return jnp.concatenate([mine, other], axis=0)


def reduce_context_steps(value):
    lines = lax.axis_size("line")
    two, total, width = value.shape
    value = value.reshape(two, 2, lines, total // (2 * lines), width)
    (got,) = yield [swap(value[:, 1])]
    value = add(value[:, 0], got)
    for bit in bits_of(lines):
        value = value.reshape(two, value.shape[1] // 2, 2, value.shape[2], width)
        (got,) = yield [cross(value[:, :, 1], "line", bit)]
        value = add(value[:, :, 0], got)
    return value[:, 0]


def body(
    inputs, encoder, teacher, valid_mask, doc_ids, block_order, buckets,
    gain_self, w_query, w_key, w_value, w_out, gain_cross, c_query, c_key, c_value, c_out,
    gain_ffn, w_gate, w_up, w_down, bias_table,
):
    rows, width = inputs.shape[1:]
    lines = lax.axis_size("line")
    shards = lax.axis_size("fsdp")
    contexts = 2 * lines
    length = rows * contexts
    pair = rows // BLOCK
    token_total = length * shards
    key_width = KV_HEADS * HEAD
    context = lax.axis_index("line") * 2 + lax.axis_index("core")
    fsdp = lax.axis_index("fsdp")

    core = lax.axis_index("core")
    hidden_ff = w_gate.shape[1]
    joint = jnp.concatenate
    halves = D // 2
    share = gain_self.shape[0]

    def times(left, weight):
        return joint(by_core(nn(left, weight[0]), nn(left, weight[1])), axis=1)

    def times_back(grad, weight):
        return nt(columns_of(grad, core), weight[0]) + nt(columns_of(grad, 1 - core), weight[1])

    mask_rows = valid_mask.reshape(rows).astype(F32)
    assert rows <= 256
    local_count = jnp.broadcast_to(jnp.sum(mask_rows), (128,)).astype(BF16)
    lane_qkv = Lane(gather_steps(half_columns([joint([w_query, w_key, w_value], axis=1)])))
    lane_small = Lane(small_steps(joint([gain_self, gain_cross, gain_ffn, bias_table.reshape(-1), local_count])))
    mid_parts = tick([lane_qkv, lane_small], (w_out, c_query, c_key, c_value, c_out))

    mid_shard = half_columns([mid_parts[0], mid_parts[1], joint(mid_parts[2:4], axis=1), mid_parts[4]])
    mid_shard, late = tick([lane_qkv, lane_small], (mid_shard, (w_gate, w_up, doc_ids, block_order, buckets)))
    w_gate, w_up, doc_ids, block_order, buckets = late

    small = lane_small.take()
    gain_one, gain_two, gain_three = [
        small[:, index * share : (index + 1) * share].reshape(D).astype(F32) for index in range(3)
    ]
    table_whole = small[:, 3 * share : -128].reshape(BUCKETS, HEADS)
    lane_count = Lane(count_steps(jnp.broadcast_to(jnp.sum(small[:, -128:].astype(F32), axis=0), (8, 128))))
    flat_in = inputs.reshape(rows, width).astype(F32)
    normed_one, scale_one, hidden_one = norm_rows(flat_in, gain_one)
    gu_shard = half_columns([joint([w_gate, w_up], axis=1)])

    query_blocks = lax.dynamic_slice_in_dim(block_order, context * pair, pair)
    slots = jnp.arange(contexts * pair, dtype=jnp.int32)
    owner = slots // pair
    near = ((owner % 2) ^ core) * lines + ((owner // 2) ^ lax.axis_index("line"))
    slots_near = near * pair + slots % pair
    inverse = jnp.sum(jnp.where(block_order[None, :] == slots[:, None], slots_near[None, :], 0), axis=1)
    docs = doc_ids.reshape(length)
    query_docs = jnp.stack(
        [lax.dynamic_slice_in_dim(docs, query_blocks[index] * BLOCK, BLOCK) for index in range(pair)]
    )
    low = jnp.sum((docs[None, None, :] < query_docs[:, :, None]).astype(jnp.int32), axis=-1)
    high = jnp.sum((docs[None, None, :] <= query_docs[:, :, None]).astype(jnp.int32), axis=-1) - 1
    place_table = jnp.concatenate([query_blocks, low[:, 0] // BLOCK, inverse]).astype(jnp.int32)
    behind, index_of = offset_index(length)
    bucket_match = (jnp.take(buckets, index_of)[None, :] == jnp.arange(BUCKETS, dtype=jnp.int32)[:, None])

    vectors = tn(table_whole, bucket_match.astype(BF16)).reshape(HEADS // 4, 4, SPAN)
    hidden_one, gu_shard, low, high, place_table, bucket_match, vectors = tick(
        [lane_qkv, lane_count], (hidden_one, gu_shard, low, high, place_table, bucket_match, vectors)
    )
    extra = (vectors, low, high)

    qkv_mine, qkv_other = lane_qkv.take()
    lane_mid = Lane(gather_steps(mid_shard))
    query, pairs = by_core(nn(hidden_one, qkv_mine).astype(BF16), nn(hidden_one, qkv_other).astype(BF16))
    query, pairs, w_down = tick([lane_mid, lane_count], (query, pairs, w_down))

    lane_keys = Lane(gather_context_steps(pairs))
    wd_shard = half_columns([w_down])
    wd_shard = tick([lane_keys, lane_mid], wd_shard)

    lane_gu = Lane(gather_steps(gu_shard, True))
    tick([lane_keys, lane_mid, lane_gu], ())
    mid_mine, mid_other = lane_mid.take()
    wo, wcq, wckv, wco = [
        (mid_mine[:, index * halves : (index + 1) * halves], mid_other[:, index * halves : (index + 1) * halves])
        for index in range(4)
    ]
    encoder_rows = encoder.reshape(encoder.shape[1], width)
    encoder_pairs = times(encoder_rows, wckv).astype(BF16)
    encoder_pairs, wd_shard = tick([lane_keys], (encoder_pairs, wd_shard))
    pairs_whole = lane_keys.take()

    lane_encoder = Lane(gather_context_steps(encoder_pairs))
    lane_encoder_rows = Lane(swap_steps(encoder_rows))
    lane_wd = Lane(gather_steps(wd_shard))
    lane_hidden_one = Lane(swap_steps(hidden_one))
    attention, outs_one, logs_one = attend(query, pairs_whole, place_table, extra, True)
    attention, outs_one, logs_one = tick(
        [lane_encoder, lane_encoder_rows, lane_gu, lane_hidden_one], (attention, outs_one, logs_one)
    )

    lane_attention = Lane(swap_steps(attention))
    mid_one = flat_in + times(attention, wo)
    normed_two, scale_two, hidden_two = norm_rows(mid_one, gain_two)
    cross_q = times(hidden_two, wcq).astype(BF16)
    mid_one, normed_two, hidden_two, cross_q, scale_two = tick(
        [lane_encoder, lane_attention, lane_gu, lane_wd], (mid_one, normed_two, hidden_two, cross_q, scale_two)
    )
    tick([lane_encoder], ())
    encoder_whole = lane_encoder.take()

    lane_hidden_two = Lane(swap_steps(hidden_two))
    crossed, outs_two, logs_two = attend(cross_q, encoder_whole, place_table, (), False)
    crossed, outs_two, logs_two = tick([lane_gu, lane_wd, lane_hidden_two], (crossed, outs_two, logs_two))

    lane_crossed = Lane(swap_steps(crossed))
    mid_two = mid_one + times(crossed, wco)
    normed_three, scale_three, hidden_three = norm_rows(mid_two, gain_three)
    mid_two, normed_three, hidden_three, scale_three = tick(
        [lane_wd, lane_crossed], (mid_two, normed_three, hidden_three, scale_three)
    )

    gu_mine, gu_other = lane_gu.take()
    lane_hidden_three = Lane(swap_steps(hidden_three))
    gate, up = by_core(nn(hidden_three, gu_mine), nn(hidden_three, gu_other))
    active, gelu_pull = jax.vjp(gelu_tanh, gate)
    mixed = (active * up).astype(BF16)
    mixed, gate, up, active = tick([lane_hidden_three], (mixed, gate, up, active))
    lane_mixed = Lane(swap_steps(mixed))

    wd_mine, wd_other = lane_wd.take()
    count = jnp.maximum(lane_count.take()[0, 0], 1.0)
    result = mid_two + times(mixed, (wd_mine, wd_other))
    layer_out = result.astype(BF16)
    diff = result - teacher.reshape(rows, width).astype(F32)
    squared_local = jnp.sum(mask_rows[:, None] * diff * diff)
    grad_result = token_total / count * mask_rows[:, None] * diff

    e_three = grad_result.astype(BF16)
    down_mine, down_away = grad_halves(e_three)
    grad_result, e_three, down_mine, down_away, squared_local, layer_out = tick(
        [lane_mixed], (grad_result, e_three, down_mine, down_away, squared_local, layer_out)
    )
    lane_down = Lane(swap_steps(down_away))
    grad_mixed = times_back(e_three, (wd_mine, wd_other))
    (gelu_slope,) = gelu_pull(grad_mixed * up)
    grad_gate = gelu_slope.astype(BF16)
    grad_up = (grad_mixed * active).astype(BF16)
    wide_mine, wide_away = grad_halves(grad_gate, grad_up)
    grad_gate, grad_up, wide_mine, wide_away = tick([lane_down], (grad_gate, grad_up, wide_mine, wide_away))

    lane_wide = Lane(swap_steps(wide_away))
    partial_down = weight_grad(mixed, lane_mixed.take()[0], down_mine, lane_down.take()[0])
    partial_down = tick([lane_wide], partial_down)

    lane_down = Lane(reduce_steps([partial_down], [(D,)]))
    partial_wide = weight_grad(hidden_three, lane_hidden_three.take()[0], wide_mine, lane_wide.take()[0])
    grad_hidden_three = times_back(joint([grad_gate, grad_up], axis=1), (gu_mine, gu_other))
    partial_wide, grad_hidden_three = tick([lane_down], (partial_wide, grad_hidden_three))

    lane_wide = Lane(reduce_steps([partial_wide], [(hidden_ff, hidden_ff)]))
    grad_norm_three, grad_gain_three = norm_back(grad_hidden_three, normed_three, scale_three, gain_three)
    grad_mid_two = grad_result + grad_norm_three

    e_two = grad_mid_two.astype(BF16)
    grad_cross = times_back(e_two, wco).astype(BF16)
    grad_cross_q, encoder_grad = attend_back(
        cross_q, encoder_whole, grad_cross, outs_two, logs_two, place_table, (), False
    )
    out_mine, out_away = grad_halves(e_two, grad_cross_q)
    grad_mid_two, grad_cross_q, encoder_grad, out_mine, out_away = tick(
        [lane_down, lane_wide], (grad_mid_two, grad_cross_q, encoder_grad, out_mine, out_away)
    )

    lane_encoder = Lane(reduce_context_steps(encoder_grad))
    lane_out = Lane(swap_steps(out_away))
    grad_norm_two, grad_gain_two = norm_back(times_back(grad_cross_q, wcq), normed_two, scale_two, gain_two)
    grad_mid_one = grad_mid_two + grad_norm_two

    e_one = grad_mid_one.astype(BF16)
    one_mine, one_away = grad_halves(e_one)
    grad_attention = times_back(e_one, wo).astype(BF16)
    grad_mid_one, one_mine, one_away, grad_attention = tick(
        [lane_down, lane_wide, lane_encoder, lane_out], (grad_mid_one, one_mine, one_away, grad_attention)
    )
    lane_one = Lane(swap_steps(one_away))

    def attend_part(part):
        return attend_back(
            query, pairs_whole, grad_attention, outs_one, logs_one, place_table, extra, True, part, 2
        )

    query_first, pairs_first, vectors_first = attend_part(0)
    query_first, pairs_first, vectors_first, grad_attention = tick(
        [lane_down, lane_wide, lane_encoder, lane_one], (query_first, pairs_first, vectors_first, grad_attention)
    )
    lane_first = Lane(reduce_context_steps(pairs_first))
    query_second, pairs_second, vectors_second = attend_part(1)
    grad_query = joint([query_first, query_second], axis=1)
    grad_vectors = joint([vectors_first, vectors_second], axis=0)
    query_mine, query_away = grad_halves(grad_query)
    pairs_second, grad_query, grad_vectors, query_mine, query_away = tick(
        [lane_down, lane_wide, lane_encoder, lane_first],
        (pairs_second, grad_query, grad_vectors, query_mine, query_away),
    )

    lane_second = Lane(reduce_context_steps(pairs_second))
    lane_query = Lane(swap_steps(query_away))
    arrived = lane_out.take()[0]
    partial_out = weight_grad(crossed, lane_crossed.take()[0], out_mine[:, :halves], arrived[:, :halves])
    partial_cross = weight_grad(hidden_two, lane_hidden_two.take()[0], out_mine[:, halves:], arrived[:, halves:])
    partial_one = weight_grad(attention, lane_attention.take()[0], one_mine, lane_one.take()[0])
    encoder_got = lane_encoder.take()
    encoder_mine = joint([encoder_got[0], encoder_got[1]], axis=1)
    keys_mine, keys_away = grad_halves(encoder_mine[:, :key_width], encoder_mine[:, key_width:])
    partial_out, partial_cross, partial_one, encoder_mine, keys_mine, keys_away = tick(
        [lane_first, lane_second, lane_down, lane_wide, lane_query],
        (partial_out, partial_cross, partial_one, encoder_mine, keys_mine, keys_away),
    )

    lane_keys = Lane(swap_steps(keys_away))
    partial_query = weight_grad(hidden_one, lane_hidden_one.take()[0], query_mine, lane_query.take()[0])
    lane_mid = Lane(reduce_steps([partial_out, partial_cross, partial_one, partial_query], [(D,)] * 4))
    grad_encoder = times_back(encoder_mine, wckv)
    grad_encoder = tick([lane_first, lane_second, lane_down, lane_keys], grad_encoder)

    partial_keys = weight_grad(encoder_rows, lane_encoder_rows.take()[0], keys_mine, lane_keys.take()[0])
    partial_keys = tick([lane_second, lane_mid], partial_keys)
    pairs_first, pairs_second = lane_first.take(), lane_second.take()
    mine = [joint([pairs_first[index], pairs_second[index]], axis=1) for index in range(2)]
    last_mine, last_away = grad_halves(mine[0], mine[1])
    mine, last_mine, last_away = tick([], (mine, last_mine, last_away))

    lane_last = Lane(swap_steps(last_away))
    tick([lane_last], ())
    partial_last = weight_grad(hidden_one, lane_hidden_one.take()[0], last_mine, lane_last.take()[0])
    partial_last = tick([lane_mid, lane_wide], partial_last)

    lane_last = Lane(reduce_steps([partial_last, partial_keys], [(key_width, key_width)] * 2))
    grad_packed = joint([grad_query, mine[0], mine[1]], axis=1)
    grad_norm_one, grad_gain_one = norm_back(
        times_back(grad_packed, (qkv_mine, qkv_other)), normed_one, scale_one, gain_one
    )
    grad_inputs = grad_mid_one + grad_norm_one

    grad_table = lax.dot_general(
        bucket_match.astype(F32) * ((behind >= 1 - BLOCK) & (behind < 2 * BLOCK)).astype(F32)[None, :],
        grad_vectors.reshape(HEADS, SPAN),
        (((1,), (1,)), ((), ())),
        precision=lax.Precision.HIGHEST,
        preferred_element_type=F32,
    )
    sums = jnp.concatenate(
        [
            grad_gain_one,
            grad_gain_two,
            grad_gain_three,
            grad_table.reshape(-1),
            jnp.broadcast_to(squared_local, (512,)),
        ]
    )
    sums, grad_inputs = tick([lane_last, lane_wide, lane_mid, lane_down], (sums.reshape(-1, 128), grad_inputs))
    lane_sums = Lane(sum_steps(sums))
    lanes = [lane_last, lane_wide, lane_mid, lane_down, lane_sums]
    while any(lane.pending is not None for lane in lanes):
        tick(lanes, ())
    sums = lane_sums.take().reshape(-1)
    (grad_down,) = lane_down.take()
    grad_gate_weight, grad_up_weight = lane_wide.take()
    grad_cross_out, grad_cross_query, grad_out_weight, grad_query_weight = lane_mid.take()
    grad_key_weight, grad_value_weight, grad_cross_key, grad_cross_value = lane_last.take()
    loss = sums[3 * D + 512] / (D * count)

    def shard_of(offset, amount):
        return lax.dynamic_slice_in_dim(sums, offset + fsdp * (amount // shards), amount // shards)

    return (
        layer_out.reshape(1, rows, width),
        loss,
        grad_inputs.reshape(1, rows, width),
        grad_encoder.reshape(1, encoder.shape[1], width),
        shard_of(0, D),
        grad_query_weight,
        grad_key_weight,
        grad_value_weight,
        grad_out_weight,
        shard_of(D, D),
        grad_cross_query,
        grad_cross_key,
        grad_cross_value,
        grad_cross_out,
        shard_of(2 * D, D),
        grad_gate_weight,
        grad_up_weight,
        grad_down,
        shard_of(3 * D, 512).reshape(BUCKETS // shards, HEADS),
    )


def solution(mesh):
    shape = mesh.devices.shape
    fine = Mesh(mesh.devices.reshape(shape[0] // 2, 2, shape[1]), ("line", "core", "fsdp"))
    tokens = P("fsdp", CTX, None)
    matrix = P("fsdp", None)
    vector = P("fsdp")
    weights = (vector, matrix, matrix, matrix, matrix, vector, matrix, matrix, matrix, matrix, vector)
    weights = weights + (matrix, matrix, matrix, matrix)
    in_specs = (tokens, tokens, tokens, P("fsdp", CTX), matrix, P(), P()) + weights
    out_specs = (tokens, P(), tokens, tokens) + weights
    return jax.shard_map(body, mesh=fine, in_specs=in_specs, out_specs=out_specs, check_vma=False)
```

```python
import functools
import jax
import jax.numpy as jnp
from jax import lax
from jax.experimental import pallas as pl
from jax.experimental.pallas import tpu as pltpu
from jax.sharding import Mesh
from jax.sharding import PartitionSpec as P

HEAD = 64
BLOCK = 128
NEGATIVE = -1e30
SPAN = 512
F32 = jnp.float32
BF16 = jnp.bfloat16


def nt(left, right):
    return lax.dot_general(left, right, (((1,), (1,)), ((), ())), preferred_element_type=F32)


def nn(left, right):
    return jnp.dot(left, right, preferred_element_type=F32)


def pad_heads(block):
    wide = block.astype(F32)
    lane = lax.broadcasted_iota(jnp.int32, (BLOCK, BLOCK), 1)
    parts = []
    for group in range(2):
        slab = wide[:, group * BLOCK : (group + 1) * BLOCK]
        turned = pltpu.roll(slab, HEAD, 1)
        keep = (lane < HEAD) if group == 0 else (lane >= HEAD)
        for part in range(2):
            source = slab if part == group else turned
            parts.append(jnp.where(keep, source, 0.0))
    return jnp.concatenate(parts, axis=0).astype(BF16)


def unpad_heads(turned):
    parts = [turned[:, index * BLOCK : (index + 1) * BLOCK].T for index in range(4)]
    return jnp.concatenate(parts, axis=1)


def fill_bias(vectors_ref, bias_ref):
    for head in range(4):
        row = jnp.broadcast_to(vectors_ref[0, head : head + 1, :], (BLOCK, SPAN))
        turned = pltpu.roll(row, 0, 1, stride=1, stride_axis=0)
        lanes = slice(head * BLOCK, (head + 1) * BLOCK)
        bias_ref[0, :, lanes] = turned[:, :BLOCK]
        bias_ref[1, :, lanes] = turned[:, BLOCK : 2 * BLOCK]
        bias_ref[2, :, lanes] = jnp.broadcast_to(row[:, BLOCK : BLOCK + 1], (BLOCK, BLOCK))


def four(tile):
    return jnp.concatenate([tile] * 4, axis=1)


def forward_kernel(masked, table, *refs):
    if masked:
        q_ref, k_ref, v_ref, vec_ref, low_ref, high_ref, a_ref, o_ref, l_ref, bias_ref, acc_ref = refs
        fill_bias(vec_ref, bias_ref)
    else:
        q_ref, k_ref, v_ref, a_ref, o_ref, l_ref, acc_ref = refs
    pairs = q_ref.shape[0] // BLOCK
    steps = k_ref.shape[0] // BLOCK
    row = lax.broadcasted_iota(jnp.int32, (BLOCK, BLOCK), 0)
    for index in range(pairs):
        rows = slice(index * BLOCK, (index + 1) * BLOCK)
        query = pad_heads(q_ref[rows, :])
        if masked:
            mine = table[index]
            first = table[pairs + index]
            low = low_ref[index : index + 1, :]
            high = high_ref[index : index + 1, :]

        def scores(step, near):
            if not masked:
                place = pl.multiple_of(step * BLOCK, BLOCK)
                return place, nt(k_ref[pl.ds(place, BLOCK), :], query)
            block = mine - step
            place = pl.multiple_of(table[2 * pairs + block] * BLOCK, BLOCK)
            raw = nt(k_ref[pl.ds(place, BLOCK), :], query)
            position = row + block * BLOCK
            allowed = position >= low
            if near:
                allowed = allowed & (position <= high)
                raw = raw + bias_ref[0]
            else:
                raw = raw + bias_ref[jnp.minimum(step, 2)]
            return place, jnp.where(four(allowed), raw, NEGATIVE)

        def gather(place, weight):
            turned = v_ref[pl.ds(place, BLOCK), :].astype(F32).T.astype(BF16)
            low_half = nn(turned[:HEAD], weight[:, : 2 * BLOCK])
            high_half = nn(turned[HEAD:], weight[:, 2 * BLOCK :])
            return jnp.concatenate([low_half, high_half], axis=1)

        place, raw = scores(0, True)
        top = jnp.max(raw, axis=0, keepdims=True)
        weight = jnp.exp(raw - top)
        total = jnp.sum(weight, axis=0, keepdims=True)
        acc_ref[...] = gather(place, weight.astype(BF16))

        def advance(step, carry):
            top, total = carry
            place, raw = scores(step, False)
            new_top = jnp.maximum(top, jnp.max(raw, axis=0, keepdims=True))
            factor = jnp.exp(top - new_top)
            weight = jnp.exp(raw - new_top)
            total = total * factor + jnp.sum(weight, axis=0, keepdims=True)
            acc_ref[...] = acc_ref[...] * factor + gather(place, weight.astype(BF16))
            return new_top, total

        count = mine - first + 1 if masked else steps
        top, total = lax.fori_loop(1, count, advance, (top, total))
        out = acc_ref[...] / total
        o_ref[0, index] = out
        l_ref[0, index] = jnp.broadcast_to(top + jnp.log(total), (8, 4 * BLOCK))
        a_ref[rows, :] = unpad_heads(out).astype(BF16)


def backward_kernel(masked, table, *refs):
    if masked:
        (q_ref, k_ref, v_ref, g_ref, o_ref, l_ref, vec_ref, low_ref, high_ref,
         dq_ref, dkv_ref, dvec_ref, bias_ref, dk_acc, dv_acc, dq_acc, near_ref, far_ref) = refs
        fill_bias(vec_ref, bias_ref)
        near_ref[...] = jnp.zeros_like(near_ref)
        far_ref[...] = jnp.zeros_like(far_ref)
    else:
        (q_ref, k_ref, v_ref, g_ref, o_ref, l_ref, dq_ref, dkv_ref, dk_acc, dv_acc, dq_acc) = refs
    pairs = q_ref.shape[0] // BLOCK
    steps = k_ref.shape[0] // BLOCK
    dk_acc[...] = jnp.zeros_like(dk_acc)
    dv_acc[...] = jnp.zeros_like(dv_acc)
    row = lax.broadcasted_iota(jnp.int32, (BLOCK, BLOCK), 0)
    for index in range(pairs):
        rows = slice(index * BLOCK, (index + 1) * BLOCK)
        query = pad_heads(q_ref[rows, :])
        grad = pad_heads(g_ref[rows, :])
        log_total = l_ref[0, index, :1, :]
        raw_grad = g_ref[rows, :].astype(F32)
        turned_grad = jnp.concatenate(
            [raw_grad[:, head * HEAD : (head + 1) * HEAD].T for head in range(4)], axis=1
        )
        delta = jnp.sum(turned_grad * o_ref[0, index], axis=0, keepdims=True)
        if masked:
            mine = table[index]
            first = table[pairs + index]
            low = low_ref[index : index + 1, :]
            high = high_ref[index : index + 1, :]

        def tile(step, near, start):
            if masked:
                block = mine - step
                place = pl.multiple_of(table[2 * pairs + block] * BLOCK, BLOCK)
            else:
                place = pl.multiple_of(step * BLOCK, BLOCK)
            keys = k_ref[pl.ds(place, BLOCK), :]
            raw = nt(keys, query)
            if masked:
                position = row + block * BLOCK
                allowed = position >= low
                if near:
                    allowed = allowed & (position <= high)
                    raw = raw + bias_ref[0]
                else:
                    raw = raw + bias_ref[jnp.minimum(step, 2)]
                raw = jnp.where(four(allowed), raw, NEGATIVE)
            prob = jnp.exp(raw - log_total)
            grad_prob = nt(v_ref[pl.ds(place, BLOCK), :], grad)
            grad_score = (prob * (grad_prob - delta)).astype(BF16)
            dv_acc[pl.ds(place, BLOCK), :] += nn(prob.astype(BF16), grad)
            dk_acc[pl.ds(place, BLOCK), :] += nn(grad_score, query)
            turned = keys.astype(F32).T.astype(BF16)
            part = jnp.concatenate(
                [nn(turned[:HEAD], grad_score[:, : 2 * BLOCK]), nn(turned[HEAD:], grad_score[:, 2 * BLOCK :])],
                axis=1,
            )
            if start:
                dq_acc[...] = part
            else:
                dq_acc[...] += part
            return grad_score

        grad_score = tile(0, True, True)
        if masked:
            near_ref[0] += grad_score.astype(F32)
            last = mine - first

            @pl.when(last >= 1)
            def _():
                near_ref[1] += tile(1, False, False).astype(F32)

            def advance(step, carry):
                wide = tile(step, False, False).astype(F32)
                far_ref[...] += jnp.sum(wide.reshape(BLOCK // 8, 8, 4 * BLOCK), axis=0)
                return carry

            lax.fori_loop(2, last + 1, advance, 0)
        else:

            def advance(step, carry):
                tile(step, False, False)
                return carry

            lax.fori_loop(1, steps, advance, 0)
        dq_ref[rows, :] = unpad_heads(dq_acc[...]).astype(BF16)
    dkv_ref[0] = dk_acc[...].astype(BF16)
    dkv_ref[1] = dv_acc[...].astype(BF16)
    if masked:
        rowid = lax.broadcasted_iota(jnp.int32, (BLOCK, SPAN), 0)
        lane = lax.broadcasted_iota(jnp.int32, (1, SPAN), 1)
        for head in range(4):
            lanes = slice(head * BLOCK, (head + 1) * BLOCK)
            wide = jnp.concatenate(
                [near_ref[0, :, lanes], near_ref[1, :, lanes], jnp.zeros((BLOCK, 2 * BLOCK), F32)], axis=1
            )
            bit = 1
            while bit < BLOCK:
                wide = jnp.where((rowid & bit) != 0, pltpu.roll(wide, SPAN - bit, 1), wide)
                bit = bit * 2
            sums = jnp.sum(wide, axis=0, keepdims=True)
            far = jnp.sum(far_ref[:, lanes])
            dvec_ref[0, head : head + 1, :] = sums + jnp.where(lane == BLOCK, far, 0.0)


def specs_of(rows, length, pairs, groups, first=0):
    cols = pl.BlockSpec((rows, 2 * BLOCK), lambda g, *_: (0, g + first))
    keys = pl.BlockSpec((length, BLOCK), lambda g, *_: (0, g + first))
    values = pl.BlockSpec((length, BLOCK), lambda g, *_: (0, groups + g + first))
    outs = pl.BlockSpec((1, pairs, HEAD, 4 * BLOCK), lambda g, *_: (g + first, 0, 0, 0))
    logs = pl.BlockSpec((1, pairs, 8, 4 * BLOCK), lambda g, *_: (g + first, 0, 0, 0))
    vecs = pl.BlockSpec((1, 4, SPAN), lambda g, *_: (g + first, 0, 0))
    lims = pl.BlockSpec((pairs, BLOCK), lambda g, *_: (0, 0))
    return cols, keys, values, outs, logs, vecs, lims


def attend(query, keys_values, table, extra, masked):
    rows, width = query.shape
    length = keys_values.shape[0]
    groups = width // (4 * HEAD)
    pairs = rows // BLOCK
    cols, kspec, vspec, outs, logs, vecs, lims = specs_of(rows, length, pairs, groups)
    scratch = [pltpu.VMEM((HEAD, 4 * BLOCK), F32)]
    if masked:
        scratch = [pltpu.VMEM((3, BLOCK, 4 * BLOCK), F32)] + scratch
    return pl.pallas_call(
        functools.partial(forward_kernel, masked),
        grid_spec=pltpu.PrefetchScalarGridSpec(
            num_scalar_prefetch=1,
            grid=(groups,),
            in_specs=[cols, kspec, vspec] + ([vecs, lims, lims] if masked else []),
            out_specs=[cols, outs, logs],
            scratch_shapes=scratch,
        ),
        out_shape=[
            jax.ShapeDtypeStruct((rows, width), BF16),
            jax.ShapeDtypeStruct((groups, pairs, HEAD, 4 * BLOCK), F32),
            jax.ShapeDtypeStruct((groups, pairs, 8, 4 * BLOCK), F32),
        ],
        cost_estimate=pl.CostEstimate(
            flops=4 * rows * length * width, bytes_accessed=4 * length * width, transcendentals=rows * length * 16
        ),
        name="attend_self" if masked else "attend_cross",
    )(table, query, keys_values, keys_values, *extra)


def attend_back(query, keys_values, grad, outs_in, logs_in, table, extra, masked, part=0, parts=1):
    rows, width = query.shape
    length = keys_values.shape[0]
    groups = width // (4 * HEAD)
    pairs = rows // BLOCK
    count = groups // parts
    cols, kspec, vspec, outs, logs, vecs, lims = specs_of(rows, length, pairs, groups, part * count)
    scratch = [pltpu.VMEM((length, BLOCK), F32), pltpu.VMEM((length, BLOCK), F32), pltpu.VMEM((HEAD, 4 * BLOCK), F32)]
    out_specs = [pl.BlockSpec((rows, 2 * BLOCK), lambda g, *_: (0, g)), pl.BlockSpec((2, length, BLOCK), lambda g, *_: (0, 0, g))]
    out_shape = [
        jax.ShapeDtypeStruct((rows, width // parts), BF16),
        jax.ShapeDtypeStruct((2, length, width // 2 // parts), BF16),
    ]
    if masked:
        scratch = [pltpu.VMEM((3, BLOCK, 4 * BLOCK), F32)] + scratch
        scratch += [pltpu.VMEM((2, BLOCK, 4 * BLOCK), F32), pltpu.VMEM((8, 4 * BLOCK), F32)]
        out_specs = out_specs + [pl.BlockSpec((1, 4, SPAN), lambda g, *_: (g, 0, 0))]
        out_shape = out_shape + [jax.ShapeDtypeStruct((count, 4, SPAN), F32)]
    return pl.pallas_call(
        functools.partial(backward_kernel, masked),
        grid_spec=pltpu.PrefetchScalarGridSpec(
            num_scalar_prefetch=1,
            grid=(count,),
            in_specs=[cols, kspec, vspec, cols, outs, logs] + ([vecs, lims, lims] if masked else []),
            out_specs=out_specs,
            scratch_shapes=scratch,
        ),
        out_shape=out_shape,
        cost_estimate=pl.CostEstimate(
            flops=10 * rows * length * width // parts, bytes_accessed=8 * length * width // parts,
            transcendentals=rows * length * 16 // parts
        ),
        name="attend_self_back" if masked else "attend_cross_back",
    )(table, query, keys_values, keys_values, grad, outs_in, logs_in, *extra)


def offset_index(half):
    place = jnp.arange(SPAN, dtype=jnp.int32)
    behind = jnp.where(place >= 2 * BLOCK, place - SPAN, place)
    return behind, jnp.clip(half - behind, 0, 2 * half - 1)


D = 1024
HEADS = 16
KV_HEADS = 8
BUCKETS = 32
EPS = 1e-06
CTX = ("line", "core")


def tn(left, right):
    return lax.dot_general(left, right, (((0,), (0,)), ((), ())), preferred_element_type=F32)


def norm_rows(values, gain):
    scale = lax.rsqrt(jnp.mean(values * values, axis=-1, keepdims=True) + EPS)
    normed = values * scale
    return normed, scale, (normed * gain).astype(BF16)


def norm_back(grad_out, normed, scale, gain):
    grad_gain = jnp.sum(grad_out * normed, axis=0)
    inner = grad_out * gain
    grad_in = scale * (inner - normed * jnp.mean(inner * normed, axis=-1, keepdims=True))
    return grad_in, grad_gain


def gelu_tanh(value):
    return jax.nn.gelu(value, approximate=True)


def partners(size, bit):
    return [(index, index ^ bit) for index in range(size)]


def bits_of(size):
    return [1 << place for place in range(size.bit_length() - 1)]


def cross(value, axis, bit):
    return lax.ppermute(value, axis, partners(lax.axis_size(axis), bit))


def swap(value):
    return cross(value, "core", 1)


def add(left, right):
    return (left.astype(F32) + right.astype(F32)).astype(BF16)


def place_kernel(spots, rows, me_ref, *refs):
    pieces, whole_ref, sems = refs[: len(spots)], refs[len(spots)], refs[len(spots) + 1]
    copies = []
    for index, (mask, offset) in enumerate(spots):
        count = pieces[index].shape[0]
        start = pl.multiple_of((me_ref[0] ^ mask) * rows + offset, count)
        copies.append(pltpu.make_async_copy(pieces[index], whole_ref.at[pl.ds(start, count), :], sems.at[index]))
    for copy in copies:
        copy.start()
    for copy in copies:
        copy.wait()


def place(me, pieces, spots, size, rows):
    anywhere = pl.BlockSpec(memory_space=pl.ANY)
    return pl.pallas_call(
        functools.partial(place_kernel, spots, rows),
        in_specs=[pl.BlockSpec(memory_space=pltpu.SMEM)] + [pl.BlockSpec(memory_space=pltpu.VMEM)] * len(pieces),
        out_specs=anywhere,
        out_shape=jax.ShapeDtypeStruct((size * rows, pieces[0].shape[1]), BF16),
        scratch_shapes=[pltpu.SemaphoreType.DMA((len(pieces),))],
        name="place",
    )(me.reshape(1), *pieces)


class Lane:
    def __init__(self, steps):
        self.steps = steps
        self.result = None
        self.pending = next(steps)

    def push(self, arrived):
        try:
            self.pending = self.steps.send(arrived)
        except StopIteration as end:
            self.pending, self.result = None, end.value

    def take(self):
        while self.pending is not None:
            tick([self], ())
        return self.result

    def take(self):
        while self.pending is not None:
            tick([self], ())
        return self.result


def tick(lanes, live):
    active = [lane for lane in lanes if lane.pending is not None]
    live, arrived = lax.optimization_barrier((live, [lane.pending for lane in active]))
    for lane, value in zip(active, arrived):
        lane.push(value)
    return live


def swap_steps(*values):
    got = yield [swap(value) for value in values]
    return got


def sum_steps(value):
    for axis in ("core", "fsdp", "line"):
        for bit in bits_of(lax.axis_size(axis)):
            (got,) = yield [cross(value, axis, bit)]
            value = value + got
    return value


def count_steps(value):
    (got,) = yield [swap(value)]
    value = value + got
    got = yield [cross(value, "line", mask) for mask in range(1, lax.axis_size("line"))]
    return value + sum(got)


def small_steps(value):
    size = lax.axis_size("fsdp")
    me = lax.axis_index("fsdp")
    have = [(0, value)]
    for bit in bits_of(size):
        got = yield [cross(piece, "fsdp", bit) for _, piece in have]
        have = have + [(mask ^ bit, piece) for (mask, _), piece in zip(have, got)]
    whole = jnp.zeros((size, value.shape[0]), value.dtype)
    for mask, piece in have:
        whole = lax.dynamic_update_slice(whole, piece[None], (me ^ mask, 0))
    return whole


def columns_of(value, core):
    half = value.shape[1] // 2
    return lax.dynamic_slice_in_dim(value, core * half, half, axis=1)


def half_columns(parts):
    core = lax.axis_index("core")
    return jnp.concatenate([columns_of(part, core) for part in parts], axis=1)


def gather_steps(mine, fine=False):
    size = lax.axis_size("fsdp")
    me = lax.axis_index("fsdp")
    rows, width = mine.shape
    bits = bits_of(size)
    half = rows // 2
    streams = [[(0, mine[stream * half : (stream + 1) * half])] for stream in range(2)]
    for step in range(len(bits)):
        chosen = [(bits if stream == 0 else bits[::-1])[step] for stream in range(2)]
        have = len(streams[0])
        got = [[], []]
        for spot in range(have) if fine else [slice(0, have)]:
            spot = spot if isinstance(spot, slice) else slice(spot, spot + 1)
            arrived = yield [
                [cross(piece, "fsdp", chosen[stream]) for _, piece in streams[stream][spot]] for stream in range(2)
            ]
            got = [got[stream] + arrived[stream] for stream in range(2)]
        for stream in range(2):
            fresh = [(mask ^ chosen[stream], piece) for (mask, _), piece in zip(streams[stream], got[stream])]
            streams[stream] = streams[stream] + fresh
    spots = [(0, 0)] + [(mask, stream * half) for stream in range(2) for mask, _ in streams[stream][1:]]
    pieces = [mine] + [piece for stream in range(2) for _, piece in streams[stream][1:]]
    whole = place(me, pieces, spots, size, rows)
    whole, other = yield whole, swap(whole)
    return whole, other


def by_core(mine, other):
    first = lax.axis_index("core") == 0
    return jnp.where(first, mine, other), jnp.where(first, other, mine)


def grad_halves(*grads):
    core = lax.axis_index("core")
    mine = jnp.concatenate([columns_of(item, core) for item in grads], axis=1)
    return mine, jnp.concatenate([columns_of(item, 1 - core) for item in grads], axis=1)


def weight_grad(hidden, hidden_swapped, mine, arrived):
    both_hidden = jnp.concatenate([hidden, hidden_swapped], axis=0)
    both_grad = jnp.concatenate([mine, arrived], axis=0)
    return tn(both_hidden, both_grad).astype(BF16)


def split(value, axis, bit, place):
    mine = (lax.axis_index(axis) // bit) % 2
    keep = lax.dynamic_index_in_dim(value, mine, place, keepdims=False)
    return keep, lax.dynamic_index_in_dim(value, 1 - mine, place, keepdims=False)


def reduce_steps(partials, widths):
    size = lax.axis_size("fsdp")
    lines = lax.axis_size("line")
    rows = partials[0].shape[0] // size
    width = partials[0].shape[1]
    many = len(partials)
    bits = bits_of(size)
    folded = jnp.stack(partials).reshape([many] + [2] * len(bits) + [2, rows // 2, width])
    values = [lax.index_in_dim(folded, stream, 1 + len(bits), keepdims=False) for stream in range(2)]
    left = [bits[::-1], bits[::-1]]
    for step in range(len(bits)):
        chosen = [(bits if stream == 0 else bits[::-1])[step] for stream in range(2)]
        parts = [
            split(values[stream], "fsdp", chosen[stream], 1 + left[stream].index(chosen[stream]))
            for stream in range(2)
        ]
        got = yield [cross(parts[stream][1], "fsdp", chosen[stream]) for stream in range(2)]
        values = [add(parts[stream][0], got[stream]) for stream in range(2)]
        left = [[item for item in left[stream] if item != chosen[stream]] for stream in range(2)]
    shard = jnp.stack(values, axis=1)
    line_bits = bits_of(lines)
    value = shard.reshape([many] + [2] * len(line_bits) + [rows // lines, width])
    for bit in line_bits:
        keep, send = split(value, "line", bit, value.ndim - 3)
        (got,) = yield [cross(send, "line", bit)]
        value = add(keep, got)
    mine = value[None]
    for bit in line_bits[::-1]:
        (got,) = yield [cross(mine, "line", bit)]
        mine = jnp.concatenate([mine, got], axis=0)
    (other,) = yield [swap(mine)]
    me = lax.axis_index("line")

    def spot(entry):
        mask = me ^ entry
        return sum(((mask // bit) % 2) * (lines // (2 * bit)) for bit in line_bits)

    outs = []
    for index in range(many):
        start = 0
        for wide in widths[index]:
            part = slice(start, start + wide // 2)
            both = jnp.concatenate(by_core(mine[:, index, :, part], other[:, index, :, part]), axis=2)
            ordered = [lax.dynamic_index_in_dim(both, spot(entry), 0, keepdims=False) for entry in range(lines)]
            outs.append(jnp.concatenate(ordered, axis=0).astype(F32))
            start = start + wide // 2
    return outs


def gather_context_steps(value):
    rows = value.shape[0]
    mine = value
    masks = [0]
    for bit in bits_of(lax.axis_size("line"))[::-1]:
        (got,) = yield [cross(mine, "line", bit)]
        mine = jnp.concatenate([mine, got], axis=0)
        masks = masks + [mask ^ bit for mask in masks]
    order = [masks.index(mask) for mask in range(len(masks))]
    mine = jnp.concatenate([mine[at * rows : (at + 1) * rows] for at in order], axis=0)
    (other,) = yield [swap(mine)]
    return jnp.concatenate([mine, other], axis=0)


def reduce_context_steps(value):
    lines = lax.axis_size("line")
    two, total, width = value.shape
    value = value.reshape(two, 2, lines, total // (2 * lines), width)
    (got,) = yield [swap(value[:, 1])]
    value = add(value[:, 0], got)
    for bit in bits_of(lines):
        value = value.reshape(two, value.shape[1] // 2, 2, value.shape[2], width)
        (got,) = yield [cross(value[:, :, 1], "line", bit)]
        value = add(value[:, :, 0], got)
    return value[:, 0]


def body(
    inputs, encoder, teacher, valid_mask, doc_ids, block_order, buckets,
    gain_self, w_query, w_key, w_value, w_out, gain_cross, c_query, c_key, c_value, c_out,
    gain_ffn, w_gate, w_up, w_down, bias_table,
):
    rows, width = inputs.shape[1:]
    lines = lax.axis_size("line")
    shards = lax.axis_size("fsdp")
    contexts = 2 * lines
    length = rows * contexts
    pair = rows // BLOCK
    token_total = length * shards
    key_width = KV_HEADS * HEAD
    context = lax.axis_index("line") * 2 + lax.axis_index("core")
    fsdp = lax.axis_index("fsdp")

    core = lax.axis_index("core")
    hidden_ff = w_gate.shape[1]
    joint = jnp.concatenate
    halves = D // 2
    share = gain_self.shape[0]

    def times(left, weight):
        return joint(by_core(nn(left, weight[0]), nn(left, weight[1])), axis=1)

    def times_back(grad, weight):
        return nt(columns_of(grad, core), weight[0]) + nt(columns_of(grad, 1 - core), weight[1])

    mask_rows = valid_mask.reshape(rows).astype(F32)
    assert rows <= 256
    local_count = jnp.broadcast_to(jnp.sum(mask_rows), (128,)).astype(BF16)
    lane_qkv = Lane(gather_steps(half_columns([joint([w_query, w_key, w_value], axis=1)])))
    lane_small = Lane(small_steps(joint([gain_self, gain_cross, gain_ffn, bias_table.reshape(-1), local_count])))
    mid_parts = tick([lane_qkv, lane_small], (w_out, c_query, c_key, c_value, c_out))

    mid_shard = half_columns([mid_parts[0], mid_parts[1], joint(mid_parts[2:4], axis=1), mid_parts[4]])
    mid_shard = tick([lane_qkv, lane_small], mid_shard)

    small = lane_small.take()
    gain_one, gain_two, gain_three = [
        small[:, index * share : (index + 1) * share].reshape(D).astype(F32) for index in range(3)
    ]
    table_whole = small[:, 3 * share : -128].reshape(BUCKETS, HEADS)
    lane_count = Lane(count_steps(jnp.broadcast_to(jnp.sum(small[:, -128:].astype(F32), axis=0), (8, 128))))
    flat_in = inputs.reshape(rows, width).astype(F32)
    normed_one, scale_one, hidden_one = norm_rows(flat_in, gain_one)
    hidden_one = tick([lane_qkv, lane_count], hidden_one)

    qkv_mine, qkv_other = lane_qkv.take()
    lane_mid = Lane(gather_steps(mid_shard))
    query, pairs = by_core(nn(hidden_one, qkv_mine).astype(BF16), nn(hidden_one, qkv_other).astype(BF16))
    query, pairs, late = tick(
        [lane_mid, lane_count], (query, pairs, (w_gate, w_up, w_down, doc_ids, block_order, buckets, table_whole))
    )
    gate_part, up_part, down_part, *late = late

    lane_keys = Lane(gather_context_steps(pairs))
    gu_shard = half_columns([joint([gate_part, up_part], axis=1)])
    wd_shard = half_columns([down_part])

    gu_shard, wd_shard, late = tick([lane_keys, lane_mid], (gu_shard, wd_shard, late))
    doc_ids, block_order, buckets, table_whole = late

    lane_gu = Lane(gather_steps(gu_shard, True))
    query_blocks = lax.dynamic_slice_in_dim(block_order, context * pair, pair)
    slots = jnp.arange(contexts * pair, dtype=jnp.int32)
    owner = slots // pair
    near = ((owner % 2) ^ core) * lines + ((owner // 2) ^ lax.axis_index("line"))
    slots_near = near * pair + slots % pair
    inverse = jnp.sum(jnp.where(block_order[None, :] == slots[:, None], slots_near[None, :], 0), axis=1)
    docs = doc_ids.reshape(length)
    query_docs = jnp.stack(
        [lax.dynamic_slice_in_dim(docs, query_blocks[index] * BLOCK, BLOCK) for index in range(pair)]
    )
    low = jnp.sum((docs[None, None, :] < query_docs[:, :, None]).astype(jnp.int32), axis=-1)
    high = jnp.sum((docs[None, None, :] <= query_docs[:, :, None]).astype(jnp.int32), axis=-1) - 1
    place_table = jnp.concatenate([query_blocks, low[:, 0] // BLOCK, inverse]).astype(jnp.int32)
    behind, index_of = offset_index(length)
    bucket_match = (jnp.take(buckets, index_of)[None, :] == jnp.arange(BUCKETS, dtype=jnp.int32)[:, None])

    vectors = tn(table_whole, bucket_match.astype(BF16)).reshape(HEADS // 4, 4, SPAN)
    low, high, place_table, bucket_match, vectors = tick(
        [lane_keys, lane_mid, lane_gu], (low, high, place_table, bucket_match, vectors)
    )
    extra = (vectors, low, high)
    mid_mine, mid_other = lane_mid.take()
    wo, wcq, wckv, wco = [
        (mid_mine[:, index * halves : (index + 1) * halves], mid_other[:, index * halves : (index + 1) * halves])
        for index in range(4)
    ]
    encoder_rows = encoder.reshape(encoder.shape[1], width)
    encoder_pairs = times(encoder_rows, wckv).astype(BF16)
    encoder_pairs, wd_shard = tick([lane_keys], (encoder_pairs, wd_shard))
    pairs_whole = lane_keys.take()

    lane_encoder = Lane(gather_context_steps(encoder_pairs))
    lane_encoder_rows = Lane(swap_steps(encoder_rows))
    lane_wd = Lane(gather_steps(wd_shard))
    lane_hidden_one = Lane(swap_steps(hidden_one))
    attention, outs_one, logs_one = attend(query, pairs_whole, place_table, extra, True)
    attention, outs_one, logs_one = tick(
        [lane_encoder, lane_encoder_rows, lane_gu, lane_wd, lane_hidden_one], (attention, outs_one, logs_one)
    )

    lane_attention = Lane(swap_steps(attention))
    mid_one = flat_in + times(attention, wo)
    normed_two, scale_two, hidden_two = norm_rows(mid_one, gain_two)
    cross_q = times(hidden_two, wcq).astype(BF16)
    mid_one, normed_two, hidden_two, cross_q, scale_two = tick(
        [lane_encoder, lane_attention, lane_gu], (mid_one, normed_two, hidden_two, cross_q, scale_two)
    )
    tick([lane_encoder], ())
    encoder_whole = lane_encoder.take()

    lane_hidden_two = Lane(swap_steps(hidden_two))
    crossed, outs_two, logs_two = attend(cross_q, encoder_whole, place_table, (), False)
    crossed, outs_two, logs_two = tick([lane_gu, lane_wd, lane_hidden_two], (crossed, outs_two, logs_two))

    lane_crossed = Lane(swap_steps(crossed))
    mid_two = mid_one + times(crossed, wco)
    normed_three, scale_three, hidden_three = norm_rows(mid_two, gain_three)
    mid_two, normed_three, hidden_three, scale_three = tick(
        [lane_wd, lane_crossed], (mid_two, normed_three, hidden_three, scale_three)
    )

    gu_mine, gu_other = lane_gu.take()
    lane_hidden_three = Lane(swap_steps(hidden_three))
    gate, up = by_core(nn(hidden_three, gu_mine), nn(hidden_three, gu_other))
    active, gelu_pull = jax.vjp(gelu_tanh, gate)
    mixed = (active * up).astype(BF16)
    mixed, gate, up, active = tick([lane_hidden_three], (mixed, gate, up, active))
    lane_mixed = Lane(swap_steps(mixed))

    wd_mine, wd_other = lane_wd.take()
    count = jnp.maximum(lane_count.take()[0, 0], 1.0)
    result = mid_two + times(mixed, (wd_mine, wd_other))
    layer_out = result.astype(BF16)
    diff = result - teacher.reshape(rows, width).astype(F32)
    squared_local = jnp.sum(mask_rows[:, None] * diff * diff)
    grad_result = token_total / count * mask_rows[:, None] * diff

    e_three = grad_result.astype(BF16)
    down_mine, down_away = grad_halves(e_three)
    grad_result, e_three, down_mine, down_away, squared_local, layer_out = tick(
        [lane_mixed], (grad_result, e_three, down_mine, down_away, squared_local, layer_out)
    )
    lane_down = Lane(swap_steps(down_away))
    grad_mixed = times_back(e_three, (wd_mine, wd_other))
    (gelu_slope,) = gelu_pull(grad_mixed * up)
    grad_gate = gelu_slope.astype(BF16)
    grad_up = (grad_mixed * active).astype(BF16)
    wide_mine, wide_away = grad_halves(grad_gate, grad_up)
    grad_gate, grad_up, wide_mine, wide_away = tick([lane_down], (grad_gate, grad_up, wide_mine, wide_away))

    lane_wide = Lane(swap_steps(wide_away))
    partial_down = weight_grad(mixed, lane_mixed.take()[0], down_mine, lane_down.take()[0])
    partial_down = tick([lane_wide], partial_down)

    lane_down = Lane(reduce_steps([partial_down], [(D,)]))
    partial_wide = weight_grad(hidden_three, lane_hidden_three.take()[0], wide_mine, lane_wide.take()[0])
    grad_hidden_three = times_back(joint([grad_gate, grad_up], axis=1), (gu_mine, gu_other))
    partial_wide, grad_hidden_three = tick([lane_down], (partial_wide, grad_hidden_three))

    lane_wide = Lane(reduce_steps([partial_wide], [(hidden_ff, hidden_ff)]))
    grad_norm_three, grad_gain_three = norm_back(grad_hidden_three, normed_three, scale_three, gain_three)
    grad_mid_two = grad_result + grad_norm_three

    e_two = grad_mid_two.astype(BF16)
    grad_cross = times_back(e_two, wco).astype(BF16)
    grad_cross_q, encoder_grad = attend_back(
        cross_q, encoder_whole, grad_cross, outs_two, logs_two, place_table, (), False
    )
    out_mine, out_away = grad_halves(e_two, grad_cross_q)
    grad_mid_two, grad_cross_q, encoder_grad, out_mine, out_away = tick(
        [lane_down, lane_wide], (grad_mid_two, grad_cross_q, encoder_grad, out_mine, out_away)
    )

    lane_encoder = Lane(reduce_context_steps(encoder_grad))
    lane_out = Lane(swap_steps(out_away))
    grad_norm_two, grad_gain_two = norm_back(times_back(grad_cross_q, wcq), normed_two, scale_two, gain_two)
    grad_mid_one = grad_mid_two + grad_norm_two

    e_one = grad_mid_one.astype(BF16)
    one_mine, one_away = grad_halves(e_one)
    grad_attention = times_back(e_one, wo).astype(BF16)
    grad_mid_one, one_mine, one_away, grad_attention = tick(
        [lane_down, lane_wide, lane_encoder, lane_out], (grad_mid_one, one_mine, one_away, grad_attention)
    )
    lane_one = Lane(swap_steps(one_away))

    def attend_part(part):
        return attend_back(
            query, pairs_whole, grad_attention, outs_one, logs_one, place_table, extra, True, part, 2
        )

    query_first, pairs_first, vectors_first = attend_part(0)
    query_first, pairs_first, vectors_first, grad_attention = tick(
        [lane_down, lane_wide, lane_encoder, lane_one], (query_first, pairs_first, vectors_first, grad_attention)
    )
    lane_first = Lane(reduce_context_steps(pairs_first))
    query_second, pairs_second, vectors_second = attend_part(1)
    grad_query = joint([query_first, query_second], axis=1)
    grad_vectors = joint([vectors_first, vectors_second], axis=0)
    query_mine, query_away = grad_halves(grad_query)
    pairs_second, grad_query, grad_vectors, query_mine, query_away = tick(
        [lane_down, lane_wide, lane_encoder, lane_first],
        (pairs_second, grad_query, grad_vectors, query_mine, query_away),
    )

    lane_second = Lane(reduce_context_steps(pairs_second))
    lane_query = Lane(swap_steps(query_away))
    arrived = lane_out.take()[0]
    partial_out = weight_grad(crossed, lane_crossed.take()[0], out_mine[:, :halves], arrived[:, :halves])
    partial_cross = weight_grad(hidden_two, lane_hidden_two.take()[0], out_mine[:, halves:], arrived[:, halves:])
    partial_one = weight_grad(attention, lane_attention.take()[0], one_mine, lane_one.take()[0])
    encoder_got = lane_encoder.take()
    encoder_mine = joint([encoder_got[0], encoder_got[1]], axis=1)
    keys_mine, keys_away = grad_halves(encoder_mine[:, :key_width], encoder_mine[:, key_width:])
    partial_out, partial_cross, partial_one, encoder_mine, keys_mine, keys_away = tick(
        [lane_first, lane_second, lane_down, lane_wide, lane_query],
        (partial_out, partial_cross, partial_one, encoder_mine, keys_mine, keys_away),
    )

    lane_keys = Lane(swap_steps(keys_away))
    partial_query = weight_grad(hidden_one, lane_hidden_one.take()[0], query_mine, lane_query.take()[0])
    lane_mid = Lane(reduce_steps([partial_out, partial_cross, partial_one, partial_query], [(D,)] * 4))
    grad_encoder = times_back(encoder_mine, wckv)
    grad_encoder = tick([lane_first, lane_second, lane_down, lane_keys], grad_encoder)

    partial_keys = weight_grad(encoder_rows, lane_encoder_rows.take()[0], keys_mine, lane_keys.take()[0])
    partial_keys = tick([lane_second, lane_mid], partial_keys)
    pairs_first, pairs_second = lane_first.take(), lane_second.take()
    mine = [joint([pairs_first[index], pairs_second[index]], axis=1) for index in range(2)]
    last_mine, last_away = grad_halves(mine[0], mine[1])
    mine, last_mine, last_away = tick([], (mine, last_mine, last_away))

    lane_last = Lane(swap_steps(last_away))
    tick([lane_last], ())
    partial_last = weight_grad(hidden_one, lane_hidden_one.take()[0], last_mine, lane_last.take()[0])
    partial_last = tick([lane_mid, lane_wide], partial_last)

    lane_last = Lane(reduce_steps([partial_last, partial_keys], [(key_width, key_width)] * 2))
    grad_packed = joint([grad_query, mine[0], mine[1]], axis=1)
    grad_norm_one, grad_gain_one = norm_back(
        times_back(grad_packed, (qkv_mine, qkv_other)), normed_one, scale_one, gain_one
    )
    grad_inputs = grad_mid_one + grad_norm_one

    grad_table = lax.dot_general(
        bucket_match.astype(F32) * ((behind >= 1 - BLOCK) & (behind < 2 * BLOCK)).astype(F32)[None, :],
        grad_vectors.reshape(HEADS, SPAN),
        (((1,), (1,)), ((), ())),
        precision=lax.Precision.HIGHEST,
        preferred_element_type=F32,
    )
    sums = jnp.concatenate(
        [
            grad_gain_one,
            grad_gain_two,
            grad_gain_three,
            grad_table.reshape(-1),
            jnp.broadcast_to(squared_local, (512,)),
        ]
    )
    sums, grad_inputs = tick([lane_last, lane_wide, lane_mid, lane_down], (sums.reshape(-1, 128), grad_inputs))
    lane_sums = Lane(sum_steps(sums))
    lanes = [lane_last, lane_wide, lane_mid, lane_down, lane_sums]
    while any(lane.pending is not None for lane in lanes):
        tick(lanes, ())
    sums = lane_sums.take().reshape(-1)
    (grad_down,) = lane_down.take()
    grad_gate_weight, grad_up_weight = lane_wide.take()
    grad_cross_out, grad_cross_query, grad_out_weight, grad_query_weight = lane_mid.take()
    grad_key_weight, grad_value_weight, grad_cross_key, grad_cross_value = lane_last.take()
    loss = sums[3 * D + 512] / (D * count)

    def shard_of(offset, amount):
        return lax.dynamic_slice_in_dim(sums, offset + fsdp * (amount // shards), amount // shards)

    return (
        layer_out.reshape(1, rows, width),
        loss,
        grad_inputs.reshape(1, rows, width),
        grad_encoder.reshape(1, encoder.shape[1], width),
        shard_of(0, D),
        grad_query_weight,
        grad_key_weight,
        grad_value_weight,
        grad_out_weight,
        shard_of(D, D),
        grad_cross_query,
        grad_cross_key,
        grad_cross_value,
        grad_cross_out,
        shard_of(2 * D, D),
        grad_gate_weight,
        grad_up_weight,
        grad_down,
        shard_of(3 * D, 512).reshape(BUCKETS // shards, HEADS),
    )


def solution(mesh):
    shape = mesh.devices.shape
    fine = Mesh(mesh.devices.reshape(shape[0] // 2, 2, shape[1]), ("line", "core", "fsdp"))
    tokens = P("fsdp", CTX, None)
    matrix = P("fsdp", None)
    vector = P("fsdp")
    weights = (vector, matrix, matrix, matrix, matrix, vector, matrix, matrix, matrix, matrix, vector)
    weights = weights + (matrix, matrix, matrix, matrix)
    in_specs = (tokens, tokens, tokens, P("fsdp", CTX), matrix, P(), P()) + weights
    out_specs = (tokens, P(), tokens, tokens) + weights
    return jax.shard_map(body, mesh=fine, in_specs=in_specs, out_specs=out_specs, check_vma=False)
```
